32 devices in a mesh: dp: 8 (over z, x), mp: 4 (over y, core).
Axes of the slice: x: 2, y: 2, z: 4, core: 2. Of those that a mesh axis runs over, the one named last changes fastest.
Arguments:
- tokens: bfloat16 [18944, 768], P(('dp', 'mp')), may hold values from -6 to 6
- image_group: int32 [8], P('dp'), may hold values from 0 to 1, as said below
- positions: int32 [2, 18944], P(None, 'dp'), may hold values from 0 to 23, as said below
- keep_mask: int32 [18944], P('dp'), may hold values from 0 to 1, as said below
- norm1_gain: float32 [768], replicated, may hold values from 0.25 to 1.75
- norm1_bias: float32 [768], replicated, may hold values from -1.75 to 1.75
- w_qkv: bfloat16 [768, 3, 768], P(None, None, 'mp'), may hold values from -0.21875 to 0.21875
- b_qkv: float32 [3, 768], P(None, 'mp'), may hold values from -1.75 to 1.75
- rotary_freqs: float32 [2, 12, 32], P(None, 'mp'), may hold values from -1 to 1
- w_out: bfloat16 [768, 768], P('mp'), may hold values from -0.875 to 0.875
- b_out: float32 [768], replicated, may hold values from -1.75 to 1.75
- norm2_gain: float32 [768], replicated, may hold values from 0.25 to 1.75
- norm2_bias: float32 [768], replicated, may hold values from -1.75 to 1.75
- w_up: bfloat16 [768, 3072], P(None, 'mp'), may hold values from -0.21875 to 0.21875
- b_up: bfloat16 [3072], P('mp'), may hold values from -1.75 to 1.75
- w_down: bfloat16 [3072, 768], P('mp'), may hold values from -0.109375 to 0.109375
- b_down: float32 [768], replicated, may hold values from -1.75 to 1.75
- cotangent: float32 [18944, 768], P(('dp', 'mp')), may hold values from -6 to 6
Outputs:
- output: bfloat16 [18944, 768], P(('dp', 'mp'))
- grad_tokens: float32 [18944, 768], P(('dp', 'mp'))
- grad_norm1_gain: float32 [768], replicated
- grad_norm1_bias: float32 [768], replicated
- grad_w_qkv: float32 [768, 3, 768], P(None, None, 'mp')
- grad_b_qkv: float32 [3, 768], P(None, 'mp')
- grad_rotary_freqs: float32 [2, 12, 32], P(None, 'mp')
- grad_w_out: float32 [768, 768], P('mp')
- grad_b_out: float32 [768], replicated
- grad_norm2_gain: float32 [768], replicated
- grad_norm2_bias: float32 [768], replicated
- grad_w_up: float32 [768, 3072], P(None, 'mp')
- grad_b_up: float32 [3072], P('mp')
- grad_w_down: float32 [3072, 768], P('mp')
- grad_b_down: float32 [768], replicated
The draws below stay inside these ranges and needn't reach their ends.
Inputs may be any that keep to these rules, and one draw needn't show every extreme that they name: `image_group`: exactly 4 entries are 1. `positions`: each image's slots carry each of its patches once; padding slots carry 0, 0. `keep_mask`: in each image the kept slots are its first ones, at least one; padding slots are 0.
All inputs are finite; a program needn't handle non-finite values.
Results may differ from the reference program's by a relative error of at most 0.012.
The reference program's roundings to bfloat16 on the way count: a program that leaves them out, or rounds other values in their place, can miss the bound.
Values may be sent and summed in bfloat16 or wider, within the bound.
A program may use at most 192 MiB of HBM per device.

```python
import math
import jax
import jax.numpy as jnp
from jax import lax

D = 768
HEADS = 12
HD = 64
FF = 3072
SIDE_SMALL = 14
SIDE_LARGE = 24
IMG_SMALL = 3
IMG_LARGE = 1
PACK = 592
TOK_DEV = 2368
TOKENS = 18944
N_DP = 8


def layout(key):
    base_key = jax.random.fold_in(key, 7)
    perm_order = jax.random.permutation(jax.random.fold_in(base_key, 1), N_DP)
    image_group = (perm_order >= N_DP // 2).astype(jnp.int32)
    tok_index = jnp.arange(TOKENS, dtype=jnp.int32)
    device_id = tok_index // TOK_DEV
    inpack = tok_index % PACK
    pack_id = tok_index // PACK
    is_large = image_group[device_id]
    grid_side = jnp.where(is_large == 1, SIDE_LARGE, SIDE_SMALL).astype(jnp.int32)
    patches = grid_side * grid_side
    images = jnp.where(is_large == 1, IMG_LARGE, IMG_SMALL).astype(jnp.int32)
    image_id = jnp.minimum(inpack // patches, images - 1)
    within = inpack - image_id * patches
    is_real = within < patches
    noise = jax.random.randint(jax.random.fold_in(base_key, 2), (TOKENS,), 0, 131072, dtype=jnp.int32)
    tok_score = jnp.where(is_real, noise, 131072 + within)
    sortkey = (pack_id * 4 + image_id) * 262144 + tok_score
    order_tok = jnp.argsort(sortkey, stable=True)
    sorted_place = jnp.argsort(order_tok, stable=True).astype(jnp.int32)
    image_start = tok_index - within
    patch_rank = sorted_place - image_start
    patch_id = jnp.where(is_real, patch_rank, 0)
    patch_row = patch_id // grid_side
    patch_col = patch_id % grid_side
    last_index = max(N_DP - 1, 1)
    share_floor = 200 + 600 * device_id // last_index
    per_image = jax.random.randint(jax.random.fold_in(base_key, 3), (TOKENS // PACK * 4,), 0, 200, dtype=jnp.int32)
    keep_share = share_floor + per_image[pack_id * 4 + image_id]
    kept_count = jnp.maximum(patches * keep_share // 1000, 1)
    keep_mask = (within < kept_count).astype(jnp.int32)
    return (image_group, jnp.stack([patch_row, patch_col]).astype(jnp.int32), keep_mask)


def draw_image_group(key, part):
    return layout(key)[0]


def draw_positions(key, part):
    return layout(key)[1]


def draw_keep_mask(key, part):
    return layout(key)[2]


def levels(key, extent, shards, smallest, top_value):
    level = 1.0
    for axis_at, blocks in shards:
        steps = jax.random.uniform(jax.random.fold_in(jax.random.fold_in(key, 6), axis_at), (blocks,), jnp.float32, smallest / len(shards), top_value / len(shards))
        level = level * jnp.repeat(jnp.exp(steps), extent[axis_at] // blocks).reshape((-1,) + (1,) * (len(extent) - 1 - axis_at))
    return level


def centred(stream_key, extent, deviation, limit, shards=(), held_as=jnp.bfloat16):
    drawn = jax.random.normal(stream_key, extent, jnp.float32) * deviation
    if len(shards) > 0:
        drawn = levels(stream_key, extent, shards, -0.22, 0.18) * drawn
    return jnp.clip(drawn, min=-limit, max=limit).astype(held_as)


def setup_inputs(seed: int = 0) -> dict:
    splits = jax.random.split(jax.random.key(seed), 19)
    tokens = centred(splits[0], (TOKENS, D), 1.0, 6.0, ((0, 32),))
    image_group = draw_image_group(jax.random.fold_in(splits[18], 71), 0)
    positions = draw_positions(jax.random.fold_in(splits[18], 71), 0)
    keep_mask = draw_keep_mask(jax.random.fold_in(splits[18], 71), 0)
    norm1_gain = jnp.clip(1.0 + 0.15 * jax.random.normal(splits[4], (D,), jnp.float32), 0.25, 1.75)
    norm1_bias = centred(splits[5], (D,), 0.3, 1.75, (), jnp.float32)
    w_qkv = centred(splits[6], (D, 3, D), D ** -0.5, 0.21875, ((2, 4),))
    b_qkv = centred(splits[7], (3, D), 0.3, 1.75, ((1, 4),), jnp.float32)
    rotary_freqs = jnp.clip(jax.random.uniform(splits[8], (2, HEADS, HD // 2), jnp.float32, -1.0, 1.0) * levels(splits[8], (2, HEADS, HD // 2), ((1, 4),), -0.4, 0.0), -1.0, 1.0)
    w_out = centred(splits[9], (D, D), (D // 16) ** -0.5, 0.875, ((0, 4),))
    b_out = centred(splits[10], (D,), 0.3, 1.75, (), jnp.float32)
    norm2_gain = jnp.clip(1.0 + 0.15 * jax.random.normal(splits[11], (D,), jnp.float32), 0.25, 1.75)
    norm2_bias = centred(splits[12], (D,), 0.3, 1.75, (), jnp.float32)
    w_up = centred(splits[13], (D, FF), D ** -0.5, 0.21875, ((1, 4),))
    b_up = centred(splits[14], (FF,), 0.3, 1.75, ((0, 4),))
    w_down = centred(splits[15], (FF, D), FF ** -0.5, 0.109375, ((0, 4),))
    b_down = centred(splits[16], (D,), 0.3, 1.75, (), jnp.float32)
    cotangent = centred(splits[17], (TOKENS, D), 1.0, 6.0, ((0, 32),), jnp.float32)
    return dict(tokens=tokens, image_group=image_group, positions=positions, keep_mask=keep_mask, norm1_gain=norm1_gain, norm1_bias=norm1_bias, w_qkv=w_qkv, b_qkv=b_qkv, rotary_freqs=rotary_freqs, w_out=w_out, b_out=b_out, norm2_gain=norm2_gain, norm2_bias=norm2_bias, w_up=w_up, b_up=b_up, w_down=w_down, b_down=b_down, cotangent=cotangent)


@jax.custom_vjp
def low(v):
    return lax.optimization_barrier(v.astype(jnp.bfloat16)).astype(jnp.float32)

@jax.custom_vjp
def low_back(v):
    return v

def low_keep(v):
    return (low(v), None)

def low_pass(kept, grad):
    return (grad,)

def back_keep(v):
    return (v, None)

def back_low(kept, grad):
    return (low(grad),)
low.defvjp(low_keep, low_pass)
low_back.defvjp(back_keep, back_low)
NORM_EPS = 1e-06
MASK_FILL = -1e+30
PRECISE = lax.Precision.HIGHEST

def matmul(left, right):
    return jnp.dot(left, right, precision=PRECISE, preferred_element_type=jnp.float32)

def layer_norm(values, norm_gain, norm_bias):
    row_mean = lax.optimization_barrier(jnp.mean(values, axis=-1, keepdims=True))
    centered = values - row_mean
    variance = lax.optimization_barrier(jnp.mean(centered * centered, axis=-1, keepdims=True))
    return centered * lax.rsqrt(variance + NORM_EPS) * norm_gain + norm_bias

def rotate(vector, angles):
    half_size = vector.shape[-1] // 2
    first_half = vector[..., :half_size]
    second_half = vector[..., half_size:]
    cosine = jnp.cos(angles)
    sine_part = jnp.sin(angles)
    return jnp.concatenate([first_half * cosine - second_half * sine_part, second_half * cosine + first_half * sine_part], axis=-1)

def segments(group_id, row_count):
    inpack = jnp.arange(row_count, dtype=jnp.int32) % PACK
    grid_side = jnp.where(group_id == 1, SIDE_LARGE, SIDE_SMALL)
    image_count = jnp.where(group_id == 1, IMG_LARGE, IMG_SMALL)
    return jnp.minimum(inpack // (grid_side * grid_side), image_count - 1)

def attend_pack(pack_block):
    queries, keys_in, values, image_id, keep_pack = pack_block
    scores = jnp.einsum('hqd,hkd->hqk', queries, keys_in, precision=PRECISE) * (1.0 / math.sqrt(HD))
    scores = low_back(scores)
    key_valid = (image_id[:, None] == image_id[None, :]) & (keep_pack[None, :] > 0.5)
    masked = jnp.where(key_valid[None], scores, MASK_FILL)
    row_max = lax.optimization_barrier(jnp.max(masked, axis=-1, keepdims=True))
    exp_terms = jnp.where(key_valid[None], jnp.exp(masked - row_max), 0.0)
    attn_probs = exp_terms / lax.optimization_barrier(jnp.sum(exp_terms, axis=-1, keepdims=True))
    return jnp.einsum('hqk,hkd->hqd', low(attn_probs), values, precision=PRECISE)

def layer(params, inputs, group_id, positions, keep_mask):
    gain_one, bias_one, w_qkv, b_qkv, rotary_freqs, w_out, b_out, gain_two, bias_two, w_up, b_up, w_down, b_down = params
    tok_rows = inputs.shape[0]
    pack_count = tok_rows // PACK
    normed = low(layer_norm(inputs, gain_one, bias_one))
    projected = low_back(matmul(normed, w_qkv.reshape(D, 3 * D)) + b_qkv.reshape(3 * D))
    split_heads = projected.reshape(tok_rows, 3, HEADS, HD).transpose(1, 2, 0, 3)
    rows_f = positions[0].astype(jnp.float32)
    cols_f = positions[1].astype(jnp.float32)
    angles = rotary_freqs[0][:, None, :] * rows_f[None, :, None] + rotary_freqs[1][:, None, :] * cols_f[None, :, None]
    queries = low(rotate(split_heads[0], angles))
    keys_in = low(rotate(split_heads[1], angles))
    values = low(split_heads[2])

    def by_pack(vector):
        return vector.reshape(HEADS, pack_count, PACK, HD).transpose(1, 0, 2, 3)
    image_id = segments(group_id, tok_rows).reshape(pack_count, PACK)
    keep_pack = keep_mask.astype(jnp.float32).reshape(pack_count, PACK)
    attended = lax.map(jax.checkpoint(attend_pack), (by_pack(queries), by_pack(keys_in), by_pack(values), image_id, keep_pack))
    attended = attended.transpose(0, 2, 1, 3).reshape(tok_rows, D)
    attended = low(low_back(attended))
    branch = low_back(matmul(attended, w_out) + b_out)
    middle = inputs + branch
    second = low(layer_norm(middle, gain_two, bias_two))
    hidden = low_back(matmul(second, w_up) + b_up)
    active = low(jax.nn.gelu(hidden, approximate=False))
    mlp_branch = low_back(matmul(active, w_down) + b_down)
    return middle + mlp_branch

def reference(tokens, image_group, positions, keep_mask, norm1_gain, norm1_bias, w_qkv, b_qkv, rotary_freqs, w_out, b_out, norm2_gain, norm2_bias, w_up, b_up, w_down, b_down, cotangent):
    floats = (norm1_gain, norm1_bias, w_qkv.astype(jnp.float32), b_qkv, rotary_freqs, w_out.astype(jnp.float32), b_out, norm2_gain, norm2_bias, w_up.astype(jnp.float32), b_up.astype(jnp.float32), w_down.astype(jnp.float32), b_down)
    grouped_pos = positions.reshape(2, N_DP, TOK_DEV).transpose(1, 0, 2)
    grouped_keep = keep_mask.reshape(N_DP, TOK_DEV)

    def forward(inputs, params):

        def one_group(group_item):
            return layer(params, group_item[0], group_item[1], group_item[2], group_item[3])
        result = lax.map(jax.checkpoint(one_group), (inputs.reshape(N_DP, TOK_DEV, D), image_group, grouped_pos, grouped_keep))
        return result.reshape(TOKENS, D)
    output, pullback = jax.vjp(forward, tokens.astype(jnp.float32), floats)
    keep_f = keep_mask.astype(jnp.float32)
    grad_x, grad_list = pullback(cotangent * keep_f[:, None])
    factor = N_DP / jnp.sum(keep_f)
    return (output.astype(jnp.bfloat16), grad_x, grad_list[0] * factor, grad_list[1] * factor, grad_list[2] * factor, grad_list[3] * factor, grad_list[4] * factor, grad_list[5] * factor, grad_list[6] * factor, grad_list[7] * factor, grad_list[8] * factor, grad_list[9] * factor, grad_list[10] * factor, grad_list[11] * factor, grad_list[12] * factor)
```

```python
import math

import jax
import jax.numpy as jnp
from jax import lax
from jax.sharding import PartitionSpec as P

HD = 64
SIDE_SMALL = 14
SIDE_LARGE = 24
IMG_SMALL = 3
IMG_LARGE = 1
NORM_EPS = 1e-06
MASK_FILL = -1e30
BF = jnp.bfloat16
F32 = jnp.float32
SCALE = 1.0 / math.sqrt(HD)


def swap(value, axis, bit):
    size = lax.axis_size(axis)
    return lax.ppermute(value, axis, [(i, i ^ bit) for i in range(size)])


def layer_norm(values, norm_gain, norm_bias):
    row_mean = jnp.mean(values, axis=-1, keepdims=True)
    centered = values - row_mean
    variance = jnp.mean(centered * centered, axis=-1, keepdims=True)
    scale = lax.rsqrt(variance + NORM_EPS)
    unit = centered * scale
    return unit * norm_gain + norm_bias, unit, scale


def norm_back(grad, unit, scale, gain):
    u = grad * gain
    mean_u = jnp.mean(u, axis=-1, keepdims=True)
    mean_un = jnp.mean(u * unit, axis=-1, keepdims=True)
    return scale * (u - mean_u - unit * mean_un)


def halves(value, upper):
    half = value.shape[0] // 2
    mine = lax.dynamic_slice_in_dim(value, upper * half, half, 0)
    other = lax.dynamic_slice_in_dim(value, (1 - upper) * half, half, 0)
    return mine, other


def join(mine, other, upper):
    return jnp.where(
        upper == 0, jnp.concatenate([mine, other]), jnp.concatenate([other, mine])
    )


def gather_weight(own):
    upper = lax.axis_index("dp") % 2
    mine, _ = halves(own, upper)
    got = swap(mine, "mp", 2)
    across = join(got, swap(got, "dp", 1), upper)
    return [own, swap(own, "mp", 1), across, swap(across, "mp", 1)]


def reduce_weight(parts):
    keep = [parts[0] + swap(parts[1], "mp", 1), parts[2] + swap(parts[3], "mp", 1)]
    total = keep[0] + swap(keep[1], "mp", 2)
    index = lax.axis_index("dp")
    size = lax.axis_size("dp")
    upper = index % 2
    mine, other = halves(total, upper)
    total = mine + swap(other, "dp", 1)
    groups = size // 2
    place = index // 2
    rows = total.shape[0] // groups
    pieces = [
        lax.dynamic_slice_in_dim(total, (place ^ step) * rows, rows, 0) for step in range(groups)
    ]
    total = pieces[0].astype(F32)
    for step in range(1, groups):
        total = total + swap(pieces[step], "dp", 2 * step).astype(F32)
    total = total.astype(BF)
    back = [total] + [swap(total, "dp", 2 * step) for step in range(1, groups)]
    stacked = jnp.stack(back)
    order = jnp.arange(groups) ^ place
    total = jnp.take(stacked, order, axis=0).reshape((groups * rows,) + total.shape[1:])
    return join(total, swap(total, "dp", 1), upper)


def reduce_small(vector):
    for axis in ("mp", "dp"):
        bit = 1
        while bit < lax.axis_size(axis):
            vector = vector + swap(vector, axis, bit)
            bit *= 2
    return vector


def turn(values, cosine, sine):
    a, b = values[..., :32], values[..., 32:]
    return jnp.concatenate([a * cosine - b * sine, b * cosine + a * sine], -1)


def dot(left, right):
    return jnp.dot(left, right, preferred_element_type=F32)


def dot_t(left, right):
    return lax.dot_general(left, right, (((0,), (0,)), ((), ())), preferred_element_type=F32)


def dot_r(left, right):
    return lax.dot_general(left, right, (((1,), (1,)), ((), ())), preferred_element_type=F32)


def gelu_both(v):
    cdf = 0.5 * (1.0 + lax.erf(v * (1.0 / math.sqrt(2.0))))
    pdf = jnp.exp(-0.5 * v * v) * (1.0 / math.sqrt(2.0 * math.pi))
    return v * cdf, cdf + v * pdf


def body(
    tokens,
    image_group,
    positions,
    keep_mask,
    norm1_gain,
    norm1_bias,
    w_qkv,
    b_qkv,
    rotary_freqs,
    w_out,
    b_out,
    norm2_gain,
    norm2_bias,
    w_up,
    b_up,
    w_down,
    b_down,
    cotangent,
):
    rows, width = tokens.shape
    parts = lax.axis_size("mp")
    mp_index = lax.axis_index("mp")
    heads = rotary_freqs.shape[1]
    local = heads * HD
    units = w_up.shape[1]
    is_large = image_group[0]
    grid_side = jnp.where(is_large == 1, SIDE_LARGE, SIDE_SMALL)
    image_count = jnp.where(is_large == 1, IMG_LARGE, IMG_SMALL)
    keep_all = keep_mask.astype(F32)
    keep_own = lax.dynamic_slice_in_dim(keep_all, mp_index * rows, rows)
    place = lax.dynamic_slice_in_dim(positions, mp_index * rows, rows, 1).astype(F32)
    inpack = jnp.arange(rows, dtype=jnp.int32)
    image_id = jnp.minimum(inpack // (grid_side * grid_side), image_count - 1)
    visible = (image_id[:, None] == image_id[None, :]) & (keep_own[None, :] > 0.5)

    small = jnp.concatenate(
        [b_qkv.reshape(-1), rotary_freqs.reshape(-1), b_up.astype(F32)]
    )
    smalls = [small, swap(small, "mp", 1), swap(small, "mp", 2), swap(small, "mp", 3)]
    qkv_parts = gather_weight(w_qkv.reshape(width, 3 * local))
    out_parts = gather_weight(w_out)
    up_parts = gather_weight(w_up)
    down_parts = gather_weight(w_down)

    x_own = tokens.astype(F32)
    normed_one, unit1, scale1 = layer_norm(x_own, norm1_gain, norm1_bias)
    normed_b = normed_one.astype(BF)
    saved = []
    branch = b_out
    for r in range(parts):
        bias = smalls[r][: 3 * local]
        freqs = smalls[r][3 * local : 3 * local + heads * HD].reshape(2, heads, HD // 2)
        angles = (
            place[0][:, None, None] * freqs[0][None] + place[1][:, None, None] * freqs[1][None]
        )
        cosine, sine = jnp.cos(angles), jnp.sin(angles)
        projected = (dot(normed_b, qkv_parts[r]) + bias).reshape(rows, 3, heads, HD)
        query = turn(projected[:, 0], cosine, sine)
        key = turn(projected[:, 1], cosine, sine)
        query_b, key_b, value_b = query.astype(BF), key.astype(BF), projected[:, 2].astype(BF)
        scores = jnp.einsum("qhd,khd->hqk", query_b, key_b, preferred_element_type=F32) * SCALE
        masked = jnp.where(visible[None], scores, MASK_FILL)
        row_max = jnp.max(masked, axis=-1, keepdims=True)
        terms = jnp.where(visible[None], jnp.exp(masked - row_max), 0.0)
        row_sum = jnp.sum(terms, axis=-1, keepdims=True)
        probs = terms / row_sum
        attended = jnp.einsum("hqk,khd->qhd", probs.astype(BF), value_b, preferred_element_type=F32)
        attended_b = attended.reshape(rows, local).astype(BF)
        branch = branch + dot(attended_b, out_parts[r])
        saved.append((query, key, query_b, key_b, value_b, probs, attended_b, cosine, sine))
    middle = x_own + branch
    normed_two, unit2, scale2 = layer_norm(middle, norm2_gain, norm2_bias)
    second_b = normed_two.astype(BF)
    grad_out = cotangent * keep_own[:, None]
    grad_out_b = grad_out.astype(BF)
    sum_b_down = jnp.sum(grad_out_b.astype(F32), axis=0)
    mlp = b_down
    grad_second = 0.0
    sums_b_up, raw_up, raw_down = [], [], []
    for r in range(parts):
        hidden = dot(second_b, up_parts[r]) + smalls[r][3 * local + heads * HD :]
        active, slope = gelu_both(hidden)
        active_b = active.astype(BF)
        mlp = mlp + dot(active_b, down_parts[r])
        raw_down.append(dot_t(active_b, grad_out_b).astype(BF))
        grad_hidden_b = (dot_r(grad_out_b, down_parts[r]) * slope).astype(BF)
        raw_up.append(dot_t(second_b, grad_hidden_b).astype(BF))
        sums_b_up.append(jnp.sum(grad_hidden_b.astype(F32), axis=0))
        grad_second = grad_second + dot_r(grad_hidden_b, up_parts[r])
    output = (middle + mlp).astype(BF)
    sum_w_down = reduce_weight(raw_down)
    sum_w_up = reduce_weight(raw_up)
    sum_gain2 = jnp.sum(grad_second * unit2, axis=0)
    sum_bias2 = jnp.sum(grad_second, axis=0)
    grad_middle = grad_out + norm_back(grad_second, unit2, scale2, norm2_gain)
    branch_b = grad_middle.astype(BF)
    sum_b_out = jnp.sum(branch_b.astype(F32), axis=0)
    sum_w_out = reduce_weight([dot_t(saved[r][6], branch_b).astype(BF) for r in range(parts)])
    grad_first = 0.0
    raw_qkv, sums_b_qkv, sums_freqs = [], [], []
    for r in range(parts):
        query, key, query_b, key_b, value_b, probs, attended_b, cosine, sine = saved[r]
        grad_att = dot_r(branch_b, out_parts[r]).astype(BF).reshape(rows, heads, HD)
        grad_probs = jnp.einsum("qhd,khd->hqk", grad_att, value_b, preferred_element_type=F32)
        grad_value = jnp.einsum(
            "hqk,qhd->khd", probs.astype(BF), grad_att, preferred_element_type=F32
        )
        inner = jnp.sum(probs * grad_probs, axis=-1, keepdims=True)
        grad_scores = (probs * (grad_probs - inner)).astype(BF)
        grad_query = (
            jnp.einsum("hqk,khd->qhd", grad_scores, key_b, preferred_element_type=F32) * SCALE
        )
        grad_key = (
            jnp.einsum("hqk,qhd->khd", grad_scores, query_b, preferred_element_type=F32) * SCALE
        )
        term = (
            grad_query[..., 32:] * query[..., :32]
            - grad_query[..., :32] * query[..., 32:]
            + grad_key[..., 32:] * key[..., :32]
            - grad_key[..., :32] * key[..., 32:]
        )
        sums_freqs.append(jnp.einsum("pt,thj->phj", place, term, precision=lax.Precision.HIGHEST))
        grad_qkv = jnp.concatenate(
            [
                turn(grad_query, cosine, -sine).reshape(rows, local),
                turn(grad_key, cosine, -sine).reshape(rows, local),
                grad_value.reshape(rows, local),
            ],
            axis=1,
        ).astype(BF)
        raw_qkv.append(dot_t(normed_b, grad_qkv).astype(BF))
        sums_b_qkv.append(jnp.sum(grad_qkv.astype(F32), axis=0))
        grad_first = grad_first + dot_r(grad_qkv, qkv_parts[r])
    sum_w_qkv = reduce_weight(raw_qkv)
    sum_gain1 = jnp.sum(grad_first * unit1, axis=0)
    sum_bias1 = jnp.sum(grad_first, axis=0)
    grad_tokens = grad_middle + norm_back(grad_first, unit1, scale1, norm1_gain)

    slot = [
        jnp.concatenate([sums_b_qkv[r], sums_freqs[r].reshape(-1), sums_b_up[r]])
        for r in range(parts)
    ]
    slots = jnp.take(jnp.stack(slot), jnp.arange(parts) ^ mp_index, axis=0)
    packed = jnp.concatenate(
        [
            jnp.stack([sum_gain1, sum_bias1, sum_b_out, sum_gain2, sum_bias2, sum_b_down]).reshape(-1),
            slots.reshape(-1),
            jnp.full((128,), jnp.sum(keep_own)),
        ]
    ).reshape(-1, 128)
    packed = reduce_small(packed).reshape(-1)
    factor = lax.axis_size("dp") / packed[-1]
    packed = packed * factor
    vectors = packed[: 6 * width].reshape(6, width)
    own = lax.dynamic_slice_in_dim(
        packed[6 * width : -128].reshape(parts, -1), mp_index, 1, 0
    )[0]
    return (
        output,
        grad_tokens,
        vectors[0],
        vectors[1],
        (sum_w_qkv.astype(F32) * factor).reshape(w_qkv.shape),
        own[: 3 * local].reshape(3, local),
        own[3 * local : 3 * local + heads * HD].reshape(rotary_freqs.shape),
        sum_w_out.astype(F32) * factor,
        vectors[2],
        vectors[3],
        vectors[4],
        sum_w_up.astype(F32) * factor,
        own[3 * local + heads * HD :],
        sum_w_down.astype(F32) * factor,
        vectors[5],
    )


def solution(mesh):
    placed = (
        P(("dp", "mp"), None),
        P("dp"),
        P(None, "dp"),
        P("dp"),
        P(),
        P(),
        P(None, None, "mp"),
        P(None, "mp"),
        P(None, "mp", None),
        P("mp", None),
        P(),
        P(),
        P(),
        P(None, "mp"),
        P("mp"),
        P("mp", None),
        P(),
        P(("dp", "mp"), None),
    )
    return jax.shard_map(
        body,
        mesh=mesh,
        in_specs=placed,
        out_specs=(
            P(("dp", "mp"), None),
            P(("dp", "mp"), None),
            P(),
            P(),
            P(None, None, "mp"),
            P(None, "mp"),
            P(None, "mp", None),
            P("mp", None),
            P(),
            P(),
            P(),
            P(None, "mp"),
            P("mp"),
            P("mp", None),
            P(),
        ),
        check_vma=False,
    )
```

```python
import math
import functools

import jax
import jax.numpy as jnp
from jax import lax
from jax.experimental import pallas as pl
from jax.experimental.pallas import tpu as pltpu
from jax.sharding import PartitionSpec as P

HD = 64
SIDE_SMALL = 14
SIDE_LARGE = 24
IMG_SMALL = 3
IMG_LARGE = 1
NORM_EPS = 1e-06
HIDE = -1e30
BF = jnp.bfloat16
F32 = jnp.float32
SCALE = 1.0 / math.sqrt(HD)
HALF = HD // 2
LANES = 128
AUG = HD + 16


def nn(a, b):
    return jnp.dot(a, b, preferred_element_type=F32)


def tn(a, b):
    return lax.dot_general(a, b, (((0,), (0,)), ((), ())), preferred_element_type=F32)


def nt(a, b):
    return lax.dot_general(a, b, (((1,), (1,)), ((), ())), preferred_element_type=F32)


def unit_of(values):
    mean = jnp.mean(values, axis=-1, keepdims=True)
    centered = values - mean
    variance = jnp.mean(centered * centered, axis=-1, keepdims=True)
    scale = lax.rsqrt(variance + NORM_EPS)
    return centered * scale, scale


def norm_back(grad, unit, scale, gain):
    u = grad * gain
    mean_u = jnp.mean(u, axis=-1, keepdims=True)
    mean_un = jnp.mean(u * unit, axis=-1, keepdims=True)
    return scale * (u - mean_u - unit * mean_un)


def gelu_both(v):
    cdf = 0.5 * (1.0 + lax.erf(v * (1.0 / math.sqrt(2.0))))
    pdf = jnp.exp(-0.5 * v * v) * (1.0 / math.sqrt(2.0 * math.pi))
    return v * cdf, cdf + v * pdf


def pad_rows(value, rows):
    return jnp.concatenate(
        [value, jnp.zeros((rows - value.shape[0],) + value.shape[1:], value.dtype)]
    )


def first_norm(tokens, vec, normed1):
    unit, _ = unit_of(tokens[...].astype(F32))
    normed = (unit * vec[0:1] + vec[1:2]).astype(BF)
    normed1[...] = pad_rows(normed, normed1.shape[0])


def masks(rows, place, group, feats, keep):
    wide = place.shape[1]
    slot = lax.broadcasted_iota(jnp.int32, (16, wide), 1)
    row = lax.broadcasted_iota(jnp.int32, (16, wide), 0)
    image_id = jnp.zeros((16, wide), jnp.int32)
    for is_large, side, images in ((0, SIDE_SMALL, IMG_SMALL), (1, SIDE_LARGE, IMG_LARGE)):
        mine = sum([(slot >= n * side * side).astype(jnp.int32) for n in range(1, images)], jnp.zeros((16, wide), jnp.int32))
        image_id = jnp.where(group[0] == is_large, mine, image_id)
    same = (image_id == row) & (row < max(IMG_SMALL, IMG_LARGE))
    hidden = jnp.logical_not(same & (place[2:3] > 0.5)) & (row < max(IMG_SMALL, IMG_LARGE))
    feats[0] = jnp.where(same, 1.0, 0.0).astype(BF)
    feats[1] = jnp.where(hidden, HIDE, 0.0).astype(BF)
    feats[2] = jnp.where(row == 0, 1.0, 0.0).astype(BF)
    keep[...] = place[...].T[:rows, 2:3]


def attend_chunk(r, heads, rows, normed1, wq, small, place, feats, q_all, k_all, v_all, lse, att, cosine, sine, proj):
    local = heads * HD
    column = small[r].T[:, 1:2]
    f0 = column[3 * local : 3 * local + heads * HALF]
    f1 = column[3 * local + heads * HALF : 3 * local + 2 * heads * HALF]
    angles = f0 * place[0:1] + f1 * place[1:2]
    cosine[r] = jnp.cos(angles)
    sine[r] = jnp.sin(angles)
    proj[...] = nt(wq[r], normed1[...]) + column[: 3 * local]
    for h in range(heads):
        cos_h = cosine[r, h * HALF : (h + 1) * HALF]
        sin_h = sine[r, h * HALF : (h + 1) * HALF]
        at = r * heads + h
        for base, ref, scale in ((0, q_all, SCALE), (local, k_all, 1.0)):
            a = proj[base + h * HD : base + h * HD + HALF]
            b = proj[base + h * HD + HALF : base + (h + 1) * HD]
            ref[at, :HALF] = ((a * cos_h - b * sin_h) * scale).astype(BF)
            ref[at, HALF:HD] = ((b * cos_h + a * sin_h) * scale).astype(BF)
        v_all[at, :HD] = proj[2 * local + h * HD : 2 * local + (h + 1) * HD].astype(BF)
        q_all[at, HD:] = feats[0]
        k_all[at, HD:] = feats[1]
        v_all[at, HD:] = feats[2]

    def head(h, carry):
        at = r * heads + h
        scores = tn(k_all[at, :, :rows], q_all[at])
        top = jnp.max(scores, axis=0, keepdims=True)
        terms = jnp.exp(scores - top).astype(BF)
        mixed = nn(v_all[at, :, :rows], terms)
        total = mixed[HD : HD + 1]
        att[pl.ds(pl.multiple_of(at * HD, HD), HD)] = (mixed[:HD] * (1.0 / total)).astype(BF)
        lse[at] = jnp.broadcast_to(top + jnp.log(total), lse.shape[1:])
        return carry

    lax.fori_loop(0, heads, head, 0)


def second_norm(rows, tokens, vec, att, wo, middle, normed2):
    branch = tn(att[...], wo[...].reshape(att.shape[0], wo.shape[2]))
    middle[...] = tokens[...].astype(F32) + branch[:rows] + vec[4:5]
    unit, _ = unit_of(middle[...])
    normed2[...] = (unit * vec[2:3] + vec[3:4]).astype(BF)


def mlp_chunk(r, first, normed2, g, wu, wd, small, mlp, gsecond, target, sums, active, slope, hook):
    width = normed2.shape[1]
    hidden = nn(normed2[...], wu[r]) + small[r][0:1]
    act, der = gelu_both(hidden)
    active[...] = act.astype(BF)
    slope[...] = der
    hook(0)
    target[width:] = tn(active[...], g[...]).astype(BF)
    hook(1)
    if first:
        mlp[...] = nn(active[...], wd[r])
    else:
        mlp[...] += nn(active[...], wd[r])
    hook(2)
    gh = nt(g[...], wd[r]) * slope[...]
    active[...] = gh.astype(BF)
    hook(3)
    sums[r] = jnp.sum(active[...].astype(F32), axis=0, keepdims=True)
    target[:width] = tn(normed2[...], active[...]).astype(BF)
    hook(4)
    if first:
        gsecond[...] = nt(active[...], wu[r])
    else:
        gsecond[...] += nt(active[...], wu[r])
    hook(5)


def finish_mlp(cot, keep, vec, middle, mlp, gsecond, g, out, branch, sums_vec):
    out[...] = (middle[...] + mlp[...] + vec[5:6]).astype(BF)
    unit, scale = unit_of(middle[...])
    grad = gsecond[...]
    gm = cot[...] * keep[...] + norm_back(grad, unit, scale, vec[2:3])
    low = gm.astype(BF)
    sums_vec[...] = jnp.concatenate(
        [
            jnp.sum(low.astype(F32), axis=0, keepdims=True),
            jnp.sum(grad * unit, axis=0, keepdims=True),
            jnp.sum(grad, axis=0, keepdims=True),
            jnp.sum(g[...].astype(F32), axis=0, keepdims=True),
            jnp.full((4, grad.shape[1]), 1.0, F32) * jnp.sum(keep[...]),
        ]
    )
    middle[...] = gm
    branch[...] = pad_rows(low, branch.shape[0])


def attend_back(at, heads, rows, q_all, k_all, v_all, lse, att, gatt, cosine, sine, place, gqkv, column, sums):
    local = heads * HD
    r, h = at // heads, at % heads
    here = pl.ds(pl.multiple_of(at * HD, HD), HD)
    wide = q_all.shape[2]
    scores = tn(k_all[at, :, :rows], q_all[at])
    probs = jnp.exp(scores - lse[at, 0:1])
    go = gatt[here]
    inner = jnp.sum(go.astype(F32) * att[here].astype(F32), axis=0, keepdims=True)
    gp = tn(v_all[at, :HD, :rows], go)
    gs = (probs * (gp - inner)).astype(BF)
    gv = nt(go, probs.astype(BF))
    gk = nt(q_all[at, :HD], gs)
    gq = nn(k_all[at, :HD, :rows], gs) * SCALE
    hs = pl.ds(pl.multiple_of(h * HALF, HALF), HALF)
    cos_h, sin_h = cosine[r, hs], sine[r, hs]
    term = jnp.zeros((HALF, wide), F32)
    pad = jnp.zeros((HD, wide - rows), F32)
    gk = jnp.concatenate([gk, pad], axis=1)
    gv = jnp.concatenate([gv, pad], axis=1)
    lows = []
    for ref, grad, back in ((q_all, gq, 1.0 / SCALE), (k_all, gk, 1.0)):
        a, b = grad[:HALF], grad[HALF:]
        ra = ref[at, :HALF].astype(F32)
        rb = ref[at, HALF:HD].astype(F32)
        term += (b * ra - a * rb) * back
        lows.append(jnp.concatenate([a * cos_h + b * sin_h, b * cos_h - a * sin_h], axis=0).astype(BF))
    lows.append(gv.astype(BF))
    for n, low in enumerate(lows):
        gqkv[r, pl.ds(pl.multiple_of(n * local + h * HD, HD), HD), :wide] = low
        total = jnp.sum(low.astype(F32), axis=1, keepdims=True)
        column[n * HD : (n + 1) * HD] = jnp.broadcast_to(total, (HD, LANES))
    for n in range(2):
        total = jnp.sum(term * place[n : n + 1], axis=1, keepdims=True)
        column[3 * HD + n * HALF : 3 * HD + (n + 1) * HALF] = jnp.broadcast_to(total, (HALF, LANES))
    sums[pl.ds(at, 1)] = column[...].T[0:1]


UNIT = 128
DEPTH = 3
CUTS = (2, 1, 3, 3)
SLOTS = 6
TILE = 16
BITS_MP = (1, 2)


def flip(axis, bit):
    me = lax.axis_index(axis)
    return {axis: me + bit * (1 - 2 * ((me // bit) % 2))}


def bit_of(axis, bit):
    return (lax.axis_index(axis) // bit) % 2


def powers(axis):
    size = lax.axis_size(axis)
    return [1 << k for k in range(size.bit_length() - 1)]


def greet(peers):
    barrier = pltpu.get_barrier_semaphore()
    for peer in peers:
        pl.semaphore_signal(barrier, inc=1, device_id=peer, device_id_type=pl.DeviceIdType.MESH)
    pl.semaphore_wait(barrier, len(peers))


def remote(src, dst, send, recv, peer):
    return pltpu.make_async_remote_copy(
        src_ref=src, dst_ref=dst, send_sem=send, recv_sem=recv, device_id=peer, device_id_type=pl.DeviceIdType.MESH
    )


def steps_of(bits):
    sizes, size = [], UNIT
    for _ in bits:
        if size // 2 >= TILE:
            size //= 2
        sizes.append(size)
    return sizes


class Gather:
    def __init__(self, shards, full, cuts, send, recv, send_w, recv_w, local):
        self.shards, self.full = shards, full
        self.upper = bit_of("dp", 1)
        self.pieces = []
        for w, cut in enumerate(cuts):
            half = shards[w].shape[0] // 2
            for n in range(cut):
                self.pieces.append((w, half, n * (half // cut), half // cut))
        self.send, self.recv = send, recv
        self.send_w, self.recv_w, self.local = send_w, recv_w, local

    def rows(self, i, upper):
        _, half, start, size = self.pieces[i]
        return pl.ds(pl.multiple_of(upper * half + start, TILE), size)

    def pass_on(self, i, stage, source, target, rows, peer):
        w = self.pieces[i][0]
        full = self.full[w]
        src = self.shards[w].at[rows] if source is None else full.at[source, rows]
        return remote(src, full.at[target, rows], self.send.at[stage, i], self.recv.at[stage, i], peer)

    def across(self, i):
        return self.pass_on(i, 0, None, 2, self.rows(i, self.upper), flip("mp", 2))

    def beside(self, i):
        return self.pass_on(i, 1, 2, 2, self.rows(i, self.upper), flip("dp", 1))

    def near_half(self, i):
        return self.pass_on(i, 2, 2, 3, self.rows(i, self.upper), flip("mp", 1))

    def far_half(self, i):
        return self.pass_on(i, 3, 2, 3, self.rows(i, 1 - self.upper), flip("mp", 1))

    def whole(self, w):
        return remote(self.shards[w], self.full[w].at[1], self.send_w.at[w], self.recv_w.at[w], flip("mp", 1))

    def own(self, w):
        return pltpu.make_async_copy(self.shards[w], self.full[w].at[0], self.local.at[w])

    def got_across(self, i):
        self.across(i).wait()
        self.beside(i).start()
        self.near_half(i).start()
        if i + DEPTH < len(self.pieces):
            self.across(i + DEPTH).start()

    def got_beside(self, i):
        self.beside(i).wait()
        self.far_half(i).start()

    def got_all(self, i):
        self.near_half(i).wait()
        self.far_half(i).wait()


class Reducer:
    def __init__(self, units, early, near, keep, cross, got1, got3, got2, got_dp, total, send, recv):
        self.units, self.early, self.near = units, early, near
        self.keep, self.cross = keep, cross
        self.got1, self.got3, self.got2, self.got_dp = got1, got3, got2, got_dp
        self.total, self.send, self.recv = total, send, recv
        self.bits = powers("dp")
        self.sizes = steps_of(self.bits)
        count = len(self.bits)
        self.halved = [k for k in range(count) if self.sizes[k] < (UNIT if k == 0 else self.sizes[k - 1])]
        offset, self.offsets = 0, []
        for k in range(count):
            if k in self.halved:
                offset = offset + bit_of("dp", self.bits[k]) * self.sizes[k]
            self.offsets.append(offset)
        self.last = 4 + count + len(self.halved)
        self.ticks = units + self.last

    def rows(self, u, size, offset=0, base=UNIT):
        return pl.ds(pl.multiple_of(u * base + offset, TILE), size)

    def slot(self, u, size):
        return pl.ds(pl.multiple_of((u % SLOTS) * size, TILE), size)

    def first(self, u):
        at, here, peer = self.rows(u % self.early, UNIT), self.slot(u, UNIT), flip("mp", 1)
        return (
            remote(self.near.at[0, at], self.got1.at[here], self.send.at[0, u], self.recv.at[0, u], peer),
            remote(self.near.at[1, at], self.got3.at[here], self.send.at[1, u], self.recv.at[1, u], peer),
        )

    def second(self, u):
        return remote(
            self.cross.at[self.rows(u, UNIT)],
            self.got2.at[self.slot(u, UNIT)],
            self.send.at[2, u],
            self.recv.at[2, u],
            flip("mp", 2),
        )

    def spread(self, u, k):
        size = self.sizes[k]
        if k in self.halved:
            before = self.offsets[k - 1] if k else 0
            offset = before + (1 - bit_of("dp", self.bits[k])) * size
        else:
            offset = self.offsets[k]
        return remote(
            self.keep.at[self.rows(u, size, offset)],
            self.got_dp[k].at[self.slot(u, size)],
            self.send.at[3 + k, u],
            self.recv.at[3 + k, u],
            flip("dp", self.bits[k]),
        )

    def gather(self, u, n):
        k = self.halved[len(self.halved) - 1 - n]
        part = self.total.at[self.rows(u, self.sizes[k], self.offsets[k])]
        stage = 3 + len(self.bits) + n
        return remote(part, part, self.send.at[stage, u], self.recv.at[stage, u], flip("dp", self.bits[k]))

    def add(self, source, target, u, size, offset, terms):
        def tile(i, carry):
            at = pl.ds(pl.multiple_of(u * UNIT + offset + i * TILE, TILE), TILE)
            value = source[at].astype(F32)
            for ref in terms:
                value += ref[pl.ds(pl.multiple_of((u % SLOTS) * size + i * TILE, TILE), TILE)].astype(F32)
            target[at] = value.astype(BF)
            return carry

        lax.fori_loop(0, size // TILE, tile, 0)

    def tick(self, t):
        units, count = self.units, len(self.bits)

        def at(lag, body):
            u = t - lag

            @pl.when((u >= 0) & (u < units))
            def _():
                body(u)

        def start_first(u):
            for copy in self.first(u):
                copy.start()

        def after_first(u):
            for copy in self.first(u):
                copy.wait()
            self.add(self.cross, self.cross, u, UNIT, 0, [self.got3])
            self.second(u).start()

        def after_second(u):
            self.second(u).wait()
            self.add(self.keep, self.keep, u, UNIT, 0, [self.got1, self.got2])
            self.spread(u, 0).start()

        def after_spread(k):
            def body(u):
                self.spread(u, k).wait()
                size = self.sizes[k]
                final = k == count - 1
                self.add(self.keep, self.total if final else self.keep, u, size, self.offsets[k], [self.got_dp[k]])
                if final:
                    self.gather(u, 0).start()
                else:
                    self.spread(u, k + 1).start()

            return body

        def after_gather(n):
            def body(u):
                self.gather(u, n).wait()
                if n + 1 < len(self.halved):
                    self.gather(u, n + 1).start()

            return body

        at(0, start_first)
        at(1, after_first)
        at(3, after_second)
        for k in range(count):
            at(4 + k, after_spread(k))
        for n in range(len(self.halved)):
            at(4 + count + n, after_gather(n))


class SmallSum:
    def __init__(self, value, got, send, recv):
        self.value, self.got, self.send, self.recv = value, got, send, recv
        self.peers = [flip("mp", b) for b in BITS_MP] + [flip("dp", b) for b in powers("dp")]

    def copy(self, k):
        return remote(self.value, self.got.at[k], self.send.at[k], self.recv.at[k], self.peers[k])

    def finish(self, k):
        self.copy(k).wait()
        value, got = self.value, self.got
        value[:8] += got[k, :8]
        if k == 0:
            value[8:10] += got[k, 10:12]
            value[12:14] += got[k, 14:16]
        elif k == 1:
            value[8:10] += got[k, 12:14]
        else:
            value[8:10] += got[k, 8:10]


def layer_body(
    heads,
    rows,
    tokens,
    gain1,
    bias1,
    gain2,
    bias2,
    bias_out,
    bias_down,
    place,
    group,
    cot,
    s_qkv,
    s_out,
    s_up,
    s_down,
    s_small,
    out,
    gx,
    o_up,
    o_down,
    o_out,
    o_qkv,
    small_sum,
    factor_out,
    wq,
    wo,
    wu,
    wd,
    small,
    q_all,
    k_all,
    v_all,
    lse,
    att,
    cosine,
    sine,
    normed1,
    middle,
    branch,
    g,
    mlp,
    gsecond,
    active,
    slope,
    vec,
    keep_col,
    feats,
    sums_up,
    sums_vec,
    column,
    head_sums,
    near,
    keep,
    cross,
    got1,
    got3,
    got2,
    total,
    got_small,
    send_g,
    recv_g,
    send_w,
    recv_w,
    send_s,
    recv_s,
    local_sem,
    send,
    recv,
    send_v,
    recv_v,
    *got_dp,
):
    parts, count = wq.shape[0], q_all.shape[0]
    local = heads * HD
    width = tokens.shape[1]
    wide = q_all.shape[2]
    mlp_rows = near.shape[1]
    early, units = mlp_rows // UNIT, keep.shape[0] // UNIT
    weights = Gather((s_qkv, s_out, s_up, s_down), (wq, wo, wu, wd), CUTS, send_g, recv_g, send_w, recv_w, local_sem)
    owns = [weights.own(w) for w in range(4)]
    load_small = pltpu.make_async_copy(s_small, small.at[0], local_sem.at[4])
    load_cot = pltpu.make_async_copy(cot, slope, local_sem.at[5])
    owns[0].start()
    load_small.start()
    both = {"mp": lax.axis_index("mp") + 1 * (1 - 2 * bit_of("mp", 1)) + 2 * (1 - 2 * bit_of("mp", 2))}
    sums = SmallSum(small_sum, got_small, send_v, recv_v)
    greet(sums.peers + [both])
    peers = [flip("mp", 1), flip("mp", 2), both]
    smalls = [
        remote(s_small, small.at[r], send_s.at[r - 1], recv_s.at[r - 1], peers[r - 1]) for r in range(1, 4)
    ]
    for copy in smalls:
        copy.start()
    for i in range(DEPTH):
        weights.across(i).start()
    weights.whole(0).start()
    for n, ref in enumerate((gain1, bias1, gain2, bias2, bias_out, bias_down)):
        vec[n : n + 1] = ref[...].reshape(1, width)
    first_norm(tokens, vec, normed1)
    masks(rows, place, group, feats, keep_col)
    owns[0].wait()
    load_small.wait()
    weights.whole(1).start()
    for w in (1, 2, 3):
        owns[w].start()
    load_cot.start()
    proj = mlp.at[: 3 * local, :wide]

    def chunk(r):
        attend_chunk(r, heads, rows, normed1, wq, small, place, feats, q_all, k_all, v_all, lse, att, cosine, sine, proj)

    chunk(0)
    weights.got_across(0)
    weights.whole(0).wait()
    smalls[0].wait()
    weights.whole(2).start()
    chunk(1)
    weights.whole(3).start()
    weights.got_across(1)
    weights.got_beside(0)
    load_cot.wait()
    g[...] = (slope[...] * keep_col[...]).astype(BF)
    weights.got_across(2)
    smalls[1].wait()
    weights.got_beside(1)
    chunk(2)
    weights.got_beside(2)
    weights.got_across(3)
    weights.got_all(0)
    weights.got_all(1)
    smalls[2].wait()
    chunk(3)
    weights.got_across(4)
    weights.got_beside(3)
    owns[1].wait()
    weights.whole(1).wait()
    weights.got_all(2)
    normed2 = branch.at[:rows]
    second_norm(rows, tokens, vec, att, wo, middle, normed2)
    weights.got_across(5)
    weights.got_beside(4)
    owns[2].wait()
    owns[3].wait()
    todo = {
        0: [[], [("a", 6), ("b", 5)], [], [("a", 7)], [("b", 6)], []],
        1: [[], [("a", 8), ("b", 7)], [], [], [("b", 8)], []],
    }

    def hook(r, n):
        for kind, i in todo.get(r, [[]] * 6)[n]:
            (weights.got_across if kind == "a" else weights.got_beside)(i)

    targets = [keep.at[:mlp_rows], near.at[0], cross.at[:mlp_rows], near.at[1]]
    for r in range(parts):
        if r == 1:
            weights.whole(2).wait()
            weights.whole(3).wait()
        if r == 3:
            for i in range(3, 9):
                weights.got_all(i)
        mlp_chunk(r, r == 0, normed2, g, wu, wd, small, mlp, gsecond, targets[r], sums_up, active, slope, functools.partial(hook, r))
    load_cot.start()
    net = Reducer(units, early, near, keep, cross, got1, got3, got2, got_dp, total, send, recv)

    def step(t, carry):
        net.tick(t)
        return carry

    def ticks(start, stop):
        lax.fori_loop(start, stop, step, 0)

    ticks(0, 1)
    load_cot.wait()
    finish_mlp(slope, keep_col, vec, middle, mlp, gsecond, g, active, branch, sums_vec)
    store_out = pltpu.make_async_copy(active, out, local_sem.at[6])
    store_out.start()
    ticks(1, 2)
    gatt = wd.at[0, :, :wide]
    gqkv = wu
    gatt[...] = nt(wo[...].reshape(parts * local, width), branch[...]).astype(BF)

    def some_heads(i, carry):
        net.tick(2 + i)

        def head(n, c):
            attend_back(2 * i + n, heads, rows, q_all, k_all, v_all, lse, att, gatt, cosine, sine, place, gqkv, column, head_sums)
            return c

        return lax.fori_loop(0, 2, head, carry)

    lax.fori_loop(0, count // 2, some_heads, 0)
    base = 2 + count // 2
    for r, (ref, at) in enumerate(((keep, None), (near, 0), (cross, None), (near, 1))):
        ticks(base + r, base + r + 1)
        out_r = nn(att[r * local : (r + 1) * local], branch[...]).astype(BF)
        qkv_r = nn(gqkv[r, : 3 * local, :wide], normed1[...]).astype(BF)
        if at is None:
            ref[mlp_rows : mlp_rows + local] = out_r
            ref[mlp_rows + local : mlp_rows + 4 * local] = qkv_r
        else:
            ref[at, :local] = out_r
            ref[at, local : 4 * local] = qkv_r
        part = tn(gqkv[r, : 3 * local, :wide], wq[r])[:rows]
        gsecond[...] = part if r == 0 else gsecond[...] + part
    base = base + parts
    ticks(base, base + 1)
    grad = gsecond[...]
    unit, scale = unit_of(tokens[...].astype(F32))
    gsecond[...] = middle[...] + norm_back(grad, unit, scale, vec[0:1])
    store_gx = pltpu.make_async_copy(gsecond, gx, local_sem.at[7])
    store_gx.start()
    small_sum[...] = jnp.zeros_like(small_sum)
    small_sum[0:1] = jnp.sum(grad * unit, axis=0, keepdims=True)
    small_sum[1:2] = jnp.sum(grad, axis=0, keepdims=True)
    small_sum[2:7] = sums_vec[0:5]
    for r in range(parts):
        small_sum[8 + 2 * r : 9 + 2 * r] = sums_up[r]
        mine = [head_sums[r * heads + h : r * heads + h + 1] for h in range(heads)]
        pieces = [v[:, n * HD : (n + 1) * HD] for n in range(3) for v in mine]
        pieces += [v[:, 3 * HD + n * HALF : 3 * HD + (n + 1) * HALF] for n in range(2) for v in mine]
        small_sum[9 + 2 * r : 10 + 2 * r] = jnp.concatenate(pieces, axis=1)
    base = base + 1
    exchanges = len(sums.peers)

    def step_small(t, carry):
        net.tick(t)
        for k in range(exchanges + 1):
            @pl.when(t == base + k)
            def _():
                if k > 0:
                    sums.finish(k - 1)
                if k == exchanges:
                    factor = lax.axis_size("dp") / small_sum[6:7]
                    factor_out[0] = factor[0, 0]
                    small_sum[...] *= factor
                if k < exchanges:
                    sums.copy(k).start()
        return carry

    lax.fori_loop(base, base + exchanges + 1, step_small, 0)
    ticks(base + exchanges + 1, max(net.ticks, base + exchanges + 1))
    stores = []
    start = 0
    for n, ref in enumerate((o_up, o_down, o_out, o_qkv)):
        stores.append(pltpu.make_async_copy(total.at[pl.ds(start, ref.shape[0])], ref, local_sem.at[8 + n]))
        stores[-1].start()
        start += ref.shape[0]
    for copy in stores + [store_out, store_gx]:
        copy.wait()


def sds(shape, dtype):
    return jax.ShapeDtypeStruct(shape, dtype)


def body(
    tokens,
    image_group,
    positions,
    keep_mask,
    norm1_gain,
    norm1_bias,
    w_qkv,
    b_qkv,
    rotary_freqs,
    w_out,
    b_out,
    norm2_gain,
    norm2_bias,
    w_up,
    b_up,
    w_down,
    b_down,
    cotangent,
):
    rows, width = tokens.shape
    wide = -(-rows // LANES) * LANES
    parts = lax.axis_size("mp")
    mp_index = lax.axis_index("mp")
    heads = rotary_freqs.shape[1]
    local = heads * HD
    units = w_up.shape[1]
    spots = jnp.concatenate([positions, keep_mask[None]]).reshape(3, parts, rows)
    spots = lax.dynamic_index_in_dim(spots, mp_index, 1, keepdims=False).astype(F32)
    place = jnp.pad(spots, ((0, 5), (0, wide - rows)))

    def spot(value, row, lane):
        return jnp.pad(value, ((row, 7 - row), (lane, width - lane - value.shape[1])))

    small = spot(b_up[None].astype(F32), 0, 0)
    for n in range(3):
        small += spot(b_qkv[n : n + 1], 1, n * local)
    for n in range(2):
        for h in range(heads):
            small += spot(rotary_freqs[n, h : h + 1], 1, 3 * local + (n * heads + h) * HALF)
    w_qkv_t = w_qkv.reshape(width, 3 * local).T
    count = parts * heads
    bits = powers("dp")
    sizes = steps_of(bits)
    stages = 3 + 2 * len(bits)
    total_rows = 2 * width + 4 * local
    unit_count = total_rows // UNIT
    pieces = sum(CUTS)
    swaps = 2 + len(bits)
    in_vmem = pl.BlockSpec(memory_space=pltpu.VMEM)
    in_smem = pl.BlockSpec(memory_space=pltpu.SMEM)
    anywhere = pl.BlockSpec(memory_space=pl.ANY)
    dma = pltpu.SemaphoreType.DMA
    vmem = pltpu.VMEM
    out, gx, o_up, o_down, o_out, o_qkv, small_sum, factor = pl.pallas_call(
        functools.partial(layer_body, heads, rows),
        out_shape=[
            sds((rows, width), BF),
            sds((rows, width), F32),
            sds((width, units), BF),
            sds((units, width), BF),
            sds((local, width), BF),
            sds((3 * local, width), BF),
            sds((16, width), F32),
            sds((1,), F32),
        ],
        in_specs=[in_vmem] * 8 + [in_smem] + [anywhere] * 6,
        out_specs=[anywhere] * 6 + [in_vmem, in_smem],
        scratch_shapes=[
            vmem((parts, 3 * local, width), BF),
            vmem((parts, local, width), BF),
            vmem((parts, width, units), BF),
            vmem((parts, units, width), BF),
            vmem((parts, 8, width), F32),
            vmem((count, AUG, wide), BF),
            vmem((count, AUG, wide), BF),
            vmem((count, AUG, wide), BF),
            vmem((count, 8, wide), F32),
            vmem((count * HD, wide), BF),
            vmem((parts, heads * HALF, wide), F32),
            vmem((parts, heads * HALF, wide), F32),
            vmem((wide, width), BF),
            vmem((rows, width), F32),
            vmem((wide, width), BF),
            vmem((rows, width), BF),
            vmem((rows, width), F32),
            vmem((rows, width), F32),
            vmem((rows, units), BF),
            vmem((rows, units), F32),
            vmem((8, width), F32),
            vmem((rows, 1), F32),
            vmem((3, 16, wide), BF),
            vmem((parts, 1, units), F32),
            vmem((8, width), F32),
            vmem((3 * HD + 2 * HALF, LANES), F32),
            vmem((-(-count // 8) * 8, 3 * HD + 2 * HALF), F32),
            vmem((2, 2 * width, width), BF),
            vmem((total_rows, width), BF),
            vmem((total_rows, width), BF),
            vmem((SLOTS * UNIT, width), BF),
            vmem((SLOTS * UNIT, width), BF),
            vmem((SLOTS * UNIT, width), BF),
            vmem((total_rows, width), BF),
            vmem((swaps, 16, width), F32),
            dma((4, pieces)),
            dma((4, pieces)),
            dma((4,)),
            dma((4,)),
            dma((3,)),
            dma((3,)),
            dma((12,)),
            dma((stages, unit_count)),
            dma((stages, unit_count)),
            dma((swaps,)),
            dma((swaps,)),
        ]
        + [vmem((SLOTS * size, width), BF) for size in sizes],
        compiler_params=pltpu.CompilerParams(vmem_limit_bytes=61 << 20, collective_id=0, has_side_effects=True),
    )(tokens, norm1_gain, norm1_bias, norm2_gain, norm2_bias, b_out, b_down, place, image_group, cotangent, w_qkv_t,
      w_out, w_up, w_down, small)
    factor = factor[0]

    def final(value):
        return value.astype(F32) * factor

    sum_w_up, sum_w_down, sum_w_out, sum_w_qkv = final(o_up), final(o_down), final(o_out), final(o_qkv).T
    return (
        out,
        gx,
        small_sum[0],
        small_sum[1],
        sum_w_qkv.reshape(w_qkv.shape),
        small_sum[9, : 3 * local].reshape(3, local),
        small_sum[9, 3 * local :].reshape(rotary_freqs.shape),
        sum_w_out,
        small_sum[2],
        small_sum[3],
        small_sum[4],
        sum_w_up,
        small_sum[8],
        sum_w_down,
        small_sum[5],
    )


def solution(mesh):
    placed = (
        P(("dp", "mp"), None),
        P("dp"),
        P(None, "dp"),
        P("dp"),
        P(),
        P(),
        P(None, None, "mp"),
        P(None, "mp"),
        P(None, "mp", None),
        P("mp", None),
        P(),
        P(),
        P(),
        P(None, "mp"),
        P("mp"),
        P("mp", None),
        P(),
        P(("dp", "mp"), None),
    )
    return jax.shard_map(
        body,
        mesh=mesh,
        in_specs=placed,
        out_specs=(
            P(("dp", "mp"), None),
            P(("dp", "mp"), None),
            P(),
            P(),
            P(None, None, "mp"),
            P(None, "mp"),
            P(None, "mp", None),
            P("mp", None),
            P(),
            P(),
            P(),
            P(None, "mp"),
            P("mp"),
            P("mp", None),
            P(),
        ),
        check_vma=False,
    )
```

```python
import math
import functools

import jax
import jax.numpy as jnp
from jax import lax
from jax.experimental import pallas as pl
from jax.experimental.pallas import tpu as pltpu
from jax.sharding import PartitionSpec as P

HD = 64
SIDE_SMALL = 14
SIDE_LARGE = 24
IMG_SMALL = 3
IMG_LARGE = 1
NORM_EPS = 1e-06
HIDE = -1e30
BF = jnp.bfloat16
F32 = jnp.float32
SCALE = 1.0 / math.sqrt(HD)
HALF = HD // 2
LANES = 128
AUG = HD + 16


def nn(a, b):
    return jnp.dot(a, b, preferred_element_type=F32)


def tn(a, b):
    return lax.dot_general(a, b, (((0,), (0,)), ((), ())), preferred_element_type=F32)


def nt(a, b):
    return lax.dot_general(a, b, (((1,), (1,)), ((), ())), preferred_element_type=F32)


def unit_of(values):
    mean = jnp.mean(values, axis=-1, keepdims=True)
    centered = values - mean
    variance = jnp.mean(centered * centered, axis=-1, keepdims=True)
    scale = lax.rsqrt(variance + NORM_EPS)
    return centered * scale, scale


def norm_back(grad, unit, scale, gain):
    u = grad * gain
    mean_u = jnp.mean(u, axis=-1, keepdims=True)
    mean_un = jnp.mean(u * unit, axis=-1, keepdims=True)
    return scale * (u - mean_u - unit * mean_un)


def gelu_both(v):
    cdf = 0.5 * (1.0 + lax.erf(v * (1.0 / math.sqrt(2.0))))
    pdf = jnp.exp(-0.5 * v * v) * (1.0 / math.sqrt(2.0 * math.pi))
    return v * cdf, cdf + v * pdf


def pad_rows(value, rows):
    return jnp.concatenate(
        [value, jnp.zeros((rows - value.shape[0],) + value.shape[1:], value.dtype)]
    )


def first_norm(tokens, vec, normed1):
    unit, _ = unit_of(tokens[...].astype(F32))
    normed = (unit * vec[0:1] + vec[1:2]).astype(BF)
    normed1[...] = pad_rows(normed, normed1.shape[0])


def masks(rows, place, group, feats, keep):
    wide = place.shape[1]
    slot = lax.broadcasted_iota(jnp.int32, (16, wide), 1)
    row = lax.broadcasted_iota(jnp.int32, (16, wide), 0)
    image_id = jnp.zeros((16, wide), jnp.int32)
    for is_large, side, images in ((0, SIDE_SMALL, IMG_SMALL), (1, SIDE_LARGE, IMG_LARGE)):
        mine = sum([(slot >= n * side * side).astype(jnp.int32) for n in range(1, images)], jnp.zeros((16, wide), jnp.int32))
        image_id = jnp.where(group[0] == is_large, mine, image_id)
    same = (image_id == row) & (row < max(IMG_SMALL, IMG_LARGE))
    hidden = jnp.logical_not(same & (place[2:3] > 0.5)) & (row < max(IMG_SMALL, IMG_LARGE))
    feats[0] = jnp.where(same, 1.0, 0.0).astype(BF)
    feats[1] = jnp.where(hidden, HIDE, 0.0).astype(BF)
    feats[2] = jnp.where(row == 0, 1.0, 0.0).astype(BF)
    keep[...] = place[...].T[:rows, 2:3]


def attend_chunk(r, heads, rows, normed1, weights, hook, small, place, feats, q_all, k_all, v_all, lse, att, cosine, sine, proj):
    local = heads * HD
    column = small[r].T[:, 1:2]
    f0 = column[3 * local : 3 * local + heads * HALF]
    f1 = column[3 * local + heads * HALF : 3 * local + 2 * heads * HALF]
    angles = f0 * place[0:1] + f1 * place[1:2]
    cosine[r] = jnp.cos(angles)
    sine[r] = jnp.sin(angles)
    proj[...] = nt(weights[r, : 3 * local], normed1[...]) + column[: 3 * local]
    hook()
    for h in range(heads):
        cos_h = cosine[r, h * HALF : (h + 1) * HALF]
        sin_h = sine[r, h * HALF : (h + 1) * HALF]
        at = r * heads + h
        for base, ref, scale in ((0, q_all, SCALE), (local, k_all, 1.0)):
            a = proj[base + h * HD : base + h * HD + HALF]
            b = proj[base + h * HD + HALF : base + (h + 1) * HD]
            ref[at, :HALF] = ((a * cos_h - b * sin_h) * scale).astype(BF)
            ref[at, HALF:HD] = ((b * cos_h + a * sin_h) * scale).astype(BF)
        v_all[at, :HD] = proj[2 * local + h * HD : 2 * local + (h + 1) * HD].astype(BF)
        q_all[at, HD:] = feats[0]
        k_all[at, HD:] = feats[1]
        v_all[at, HD:] = feats[2]

    def head(h, carry):
        at = r * heads + h
        scores = tn(k_all[at, :, :rows], q_all[at])
        top = jnp.max(scores, axis=0, keepdims=True)
        terms = jnp.exp(scores - top).astype(BF)
        mixed = nn(v_all[at, :, :rows], terms)
        total = mixed[HD : HD + 1]
        att[pl.ds(pl.multiple_of(at * HD, HD), HD)] = (mixed[:HD] * (1.0 / total)).astype(BF)
        lse[at] = jnp.broadcast_to(top + jnp.log(total), lse.shape[1:])
        return carry

    lax.fori_loop(0, heads, head, 0)


def second_norm(rows, tokens, vec, att, wo, middle, normed2):
    branch = tn(att[...], wo)
    middle[...] = tokens[...].astype(F32) + branch[:rows] + vec[4:5]
    unit, _ = unit_of(middle[...])
    normed2[...] = (unit * vec[2:3] + vec[3:4]).astype(BF)


def mlp_chunk(r, normed2, g, wu, wd, small, mlp, gsecond, target, sums, active, slope, hook):
    width = normed2.shape[1]
    hidden = nn(normed2[...], wu[...]) + small[r][0:1]
    act, der = gelu_both(hidden)
    active[...] = act.astype(BF)
    slope[...] = der
    hook(0)
    target[width:] = tn(active[...], g[...]).astype(BF)
    mlp[...] += nn(active[...], wd[...])
    hook(1)
    gh = nt(g[...], wd[...]) * slope[...]
    active[...] = gh.astype(BF)
    sums[r] = jnp.sum(active[...].astype(F32), axis=0, keepdims=True)
    hook(2)
    target[:width] = tn(normed2[...], active[...]).astype(BF)
    gsecond[...] += nt(active[...], wu[...])


def finish_mlp(cot, keep, vec, middle, mlp, gsecond, g, out, branch, sums_vec):
    out[...] = (middle[...] + mlp[...] + vec[5:6]).astype(BF)
    unit, scale = unit_of(middle[...])
    grad = gsecond[...]
    gm = cot[...] * keep[...] + norm_back(grad, unit, scale, vec[2:3])
    low = gm.astype(BF)
    sums_vec[...] = jnp.concatenate(
        [
            jnp.sum(low.astype(F32), axis=0, keepdims=True),
            jnp.sum(grad * unit, axis=0, keepdims=True),
            jnp.sum(grad, axis=0, keepdims=True),
            jnp.sum(g[...].astype(F32), axis=0, keepdims=True),
            jnp.full((4, grad.shape[1]), 1.0, F32) * jnp.sum(keep[...]),
        ]
    )
    middle[...] = gm
    branch[...] = pad_rows(low, branch.shape[0])


def attend_back(at, heads, rows, q_all, k_all, v_all, lse, att, gatt, cosine, sine, place, gqkv, column, sums):
    local = heads * HD
    r, h = at // heads, at % heads
    here = pl.ds(pl.multiple_of(at * HD, HD), HD)
    wide = q_all.shape[2]
    scores = tn(k_all[at, :, :rows], q_all[at])
    probs = jnp.exp(scores - lse[at, 0:1])
    go = gatt[here]
    inner = jnp.sum(go.astype(F32) * att[here].astype(F32), axis=0, keepdims=True)
    gp = tn(v_all[at, :HD, :rows], go)
    gs = (probs * (gp - inner)).astype(BF)
    gv = nt(go, probs.astype(BF))
    gk = nt(q_all[at, :HD], gs)
    gq = nn(k_all[at, :HD, :rows], gs) * SCALE
    hs = pl.ds(pl.multiple_of(h * HALF, HALF), HALF)
    cos_h, sin_h = cosine[r, hs], sine[r, hs]
    term = jnp.zeros((HALF, wide), F32)
    pad = jnp.zeros((HD, wide - rows), F32)
    gk = jnp.concatenate([gk, pad], axis=1)
    gv = jnp.concatenate([gv, pad], axis=1)
    lows = []
    for ref, grad, back in ((q_all, gq, 1.0 / SCALE), (k_all, gk, 1.0)):
        a, b = grad[:HALF], grad[HALF:]
        ra = ref[at, :HALF].astype(F32)
        rb = ref[at, HALF:HD].astype(F32)
        term += (b * ra - a * rb) * back
        lows.append(jnp.concatenate([a * cos_h + b * sin_h, b * cos_h - a * sin_h], axis=0).astype(BF))
    lows.append(gv.astype(BF))
    for n, low in enumerate(lows):
        gqkv[r, pl.ds(pl.multiple_of(n * local + h * HD, HD), HD)] = low
        total = jnp.sum(low.astype(F32), axis=1, keepdims=True)
        column[n * HD : (n + 1) * HD] = jnp.broadcast_to(total, (HD, LANES))
    for n in range(2):
        total = jnp.sum(term * place[n : n + 1], axis=1, keepdims=True)
        column[3 * HD + n * HALF : 3 * HD + (n + 1) * HALF] = jnp.broadcast_to(total, (HALF, LANES))
    sums[pl.ds(at, 1)] = column[...].T[0:1]


UNIT = 128
PIECE = 192
LAGS = (1, 3, 5, 6)
PLAN = (1, 1, 3, 4, 9, 10, 11, 12, 13)
SLOTS = 6
TILE = 16
BITS_MP = (1, 2)


def flip(axis, bit):
    me = lax.axis_index(axis)
    return {axis: me + bit * (1 - 2 * ((me // bit) % 2))}


def bit_of(axis, bit):
    return (lax.axis_index(axis) // bit) % 2


def powers(axis):
    size = lax.axis_size(axis)
    return [1 << k for k in range(size.bit_length() - 1)]


def greet(peers):
    barrier = pltpu.get_barrier_semaphore()
    for peer in peers:
        pl.semaphore_signal(barrier, inc=1, device_id=peer, device_id_type=pl.DeviceIdType.MESH)
    pl.semaphore_wait(barrier, len(peers))


def remote(src, dst, send, recv, peer):
    return pltpu.make_async_remote_copy(
        src_ref=src, dst_ref=dst, send_sem=send, recv_sem=recv, device_id=peer, device_id_type=pl.DeviceIdType.MESH
    )


def steps_of(bits):
    return [UNIT // 2, UNIT // 8] + [UNIT // 8] * (len(bits) - 3)


def quad_peer(bits, step):
    one, two = bit_of("dp", bits[0]), bit_of("dp", bits[1])
    other_one = 1 - one if step & 1 else one
    other_two = 1 - two if step & 2 else two
    me = lax.axis_index("dp")
    return {"dp": me + bits[0] * (other_one - one) + bits[1] * (other_two - two)}, other_one + 2 * other_two


class Gather:
    def __init__(self, shards, full, cuts, send, recv, send_w, recv_w, local):
        self.shards, self.full = shards, full
        self.upper = bit_of("dp", 1)
        self.pieces = []
        for w, cut in enumerate(cuts):
            half = shards[w].shape[0] // 2
            for n in range(cut):
                self.pieces.append((w, half, n * (half // cut), half // cut))
        self.send, self.recv = send, recv
        self.send_w, self.recv_w, self.local = send_w, recv_w, local

    def rows(self, i, upper):
        _, half, start, size = self.pieces[i]
        return pl.ds(pl.multiple_of(upper * half + start, TILE), size)

    def pass_on(self, i, stage, source, target, rows, peer):
        w = self.pieces[i][0]
        full = self.full[w]
        src = self.shards[w].at[rows] if source is None else full.at[source, rows]
        return remote(src, full.at[target, rows], self.send.at[stage, i], self.recv.at[stage, i], peer)

    def across(self, i):
        return self.pass_on(i, 0, None, 2, self.rows(i, self.upper), flip("mp", 2))

    def beside(self, i):
        return self.pass_on(i, 1, 2, 2, self.rows(i, self.upper), flip("dp", 1))

    def near_half(self, i):
        return self.pass_on(i, 2, 2, 3, self.rows(i, self.upper), flip("mp", 1))

    def far_half(self, i):
        return self.pass_on(i, 3, 2, 3, self.rows(i, 1 - self.upper), flip("mp", 1))

    def whole(self, w):
        return remote(self.shards[w], self.full[w].at[1], self.send_w.at[w], self.recv_w.at[w], flip("mp", 1))

    def own(self, w):
        return pltpu.make_async_copy(self.shards[w], self.full[w].at[0], self.local.at[w])

    def got_across(self, i):
        self.across(i).wait()
        self.beside(i).start()
        self.near_half(i).start()
        if i + DEPTH < len(self.pieces):
            self.across(i + DEPTH).start()

    def got_beside(self, i):
        self.beside(i).wait()
        self.far_half(i).start()

    def got_all(self, i):
        self.near_half(i).wait()
        self.far_half(i).wait()


class Gather:
    def __init__(self, weights, send, recv):
        self.weights, self.send, self.recv = weights, send, recv
        self.pieces = weights.shape[1] // PIECE
        self.sub = PIECE // 4
        self.ticks = self.pieces + LAGS[-1]

    def place(self, u):
        one, two = bit_of("dp", 1), bit_of("dp", 2)
        first, second = flip("dp", 1)["dp"], flip("dp", 2)["dp"]
        odd = u % 2
        return (
            one + odd * (two - one),
            two + odd * (one - two),
            {"dp": first + odd * (second - first)},
            {"dp": second + odd * (first - second)},
        )

    def rows(self, u, quarter, count):
        return pl.ds(pl.multiple_of(u * PIECE + quarter * self.sub, TILE), count * self.sub)

    def copy(self, stage, u, source, target, rows, peer):
        return remote(
            self.weights.at[source, rows],
            self.weights.at[target, rows],
            self.send.at[stage, u],
            self.recv.at[stage, u],
            peer,
        )

    def own(self, u):
        return self.copy(0, u, 0, 1, self.rows(u, 0, 4), flip("mp", 1))

    def across(self, u):
        a, b, _, _ = self.place(u)
        return self.copy(1, u, 0, 2, self.rows(u, 2 * b + a, 1), flip("mp", 2))

    def quarter(self, u):
        a, b, peer, _ = self.place(u)
        return self.copy(2, u, 2, 2, self.rows(u, 2 * b + a, 1), peer)

    def half(self, u):
        _, b, _, peer = self.place(u)
        return self.copy(3, u, 2, 2, self.rows(u, 2 * b, 2), peer)

    def pass_on(self, u, n):
        a, b, _, _ = self.place(u)
        rows = (self.rows(u, 2 * b + a, 1), self.rows(u, 2 * b + 1 - a, 1), self.rows(u, 2 * (1 - b), 2))[n]
        return self.copy(4 + n, u, 2, 3, rows, flip("mp", 1))

    def owns(self, start, stop, begin):
        def each(u, carry):
            if begin:
                self.own(u).start()
            else:
                self.own(u).wait()
            return carry

        lax.fori_loop(start, stop, each, 0)

    def tick(self, t):
        def at(lag, body):
            u = t - lag

            @pl.when((u >= 0) & (u < self.pieces))
            def _():
                body(u)

        def begin(u):
            @pl.when(u == 0)
            def _():
                self.across(u).start()

            @pl.when(u + 1 < self.pieces)
            def _():
                self.across(u + 1).start()

        def got_across(u):
            self.across(u).wait()
            self.quarter(u).start()
            self.pass_on(u, 0).start()

        def got_quarter(u):
            self.quarter(u).wait()
            self.half(u).start()
            self.pass_on(u, 1).start()

        def got_half(u):
            self.half(u).wait()
            self.pass_on(u, 2).start()

        def got_all(u):
            for n in range(3):
                self.pass_on(u, n).wait()

        at(0, begin)
        for lag, body in zip(LAGS, (got_across, got_quarter, got_half, got_all)):
            at(lag, body)


class Reducer:
    def __init__(self, grads, got1, got3, got2, got_dp, send, recv):
        self.keep, self.near, self.cross, self.far = (grads.at[n] for n in range(4))
        self.total = self.near
        self.units = grads.shape[1] // UNIT
        self.got1, self.got3, self.got2 = got1, got3, got2
        self.got_half, self.got_quad, self.got_whole = got_dp[0], got_dp[1], got_dp[2:]
        self.send, self.recv = send, recv
        bits = powers("dp")
        self.bits, self.four, self.rest = bits[0], bits[1:3], bits[3:]
        self.half, self.quarter = UNIT // 2, UNIT // 8
        self.base = bit_of("dp", self.bits) * self.half
        self.offset = self.base + quad_peer(self.four, 0)[1] * self.quarter
        self.ticks = self.units + 7 + len(self.rest)

    def rows(self, u, size, offset=0):
        return pl.ds(pl.multiple_of(u * UNIT + offset, TILE), size)

    def slot(self, u, size):
        return pl.ds(pl.multiple_of((u % SLOTS) * size, TILE), size)

    def copy(self, stage, u, source, target, peer):
        return remote(source, target, self.send.at[stage, u], self.recv.at[stage, u], peer)

    def first(self, u):
        at, here, peer = self.rows(u, UNIT), self.slot(u, UNIT), flip("mp", 1)
        return (
            self.copy(0, u, self.near.at[at], self.got1.at[here], peer),
            self.copy(1, u, self.far.at[at], self.got3.at[here], peer),
        )

    def second(self, u):
        return self.copy(2, u, self.cross.at[self.rows(u, UNIT)], self.got2.at[self.slot(u, UNIT)], flip("mp", 2))

    def halve(self, u):
        source = self.keep.at[self.rows(u, self.half, self.half - self.base)]
        return self.copy(3, u, source, self.got_half.at[self.slot(u, self.half)], flip("dp", self.bits))

    def quads(self, u):
        copies = []
        for step in range(1, 4):
            peer, place = quad_peer(self.four, step)
            source = self.keep.at[self.rows(u, self.quarter, self.base + place * self.quarter)]
            target = self.got_quad.at[step - 1, self.slot(u, self.quarter)]
            copies.append(self.copy(3 + step, u, source, target, peer))
        return copies

    def whole(self, u, k):
        source = self.keep.at[self.rows(u, self.quarter, self.offset)]
        return self.copy(7 + k, u, source, self.got_whole[k].at[self.slot(u, self.quarter)], flip("dp", self.rest[k]))

    def quads_back(self, u):
        part = self.total.at[self.rows(u, self.quarter, self.offset)]
        first = 6 + len(self.rest)
        return [self.copy(first + step, u, part, part, quad_peer(self.four, step)[0]) for step in range(1, 4)]

    def half_back(self, u):
        part = self.total.at[self.rows(u, self.half, self.base)]
        return self.copy(10 + len(self.rest), u, part, part, flip("dp", self.bits))

    def add(self, source, target, u, size, offset, terms):
        def tile(i, carry):
            at = pl.ds(pl.multiple_of(u * UNIT + offset + i * TILE, TILE), TILE)
            value = source[at].astype(F32)
            for ref in terms:
                value += ref[pl.ds(pl.multiple_of((u % SLOTS) * size + i * TILE, TILE), TILE)].astype(F32)
            target[at] = value.astype(BF)
            return carry

        lax.fori_loop(0, size // TILE, tile, 0)

    def tick(self, t):
        rest = len(self.rest)

        def at(lag, body):
            u = t - lag

            @pl.when((u >= 0) & (u < self.units))
            def _():
                body(u)

        def each(copies, begin):
            for copy in copies:
                if begin:
                    copy.start()
                else:
                    copy.wait()

        def start_first(u):
            each(self.first(u), True)

        def after_first(u):
            each(self.first(u), False)
            self.add(self.cross, self.cross, u, UNIT, 0, [self.got3])
            self.second(u).start()

        def after_second(u):
            self.second(u).wait()
            self.add(self.keep, self.keep, u, UNIT, 0, [self.got1, self.got2])
            self.halve(u).start()

        def after_half(u):
            self.halve(u).wait()
            self.add(self.keep, self.keep, u, self.half, self.base, [self.got_half])
            each(self.quads(u), True)

        def after_quads(u):
            each(self.quads(u), False)
            terms = [self.got_quad.at[n] for n in range(3)]
            self.add(self.keep, self.keep if rest else self.total, u, self.quarter, self.offset, terms)
            each([self.whole(u, 0)] if rest else self.quads_back(u), True)

        def after_whole(k):
            def body(u):
                self.whole(u, k).wait()
                last = k == rest - 1
                target = self.total if last else self.keep
                self.add(self.keep, target, u, self.quarter, self.offset, [self.got_whole[k]])
                each(self.quads_back(u) if last else [self.whole(u, k + 1)], True)

            return body

        def after_quads_back(u):
            each(self.quads_back(u), False)
            self.half_back(u).start()

        def after_half_back(u):
            self.half_back(u).wait()

        at(0, start_first)
        at(1, after_first)
        at(3, after_second)
        at(4, after_half)
        at(5, after_quads)
        for k in range(rest):
            at(6 + k, after_whole(k))
        at(6 + rest, after_quads_back)
        at(7 + rest, after_half_back)


class SmallSum:
    def __init__(self, value, got, send, recv):
        self.value, self.got, self.send, self.recv = value, got, send, recv
        self.peers = [flip("mp", b) for b in BITS_MP] + [flip("dp", b) for b in powers("dp")]

    def copy(self, k):
        return remote(self.value, self.got.at[k], self.send.at[k], self.recv.at[k], self.peers[k])

    def finish(self, k):
        self.copy(k).wait()
        value, got = self.value, self.got
        value[:8] += got[k, :8]
        if k == 0:
            value[8:10] += got[k, 10:12]
            value[12:14] += got[k, 14:16]
        elif k == 1:
            value[8:10] += got[k, 12:14]
        else:
            value[8:10] += got[k, 8:10]


def layer_body(
    heads,
    rows,
    tokens_in,
    gain1_in,
    bias1_in,
    gain2_in,
    bias2_in,
    bias_out_in,
    bias_down_in,
    positions_in,
    keep_mask_in,
    bias_qkv_in,
    freqs_in,
    bias_up_in,
    group,
    cot,
    s_qkv,
    s_out,
    s_up,
    s_down,
    out,
    gx,
    o_up,
    o_down,
    o_out,
    o_qkv,
    small_sum,
    factor_out,
    tokens,
    gain1,
    bias1,
    gain2,
    bias2,
    bias_out,
    bias_down,
    positions,
    keep_mask,
    bias_qkv,
    freqs,
    bias_up,
    all_w,
    small,
    place,
    q_all,
    k_all,
    v_all,
    lse,
    att,
    cosine,
    sine,
    normed1,
    middle,
    branch,
    g,
    mlp,
    gsecond,
    active,
    slope,
    vec,
    keep_col,
    feats,
    sums_up,
    sums_vec,
    column,
    head_sums,
    grads,
    got1,
    got3,
    got2,
    got_small,
    send_g,
    recv_g,
    send_s,
    recv_s,
    local_sem,
    send,
    recv,
    send_v,
    recv_v,
    *got_dp,
):
    parts, count = all_w.shape[0], q_all.shape[0]
    local = heads * HD
    width = tokens.shape[1]
    wide = q_all.shape[2]
    top = 4 * local
    units = (all_w.shape[1] - top) // 2
    mlp_rows = 2 * width
    up_rows, down_rows = pl.ds(top, width), pl.ds(top + width, units)
    loads, start = [], 0
    for n, ref in enumerate((s_qkv, s_out, s_up, s_down)):
        loads.append(pltpu.make_async_copy(ref, all_w.at[0, pl.ds(start, ref.shape[0])], local_sem.at[n]))
        start += ref.shape[0]
    load_cot = pltpu.make_async_copy(cot, slope, local_sem.at[5])
    early = []
    for n, (source, target) in enumerate(
        (
            (bias_up_in, bias_up),
            (bias_qkv_in, bias_qkv),
            (freqs_in, freqs),
            (tokens_in, tokens),
            (gain1_in, gain1),
            (bias1_in, bias1),
            (gain2_in, gain2),
            (bias2_in, bias2),
            (bias_out_in, bias_out),
            (bias_down_in, bias_down),
            (positions_in, positions),
            (keep_mask_in, keep_mask),
        )
    ):
        early.append(pltpu.make_async_copy(source, target, local_sem.at[12 + n]))
    for load in early[:3] + loads + early[3:]:
        load.start()
    for load in early[:3]:
        load.wait()
    small[0] = jnp.zeros_like(small[0])
    small[0, 0:1] = bias_up[...].reshape(1, units).astype(F32)
    row = [bias_qkv[n : n + 1] for n in range(3)] + [freqs[h, n : n + 1] for n in range(2) for h in range(heads)]
    small[0, 1:2] = jnp.concatenate(row, axis=1)
    both = {"mp": lax.axis_index("mp") + 1 * (1 - 2 * bit_of("mp", 1)) + 2 * (1 - 2 * bit_of("mp", 2))}
    sums = SmallSum(small_sum, got_small, send_v, recv_v)
    greet(sums.peers + [both])
    peers = [flip("mp", 1), flip("mp", 2), both]
    smalls = [
        remote(small.at[0], small.at[r], send_s.at[r - 1], recv_s.at[r - 1], peers[r - 1]) for r in range(1, 4)
    ]
    for copy in smalls:
        copy.start()
    weights = Gather(all_w, send_g, recv_g)
    for load in loads + early[3:]:
        load.wait()
    weights.tick(0)
    weights.owns(0, weights.pieces, True)
    load_cot.start()
    for n, ref in enumerate((gain1, bias1, gain2, bias2, bias_out, bias_down)):
        vec[n : n + 1] = ref[...].reshape(1, width)
    first_norm(tokens, vec, normed1)
    own_part = lax.axis_index("mp")
    spot = jnp.concatenate([positions[...], keep_mask[...].reshape(1, keep_mask.shape[0])])
    mine = spot[:, :rows]
    for n in range(1, parts):
        mine = jnp.where(own_part == n, spot[:, n * rows : (n + 1) * rows], mine)
    place[...] = jnp.zeros_like(place)
    place[0:3, :rows] = mine.astype(F32)
    masks(rows, place, group, feats, keep_col)
    for copy in smalls:
        copy.wait()
    proj = mlp.at[: 3 * local, :wide]

    def gather_step(t, carry):
        weights.tick(t)
        return carry

    reached = [1]

    def gather_to(n):
        if PLAN[n] > reached[0]:
            lax.fori_loop(reached[0], PLAN[n], gather_step, 0)
            reached[0] = PLAN[n]

    first_rows = 3 * local // PIECE
    for r in range(parts):
        gather_to(2 * r)
        if r == 1:
            weights.owns(0, first_rows, False)
        attend_chunk(
            r, heads, rows, normed1, all_w, functools.partial(gather_to, 2 * r + 1), small, place, feats,
            q_all, k_all, v_all, lse, att, cosine, sine, proj,
        )
    weights.owns(first_rows, weights.pieces, False)
    load_cot.wait()
    g[...] = (slope[...] * keep_col[...]).astype(BF)
    gather_to(2 * parts)
    done = reached[0]
    wo = jnp.concatenate([all_w[r, 3 * local : top] for r in range(parts)])
    normed2 = branch.at[:rows]
    second_norm(rows, tokens, vec, att, wo, middle, normed2)
    mlp[...] = jnp.zeros_like(mlp)
    gsecond[...] = jnp.zeros_like(gsecond)

    def mlp_step(r, carry):
        mlp_chunk(
            r, normed2, g, all_w.at[r, up_rows], all_w.at[r, down_rows], small, mlp, gsecond,
            grads.at[r, pl.ds(0, mlp_rows)], sums_up, active, slope, lambda n: weights.tick(done + 3 * r + n),
        )
        return carry

    assert done + 6 >= weights.ticks
    lax.fori_loop(0, parts, mlp_step, 0)
    load_cot.start()
    net = Reducer(grads, got1, got3, got2, got_dp, send, recv)

    def step(t, carry):
        net.tick(t)
        return carry

    def ticks(start, stop):
        lax.fori_loop(start, stop, step, 0)

    ticks(0, 1)
    load_cot.wait()
    finish_mlp(slope, keep_col, vec, middle, mlp, gsecond, g, active, branch, sums_vec)
    store_out = pltpu.make_async_copy(active, out, local_sem.at[6])
    store_out.start()
    ticks(1, 2)
    gatt = all_w.at[0, down_rows, :wide]
    gqkv = all_w.at[:, pl.ds(top, 3 * local), :wide]
    wo = jnp.concatenate([all_w[r, 3 * local : top] for r in range(parts)])
    gatt[...] = nt(wo, branch[...]).astype(BF)

    def some_heads(i, carry):
        net.tick(2 + i)

        def head(n, c):
            attend_back(2 * i + n, heads, rows, q_all, k_all, v_all, lse, att, gatt, cosine, sine, place, gqkv, column, head_sums)
            return c

        return lax.fori_loop(0, 2, head, carry)

    lax.fori_loop(0, count // 2, some_heads, 0)
    base = 2 + count // 2
    gsecond[...] = jnp.zeros_like(gsecond)

    def late(r, carry):
        net.tick(base + r)
        here = att[pl.ds(pl.multiple_of(r * local, HD), local)]
        grads[r, mlp_rows : mlp_rows + local] = nn(here, branch[...]).astype(BF)
        grads[r, mlp_rows + local :] = nn(gqkv[r], normed1[...]).astype(BF)
        gsecond[...] += tn(gqkv[r], all_w[r, : 3 * local])[:rows]
        return carry

    lax.fori_loop(0, parts, late, 0)
    base = base + parts
    ticks(base, base + 1)
    grad = gsecond[...]
    unit, scale = unit_of(tokens[...].astype(F32))
    gsecond[...] = middle[...] + norm_back(grad, unit, scale, vec[0:1])
    store_gx = pltpu.make_async_copy(gsecond, gx, local_sem.at[7])
    store_gx.start()
    small_sum[...] = jnp.zeros_like(small_sum)
    small_sum[0:1] = jnp.sum(grad * unit, axis=0, keepdims=True)
    small_sum[1:2] = jnp.sum(grad, axis=0, keepdims=True)
    small_sum[2:7] = sums_vec[0:5]
    for r in range(parts):
        small_sum[8 + 2 * r : 9 + 2 * r] = sums_up[r]
        mine = [head_sums[r * heads + h : r * heads + h + 1] for h in range(heads)]
        pieces = [v[:, n * HD : (n + 1) * HD] for n in range(3) for v in mine]
        pieces += [v[:, 3 * HD + n * HALF : 3 * HD + (n + 1) * HALF] for n in range(2) for v in mine]
        small_sum[9 + 2 * r : 10 + 2 * r] = jnp.concatenate(pieces, axis=1)
    base = base + 1
    exchanges = len(sums.peers)

    def step_small(t, carry):
        net.tick(t)
        for k in range(exchanges + 1):
            @pl.when(t == base + k)
            def _():
                if k > 0:
                    sums.finish(k - 1)
                if k == exchanges:
                    factor = lax.axis_size("dp") / small_sum[6:7]
                    factor_out[0] = factor[0, 0]
                    small_sum[...] *= factor
                if k < exchanges:
                    sums.copy(k).start()
        return carry

    lax.fori_loop(base, base + exchanges + 1, step_small, 0)
    ticks(base + exchanges + 1, max(net.ticks, base + exchanges + 1))
    stores = []
    start = 0
    for n, ref in enumerate((o_up, o_down, o_out, o_qkv)):
        stores.append(pltpu.make_async_copy(grads.at[1, pl.ds(start, ref.shape[0])], ref, local_sem.at[8 + n]))
        stores[-1].start()
        start += ref.shape[0]
    for copy in stores + [store_out, store_gx]:
        copy.wait()


def finish_body(vectors, local, up, down, out, qkv, small, factor, middle, gx, *rest):
    results, (held, held_gx, copies) = rest[:-3], rest[-3:]
    loads = [pltpu.make_async_copy(middle, held, copies.at[0]), pltpu.make_async_copy(gx, held_gx, copies.at[1])]
    moves = [pltpu.make_async_copy(held, results[-2], copies.at[2]), pltpu.make_async_copy(held_gx, results[-1], copies.at[3])]

    @pl.when(pl.program_id(0) == 0)
    def _():
        for load in loads:
            load.start()
        for n, row in enumerate(vectors):
            results[4 + n][...] = small[row : row + 1].reshape(small.shape[1])
        b_qkv, freqs = results[4 + len(vectors)], results[5 + len(vectors)]
        for n in range(3):
            b_qkv[n : n + 1] = small[9:10, n * local : (n + 1) * local]
        for n in range(2):
            for h in range(freqs.shape[0]):
                start = 3 * local + (n * freqs.shape[0] + h) * HALF
                freqs[h, n : n + 1] = small[9:10, start : start + HALF]

    for source, target in zip((up, down, out, qkv), results):
        target[...] = source[...].astype(F32) * factor[0]

    @pl.when(pl.program_id(0) == 2)
    def _():
        for load in loads:
            load.wait()
        for move in moves:
            move.start()

    @pl.when(pl.program_id(0) == pl.num_programs(0) - 1)
    def _():
        for move in moves:
            move.wait()


def sds(shape, dtype):
    return jax.ShapeDtypeStruct(shape, dtype)


def body(
    tokens,
    image_group,
    positions,
    keep_mask,
    norm1_gain,
    norm1_bias,
    w_qkv,
    b_qkv,
    rotary_freqs,
    w_out,
    b_out,
    norm2_gain,
    norm2_bias,
    w_up,
    b_up,
    w_down,
    b_down,
    cotangent,
):
    rows, width = tokens.shape
    wide = -(-rows // LANES) * LANES
    parts = lax.axis_size("mp")
    mp_index = lax.axis_index("mp")
    heads = rotary_freqs.shape[1]
    local = heads * HD
    units = w_up.shape[1]
    w_qkv_t = w_qkv.reshape(width, 3 * local).T
    count = parts * heads
    bits = powers("dp")
    sizes = steps_of(bits)
    stages = 8 + len(bits)
    total_rows = 2 * width + 4 * local
    unit_count = total_rows // UNIT
    pieces = total_rows // PIECE
    swaps = 2 + len(bits)
    in_vmem = pl.BlockSpec(memory_space=pltpu.VMEM)
    in_smem = pl.BlockSpec(memory_space=pltpu.SMEM)
    anywhere = pl.BlockSpec(memory_space=pl.ANY)
    dma = pltpu.SemaphoreType.DMA
    vmem = pltpu.VMEM
    out, gx, o_up, o_down, o_out, o_qkv, small_sum, factor = pl.pallas_call(
        functools.partial(layer_body, heads, rows),
        out_shape=[
            sds((rows, width), BF),
            sds((rows, width), F32),
            sds((width, units), BF),
            sds((units, width), BF),
            sds((local, width), BF),
            sds((3 * local, width), BF),
            sds((16, width), F32),
            sds((1,), F32),
        ],
        in_specs=[anywhere] * 12 + [in_smem] + [anywhere] * 5,
        out_specs=[anywhere] * 6 + [in_vmem, in_smem],
        scratch_shapes=[
            vmem(tokens.shape, BF),
        ]
        + [vmem((width,), F32)] * 6
        + [
            vmem(positions.shape, jnp.int32),
            vmem(keep_mask.shape, jnp.int32),
            vmem(b_qkv.shape, F32),
            vmem((heads, 2, HALF), F32),
            vmem(b_up.shape, BF),
            vmem((parts, total_rows, width), BF),
            vmem((parts, 8, width), F32),
            vmem((8, wide), F32),
            vmem((count, AUG, wide), BF),
            vmem((count, AUG, wide), BF),
            vmem((count, AUG, wide), BF),
            vmem((count, 8, wide), F32),
            vmem((count * HD, wide), BF),
            vmem((parts, heads * HALF, wide), F32),
            vmem((parts, heads * HALF, wide), F32),
            vmem((wide, width), BF),
            vmem((rows, width), F32),
            vmem((wide, width), BF),
            vmem((rows, width), BF),
            vmem((rows, width), F32),
            vmem((rows, width), F32),
            vmem((rows, units), BF),
            vmem((rows, units), F32),
            vmem((8, width), F32),
            vmem((rows, 1), F32),
            vmem((3, 16, wide), BF),
            vmem((parts, 1, units), F32),
            vmem((8, width), F32),
            vmem((3 * HD + 2 * HALF, LANES), F32),
            vmem((-(-count // 8) * 8, 3 * HD + 2 * HALF), F32),
            vmem((parts, total_rows, width), BF),
            vmem((SLOTS * UNIT, width), BF),
            vmem((SLOTS * UNIT, width), BF),
            vmem((SLOTS * UNIT, width), BF),
            vmem((swaps, 16, width), F32),
            dma((7, pieces)),
            dma((7, pieces)),
            dma((3,)),
            dma((3,)),
            dma((24,)),
            dma((stages, unit_count)),
            dma((stages, unit_count)),
            dma((swaps,)),
            dma((swaps,)),
        ]
        + [vmem((SLOTS * UNIT // 2, width), BF), vmem((3, SLOTS * UNIT // 8, width), BF)]
        + [vmem((SLOTS * size, width), BF) for size in sizes[2:]],
        compiler_params=pltpu.CompilerParams(vmem_limit_bytes=61 << 20, collective_id=0, has_side_effects=True),
    )(tokens, norm1_gain, norm1_bias, norm2_gain, norm2_bias, b_out, b_down, positions, keep_mask, b_qkv,
      rotary_freqs.transpose(1, 0, 2), b_up, image_group, cotangent, w_qkv_t, w_out, w_up, w_down)
    steps = 6

    def piece(ref):
        return pl.BlockSpec((ref.shape[0] // steps, width), lambda i: (i, 0))

    sums = (o_up, o_down, o_out, o_qkv)
    vectors = [0, 1, 2, 3, 4, 5, 8]
    finished = pl.pallas_call(
        functools.partial(finish_body, vectors, local),
        grid=(steps,),
        out_shape=[sds(ref.shape, F32) for ref in sums]
        + [sds((width,), F32)] * len(vectors)
        + [sds((3, local), F32), sds((heads, 2, HALF), F32), sds(out.shape, BF), sds(gx.shape, F32)],
        in_specs=[piece(ref) for ref in sums] + [in_vmem, in_smem, anywhere, anywhere],
        out_specs=[piece(ref) for ref in sums] + [in_vmem] * (len(vectors) + 2) + [anywhere] * 2,
        scratch_shapes=[vmem(out.shape, BF), vmem(gx.shape, F32), dma((4,))],
        compiler_params=pltpu.CompilerParams(vmem_limit_bytes=60 << 20),
    )(*sums, small_sum, factor, out, gx)
    sum_w_up, sum_w_down, sum_w_out, sum_w_qkv, gain1, bias1, b_out_sum, gain2, bias2, b_down_sum, b_up_sum = finished[:11]
    b_qkv_sum, freqs_sum, out, gx = finished[11:]
    return (
        out,
        gx,
        gain1,
        bias1,
        sum_w_qkv.T.reshape(w_qkv.shape),
        b_qkv_sum,
        freqs_sum.transpose(1, 0, 2),
        sum_w_out,
        b_out_sum,
        gain2,
        bias2,
        sum_w_up,
        b_up_sum,
        sum_w_down,
        b_down_sum,
    )


def solution(mesh):
    placed = (
        P(("dp", "mp"), None),
        P("dp"),
        P(None, "dp"),
        P("dp"),
        P(),
        P(),
        P(None, None, "mp"),
        P(None, "mp"),
        P(None, "mp", None),
        P("mp", None),
        P(),
        P(),
        P(),
        P(None, "mp"),
        P("mp"),
        P("mp", None),
        P(),
        P(("dp", "mp"), None),
    )
    return jax.shard_map(
        body,
        mesh=mesh,
        in_specs=placed,
        out_specs=(
            P(("dp", "mp"), None),
            P(("dp", "mp"), None),
            P(),
            P(),
            P(None, None, "mp"),
            P(None, "mp"),
            P(None, "mp", None),
            P("mp", None),
            P(),
            P(),
            P(),
            P(None, "mp"),
            P("mp"),
            P("mp", None),
            P(),
        ),
        check_vma=False,
    )
```

```python
import math
import functools

import jax
import jax.numpy as jnp
from jax import lax
from jax.experimental import pallas as pl
from jax.experimental.pallas import tpu as pltpu
from jax.sharding import PartitionSpec as P

HD = 64
SIDE_SMALL = 14
SIDE_LARGE = 24
IMG_SMALL = 3
IMG_LARGE = 1
NORM_EPS = 1e-06
HIDE = -1e30
BF = jnp.bfloat16
F32 = jnp.float32
SCALE = 1.0 / math.sqrt(HD)
HALF = HD // 2
LANES = 128
AUG = HD + 16


def nn(a, b):
    return jnp.dot(a, b, preferred_element_type=F32)


def tn(a, b):
    return lax.dot_general(a, b, (((0,), (0,)), ((), ())), preferred_element_type=F32)


def nt(a, b):
    return lax.dot_general(a, b, (((1,), (1,)), ((), ())), preferred_element_type=F32)


def unit_of(values):
    mean = jnp.mean(values, axis=-1, keepdims=True)
    centered = values - mean
    variance = jnp.mean(centered * centered, axis=-1, keepdims=True)
    scale = lax.rsqrt(variance + NORM_EPS)
    return centered * scale, scale


def norm_back(grad, unit, scale, gain):
    u = grad * gain
    mean_u = jnp.mean(u, axis=-1, keepdims=True)
    mean_un = jnp.mean(u * unit, axis=-1, keepdims=True)
    return scale * (u - mean_u - unit * mean_un)


def gelu_both(v):
    cdf = 0.5 * (1.0 + lax.erf(v * (1.0 / math.sqrt(2.0))))
    pdf = jnp.exp(-0.5 * v * v) * (1.0 / math.sqrt(2.0 * math.pi))
    return v * cdf, cdf + v * pdf


def pad_rows(value, rows):
    return jnp.concatenate(
        [value, jnp.zeros((rows - value.shape[0],) + value.shape[1:], value.dtype)]
    )


def first_norm(tokens, vec, normed1):
    unit, _ = unit_of(tokens[...].astype(F32))
    normed = (unit * vec[0:1] + vec[1:2]).astype(BF)
    normed1[...] = pad_rows(normed, normed1.shape[0])


def masks(rows, place, group, feats, keep):
    wide = place.shape[1]
    slot = lax.broadcasted_iota(jnp.int32, (16, wide), 1)
    row = lax.broadcasted_iota(jnp.int32, (16, wide), 0)
    image_id = jnp.zeros((16, wide), jnp.int32)
    for is_large, side, images in ((0, SIDE_SMALL, IMG_SMALL), (1, SIDE_LARGE, IMG_LARGE)):
        mine = sum([(slot >= n * side * side).astype(jnp.int32) for n in range(1, images)], jnp.zeros((16, wide), jnp.int32))
        image_id = jnp.where(group[0] == is_large, mine, image_id)
    same = (image_id == row) & (row < max(IMG_SMALL, IMG_LARGE))
    hidden = jnp.logical_not(same & (place[2:3] > 0.5)) & (row < max(IMG_SMALL, IMG_LARGE))
    feats[0] = jnp.where(same, 1.0, 0.0).astype(BF)
    feats[1] = jnp.where(hidden, HIDE, 0.0).astype(BF)
    feats[2] = jnp.where(row == 0, 1.0, 0.0).astype(BF)
    keep[...] = place[...].T[:rows, 2:3]


def attend_chunk(r, heads, rows, normed1, weights, hook, small, place, feats, q_all, k_all, v_all, lse, att, cosine, sine, proj):
    local = heads * HD
    column = small[r].T[:, 1:2]
    f0 = column[3 * local : 3 * local + heads * HALF]
    f1 = column[3 * local + heads * HALF : 3 * local + 2 * heads * HALF]
    angles = f0 * place[0:1] + f1 * place[1:2]
    cosine[r] = jnp.cos(angles)
    sine[r] = jnp.sin(angles)
    proj[...] = nt(weights[r, : 3 * local], normed1[...]) + column[: 3 * local]
    hook(1)
    for h in range(heads):
        cos_h = cosine[r, h * HALF : (h + 1) * HALF]
        sin_h = sine[r, h * HALF : (h + 1) * HALF]
        at = r * heads + h
        for base, ref, scale in ((0, q_all, SCALE), (local, k_all, 1.0)):
            a = proj[base + h * HD : base + h * HD + HALF]
            b = proj[base + h * HD + HALF : base + (h + 1) * HD]
            ref[at, :HALF] = ((a * cos_h - b * sin_h) * scale).astype(BF)
            ref[at, HALF:HD] = ((b * cos_h + a * sin_h) * scale).astype(BF)
        v_all[at, :HD] = proj[2 * local + h * HD : 2 * local + (h + 1) * HD].astype(BF)
        q_all[at, HD:] = feats[0]
        k_all[at, HD:] = feats[1]
        v_all[at, HD:] = feats[2]

    def head(h, carry):
        at = r * heads + h
        scores = tn(k_all[at, :, :rows], q_all[at])
        top = jnp.max(scores, axis=0, keepdims=True)
        terms = jnp.exp(scores - top).astype(BF)
        mixed = nn(v_all[at, :, :rows], terms)
        total = mixed[HD : HD + 1]
        att[pl.ds(pl.multiple_of(at * HD, HD), HD)] = (mixed[:HD] * (1.0 / total)).astype(BF)
        lse[at] = jnp.broadcast_to(top + jnp.log(total), lse.shape[1:])
        for n in range(heads - 1):
            pl.when(h == n)(functools.partial(hook, 2 + n))
        return carry

    lax.fori_loop(0, heads, head, 0)


def second_norm(rows, tokens, vec, att, wo, middle, normed2):
    branch = tn(att[...], wo)
    middle[...] = tokens[...].astype(F32) + branch[:rows] + vec[4:5]
    unit, _ = unit_of(middle[...])
    normed2[...] = (unit * vec[2:3] + vec[3:4]).astype(BF)


def mlp_chunk(r, normed2, g, wu, wd, small, mlp, gsecond, target, sums, active, slope, hook):
    width = normed2.shape[1]
    hook(-1)
    hidden = nn(normed2[...], wu[...]) + small[r][0:1]
    act, der = gelu_both(hidden)
    active[...] = act.astype(BF)
    slope[...] = der
    hook(0)
    target[: active.shape[1]] = tn(active[...], g[...]).astype(BF)
    hook(1)
    mlp[...] += nn(active[...], wd[...])
    gh = nt(g[...], wd[...]) * slope[...]
    active[...] = gh.astype(BF)
    sums[r] = jnp.sum(active[...].astype(F32), axis=0, keepdims=True)
    hook(2)
    target[active.shape[1] :] = tn(normed2[...], active[...]).astype(BF)
    hook(3)
    gsecond[...] += nt(active[...], wu[...])


def finish_mlp(cot, keep, vec, middle, mlp, gsecond, g, out, branch, sums_vec):
    out[...] = (middle[...] + mlp[...] + vec[5:6]).astype(BF)
    unit, scale = unit_of(middle[...])
    grad = gsecond[...]
    gm = cot[...] * keep[...] + norm_back(grad, unit, scale, vec[2:3])
    low = gm.astype(BF)
    sums_vec[...] = jnp.concatenate(
        [
            jnp.sum(low.astype(F32), axis=0, keepdims=True),
            jnp.sum(grad * unit, axis=0, keepdims=True),
            jnp.sum(grad, axis=0, keepdims=True),
            jnp.sum(g[...].astype(F32), axis=0, keepdims=True),
            jnp.full((4, grad.shape[1]), 1.0, F32) * jnp.sum(keep[...]),
        ]
    )
    middle[...] = gm
    branch[...] = pad_rows(low, branch.shape[0])


def attend_back(at, heads, rows, q_all, k_all, v_all, lse, att, gatt, cosine, sine, place, gqkv, column, sums):
    local = heads * HD
    r, h = at // heads, at % heads
    here = pl.ds(pl.multiple_of(at * HD, HD), HD)
    wide = q_all.shape[2]
    scores = tn(k_all[at, :, :rows], q_all[at])
    probs = jnp.exp(scores - lse[at, 0:1])
    go = gatt[here]
    inner = jnp.sum(go.astype(F32) * att[here].astype(F32), axis=0, keepdims=True)
    gp = tn(v_all[at, :HD, :rows], go)
    gs = (probs * (gp - inner)).astype(BF)
    gv = nt(go, probs.astype(BF))
    gk = nt(q_all[at, :HD], gs)
    gq = nn(k_all[at, :HD, :rows], gs) * SCALE
    hs = pl.ds(pl.multiple_of(h * HALF, HALF), HALF)
    cos_h, sin_h = cosine[r, hs], sine[r, hs]
    term = jnp.zeros((HALF, wide), F32)
    pad = jnp.zeros((HD, wide - rows), F32)
    gk = jnp.concatenate([gk, pad], axis=1)
    gv = jnp.concatenate([gv, pad], axis=1)
    lows = []
    for ref, grad, back in ((q_all, gq, 1.0 / SCALE), (k_all, gk, 1.0)):
        a, b = grad[:HALF], grad[HALF:]
        ra = ref[at, :HALF].astype(F32)
        rb = ref[at, HALF:HD].astype(F32)
        term += (b * ra - a * rb) * back
        lows.append(jnp.concatenate([a * cos_h + b * sin_h, b * cos_h - a * sin_h], axis=0).astype(BF))
    lows.append(gv.astype(BF))
    for n, low in enumerate(lows):
        gqkv[r, pl.ds(pl.multiple_of(n * local + h * HD, HD), HD)] = low
        total = jnp.sum(low.astype(F32), axis=1, keepdims=True)
        column[n * HD : (n + 1) * HD] = jnp.broadcast_to(total, (HD, LANES))
    for n in range(2):
        total = jnp.sum(term * place[n : n + 1], axis=1, keepdims=True)
        column[3 * HD + n * HALF : 3 * HD + (n + 1) * HALF] = jnp.broadcast_to(total, (HALF, LANES))
    sums[pl.ds(at, 1)] = column[...].T[0:1]


UNIT = 128
PIECE = 192
DEPTH = 3
PLAN = {
    ('p', 0, 2): (('a', 0),),
    ('p', 1, 1): (('a', 1),),
    ('p', 1, 3): (('a', 2), ('b', 0)),
    ('p', 2, 0): (('d', 0), ('a', 3), ('b', 1), ('d', 1), ('a', 4), ('b', 2)),
    ('p', 2, 1): (('d', 2),),
    ('p', 2, 2): (('b', 3), ('a', 5)),
    ('p', 2, 3): (('d', 3),),
    ('p', 3, 1): (('b', 4), ('a', 6)),
    ('p', 3, 2): (('d', 4),),
    ('p', 3, 3): (('a', 7), ('b', 5)),
    ('w', 0, 0): (('d', 5),),
    ('f', 0, 0): (('a', 8), ('b', 6)),
    ('f', 0, 1): (('d', 6), ('a', 9), ('b', 7)),
    ('f', 0, 2): (('d', 7),),
    ('f', 0, 3): (('a', 10),),
    ('f', 0, 4): (('b', 8),),
    ('f', 1, 0): (('d', 8), ('a', 11)),
    ('f', 1, 1): (('b', 9),),
    ('f', 1, 2): (('d', 9),),
    ('f', 1, 3): (('b', 10),),
    ('f', 1, 4): (('d', 10), ('b', 11)),
    ('f', 2, 0): (('d', 11),),
}
SLOTS = 6
TILE = 16
BITS_MP = (1, 2)


def flip(axis, bit):
    me = lax.axis_index(axis)
    return {axis: me + bit * (1 - 2 * ((me // bit) % 2))}


def bit_of(axis, bit):
    return (lax.axis_index(axis) // bit) % 2


def powers(axis):
    size = lax.axis_size(axis)
    return [1 << k for k in range(size.bit_length() - 1)]


def greet(peers):
    barrier = pltpu.get_barrier_semaphore()
    for peer in peers:
        pl.semaphore_signal(barrier, inc=1, device_id=peer, device_id_type=pl.DeviceIdType.MESH)
    pl.semaphore_wait(barrier, len(peers))


def remote(src, dst, send, recv, peer):
    return pltpu.make_async_remote_copy(
        src_ref=src, dst_ref=dst, send_sem=send, recv_sem=recv, device_id=peer, device_id_type=pl.DeviceIdType.MESH
    )


def steps_of(bits):
    return [UNIT // 2, UNIT // 8] + [UNIT // 8] * (len(bits) - 3)


def quad_peer(bits, step):
    one, two = bit_of("dp", bits[0]), bit_of("dp", bits[1])
    other_one = 1 - one if step & 1 else one
    other_two = 1 - two if step & 2 else two
    me = lax.axis_index("dp")
    return {"dp": me + bits[0] * (other_one - one) + bits[1] * (other_two - two)}, other_one + 2 * other_two


class Gather:
    def __init__(self, weights, send, recv):
        self.weights, self.send, self.recv = weights, send, recv
        self.pieces = weights.shape[1] // PIECE

    def rows(self, u, mine):
        half = PIECE // 2
        upper = bit_of("dp", 1 + u % 2)
        return pl.ds(pl.multiple_of(u * PIECE + (upper if mine else 1 - upper) * half, TILE), half)

    def copy(self, stage, u, source, target, rows, peer):
        return remote(
            self.weights.at[source, rows],
            self.weights.at[target, rows],
            self.send.at[stage, u],
            self.recv.at[stage, u],
            peer,
        )

    def own(self, u):
        return self.copy(0, u, 0, 1, pl.ds(pl.multiple_of(u * PIECE, TILE), PIECE), flip("mp", 1))

    def across(self, u):
        return self.copy(1, u, 0, 2, self.rows(u, True), flip("mp", 2))

    def beside(self, u):
        return self.copy(2, u, 2, 2, self.rows(u, True), flip("dp", 1 + u % 2))

    def pass_on(self, u, n):
        return self.copy(3 + n, u, 2, 3, self.rows(u, n == 0), flip("mp", 1))

    def owns(self, start, stop, begin):
        def each(u, carry):
            if begin:
                self.own(u).start()
            else:
                self.own(u).wait()
            return carry

        lax.fori_loop(start, stop, each, 0)

    def step(self, kind, u):
        if kind == "a":
            self.across(u).wait()
            if u + DEPTH < self.pieces:
                self.across(u + DEPTH).start()
            self.beside(u).start()
            self.pass_on(u, 0).start()
        elif kind == "b":
            self.beside(u).wait()
            self.pass_on(u, 1).start()
        else:
            for n in range(2):
                self.pass_on(u, n).wait()

    def at(self, *where):
        for kind, u in PLAN.get(where, ()):
            self.step(kind, u)


class Reducer:
    def __init__(self, grads, got1, got3, got2, got_dp, send, recv):
        self.keep, self.near, self.cross, self.far = (grads.at[n] for n in range(4))
        self.total = self.near
        self.units = grads.shape[1] // UNIT
        self.got1, self.got3, self.got2 = got1, got3, got2
        self.got_half, self.got_quad, self.got_whole = got_dp[0], got_dp[1], got_dp[2:]
        self.send, self.recv = send, recv
        bits = powers("dp")
        self.bits, self.four, self.rest = bits[0], bits[1:3], bits[3:]
        self.half, self.quarter = UNIT // 2, UNIT // 8
        self.base = bit_of("dp", self.bits) * self.half
        self.offset = self.base + quad_peer(self.four, 0)[1] * self.quarter
        self.ticks = self.units + 7 + len(self.rest)

    def rows(self, u, size, offset=0):
        return pl.ds(pl.multiple_of(u * UNIT + offset, TILE), size)

    def slot(self, u, size):
        return pl.ds(pl.multiple_of((u % SLOTS) * size, TILE), size)

    def copy(self, stage, u, source, target, peer):
        return remote(source, target, self.send.at[stage, u], self.recv.at[stage, u], peer)

    def first(self, u):
        at, here, peer = self.rows(u, UNIT), self.slot(u, UNIT), flip("mp", 1)
        return (
            self.copy(0, u, self.near.at[at], self.got1.at[here], peer),
            self.copy(1, u, self.far.at[at], self.got3.at[here], peer),
        )

    def second(self, u):
        return self.copy(2, u, self.cross.at[self.rows(u, UNIT)], self.got2.at[self.slot(u, UNIT)], flip("mp", 2))

    def halve(self, u):
        source = self.keep.at[self.rows(u, self.half, self.half - self.base)]
        return self.copy(3, u, source, self.got_half.at[self.slot(u, self.half)], flip("dp", self.bits))

    def quads(self, u):
        copies = []
        for step in range(1, 4):
            peer, place = quad_peer(self.four, step)
            source = self.keep.at[self.rows(u, self.quarter, self.base + place * self.quarter)]
            target = self.got_quad.at[step - 1, self.slot(u, self.quarter)]
            copies.append(self.copy(3 + step, u, source, target, peer))
        return copies

    def whole(self, u, k):
        source = self.keep.at[self.rows(u, self.quarter, self.offset)]
        return self.copy(7 + k, u, source, self.got_whole[k].at[self.slot(u, self.quarter)], flip("dp", self.rest[k]))

    def quads_back(self, u):
        part = self.total.at[self.rows(u, self.quarter, self.offset)]
        first = 6 + len(self.rest)
        return [self.copy(first + step, u, part, part, quad_peer(self.four, step)[0]) for step in range(1, 4)]

    def half_back(self, u):
        part = self.total.at[self.rows(u, self.half, self.base)]
        return self.copy(10 + len(self.rest), u, part, part, flip("dp", self.bits))

    def add(self, source, target, u, size, offset, terms):
        def tile(i, carry):
            at = pl.ds(pl.multiple_of(u * UNIT + offset + i * TILE, TILE), TILE)
            value = source[at].astype(F32)
            for ref in terms:
                value += ref[pl.ds(pl.multiple_of((u % SLOTS) * size + i * TILE, TILE), TILE)].astype(F32)
            target[at] = value.astype(BF)
            return carry

        lax.fori_loop(0, size // TILE, tile, 0, unroll=True)

    def tick(self, t):
        rest = len(self.rest)

        def at(lag, body):
            u = t - lag

            @pl.when((u >= 0) & (u < self.units))
            def _():
                body(u)

        def each(copies, begin):
            for copy in copies:
                if begin:
                    copy.start()
                else:
                    copy.wait()

        def start_first(u):
            each(self.first(u), True)

        def after_first(u):
            each(self.first(u), False)
            self.add(self.cross, self.cross, u, UNIT, 0, [self.got3])
            self.second(u).start()

        def after_second(u):
            self.second(u).wait()
            self.add(self.keep, self.keep, u, UNIT, 0, [self.got1, self.got2])
            self.halve(u).start()

        def after_half(u):
            self.halve(u).wait()
            self.add(self.keep, self.keep, u, self.half, self.base, [self.got_half])
            each(self.quads(u), True)

        def after_quads(u):
            each(self.quads(u), False)
            terms = [self.got_quad.at[n] for n in range(3)]
            self.add(self.keep, self.keep if rest else self.total, u, self.quarter, self.offset, terms)
            each([self.whole(u, 0)] if rest else self.quads_back(u), True)

        def after_whole(k):
            def body(u):
                self.whole(u, k).wait()
                last = k == rest - 1
                target = self.total if last else self.keep
                self.add(self.keep, target, u, self.quarter, self.offset, [self.got_whole[k]])
                each(self.quads_back(u) if last else [self.whole(u, k + 1)], True)

            return body

        def after_quads_back(u):
            each(self.quads_back(u), False)
            self.half_back(u).start()

        def after_half_back(u):
            self.half_back(u).wait()

        at(0, start_first)
        at(1, after_first)
        at(3, after_second)
        at(4, after_half)
        at(5, after_quads)
        for k in range(rest):
            at(6 + k, after_whole(k))
        at(6 + rest, after_quads_back)
        at(7 + rest, after_half_back)


class SmallSum:
    def __init__(self, value, got, send, recv):
        self.value, self.got, self.send, self.recv = value, got, send, recv
        self.peers = [flip("mp", b) for b in BITS_MP] + [flip("dp", b) for b in powers("dp")]

    def copy(self, k):
        return remote(self.value, self.got.at[k], self.send.at[k], self.recv.at[k], self.peers[k])

    def finish(self, k):
        self.copy(k).wait()
        value, got = self.value, self.got
        value[:8] += got[k, :8]
        if k == 0:
            value[8:10] += got[k, 10:12]
            value[12:14] += got[k, 14:16]
        elif k == 1:
            value[8:10] += got[k, 12:14]
        else:
            value[8:10] += got[k, 8:10]


def layer_body(
    heads,
    rows,
    tokens_in,
    gain1_in,
    bias1_in,
    gain2_in,
    bias2_in,
    bias_out_in,
    bias_down_in,
    positions_in,
    keep_mask_in,
    bias_qkv_in,
    freqs_in,
    bias_up_in,
    group,
    cot,
    s_qkv,
    s_out,
    s_up,
    s_down,
    out,
    gx,
    o_up,
    o_down,
    o_out,
    o_qkv,
    small_sum,
    factor_out,
    tokens,
    gain1,
    bias1,
    gain2,
    bias2,
    bias_out,
    bias_down,
    positions,
    keep_mask,
    bias_qkv,
    freqs,
    bias_up,
    all_w,
    small,
    place,
    q_all,
    k_all,
    v_all,
    lse,
    att,
    cosine,
    sine,
    normed1,
    middle,
    branch,
    g,
    mlp,
    gsecond,
    active,
    slope,
    vec,
    keep_col,
    feats,
    sums_up,
    sums_vec,
    column,
    head_sums,
    grads,
    got1,
    got3,
    got2,
    got_small,
    send_g,
    recv_g,
    send_s,
    recv_s,
    local_sem,
    send,
    recv,
    send_v,
    recv_v,
    *got_dp,
):
    parts, count = all_w.shape[0], q_all.shape[0]
    local = heads * HD
    width = tokens.shape[1]
    wide = q_all.shape[2]
    top = 4 * local
    units = (all_w.shape[1] - top) // 2
    mlp_rows = 2 * width
    up_rows, down_rows = pl.ds(top, width), pl.ds(top + width, units)
    loads, start = [], 0
    for n, ref in enumerate((s_qkv, s_out, s_up, s_down)):
        loads.append(pltpu.make_async_copy(ref, all_w.at[0, pl.ds(start, ref.shape[0])], local_sem.at[n]))
        start += ref.shape[0]
    load_cot = pltpu.make_async_copy(cot, slope, local_sem.at[5])
    early = []
    for n, (source, target) in enumerate(
        (
            (bias_up_in, bias_up),
            (bias_qkv_in, bias_qkv),
            (freqs_in, freqs),
            (tokens_in, tokens),
            (gain1_in, gain1),
            (bias1_in, bias1),
            (gain2_in, gain2),
            (bias2_in, bias2),
            (bias_out_in, bias_out),
            (bias_down_in, bias_down),
            (positions_in, positions),
            (keep_mask_in, keep_mask),
        )
    ):
        early.append(pltpu.make_async_copy(source, target, local_sem.at[12 + n]))
    for load in early[:3] + loads + early[3:]:
        load.start()
    for load in early[:3]:
        load.wait()
    small[0] = jnp.zeros_like(small[0])
    small[0, 0:1] = bias_up[...].reshape(1, units).astype(F32)
    row = [bias_qkv[n : n + 1] for n in range(3)] + [freqs[h, n : n + 1] for n in range(2) for h in range(heads)]
    small[0, 1:2] = jnp.concatenate(row, axis=1)
    both = {"mp": lax.axis_index("mp") + 1 * (1 - 2 * bit_of("mp", 1)) + 2 * (1 - 2 * bit_of("mp", 2))}
    sums = SmallSum(small_sum, got_small, send_v, recv_v)
    greet(sums.peers + [both])
    peers = [flip("mp", 1), flip("mp", 2), both]
    smalls = [
        remote(small.at[0], small.at[r], send_s.at[r - 1], recv_s.at[r - 1], peers[r - 1]) for r in range(1, 4)
    ]
    for copy in smalls:
        copy.start()
    weights = Gather(all_w, send_g, recv_g)
    for load in loads + early[3:]:
        load.wait()
    for u in range(DEPTH):
        weights.across(u).start()
    weights.owns(0, weights.pieces, True)
    load_cot.start()
    for n, ref in enumerate((gain1, bias1, gain2, bias2, bias_out, bias_down)):
        vec[n : n + 1] = ref[...].reshape(1, width)
    first_norm(tokens, vec, normed1)
    own_part = lax.axis_index("mp")
    spot = jnp.concatenate([positions[...], keep_mask[...].reshape(1, keep_mask.shape[0])])
    mine = spot[:, :rows]
    for n in range(1, parts):
        mine = jnp.where(own_part == n, spot[:, n * rows : (n + 1) * rows], mine)
    place[...] = jnp.zeros_like(place)
    place[0:3, :rows] = mine.astype(F32)
    masks(rows, place, group, feats, keep_col)
    for copy in smalls:
        copy.wait()
    proj = mlp.at[: 3 * local, :wide]

    first_rows = 3 * local // PIECE
    for r in range(parts):
        weights.at("p", r, 0)
        if r == 1:
            weights.owns(0, first_rows, False)
        attend_chunk(
            r, heads, rows, normed1, all_w, functools.partial(weights.at, "p", r), small, place, feats,
            q_all, k_all, v_all, lse, att, cosine, sine, proj,
        )
    weights.owns(first_rows, weights.pieces, False)
    load_cot.wait()
    g[...] = (slope[...] * keep_col[...]).astype(BF)
    weights.at("w", 0, 0)
    wo = jnp.concatenate([all_w[r, 3 * local : top] for r in range(parts)])
    normed2 = branch.at[:rows]
    second_norm(rows, tokens, vec, att, wo, middle, normed2)
    mlp[...] = jnp.zeros_like(mlp)
    gsecond[...] = jnp.zeros_like(gsecond)

    net = Reducer(grads, got1, got3, got2, got_dp, send, recv)

    def between(r, n):
        for k in range(parts):
            if ("f", k, n + 1) in PLAN:
                pl.when(r == k)(functools.partial(weights.at, "f", k, n + 1))
        if n > 0:
            @pl.when(r == parts - 1)
            def _():
                net.tick(n - 1)

    def mlp_step(r, carry):
        mlp_chunk(
            r, normed2, g, all_w.at[r, up_rows], all_w.at[r, down_rows], small, mlp, gsecond,
            grads.at[r, pl.ds(0, mlp_rows)], sums_up, active, slope, functools.partial(between, r),
        )
        return carry

    lax.fori_loop(0, parts, mlp_step, 0)
    load_cot.start()

    def step(t, carry):
        net.tick(t)
        return carry

    def ticks(start, stop):
        lax.fori_loop(start, stop, step, 0)

    load_cot.wait()
    finish_mlp(slope, keep_col, vec, middle, mlp, gsecond, g, active, branch, sums_vec)
    store_out = pltpu.make_async_copy(active, out, local_sem.at[6])
    store_out.start()
    ticks(3, 4)
    gatt = all_w.at[0, down_rows, :wide]
    gqkv = all_w.at[:, pl.ds(top, 3 * local), :wide]
    wo = jnp.concatenate([all_w[r, 3 * local : top] for r in range(parts)])
    gatt[...] = nt(wo, branch[...]).astype(BF)

    per = 2

    def some_heads(i, carry):
        net.tick(4 + i)

        def head(n, c):
            attend_back(per * i + n, heads, rows, q_all, k_all, v_all, lse, att, gatt, cosine, sine, place, gqkv, column, head_sums)
            return c

        return lax.fori_loop(0, per, head, carry)

    lax.fori_loop(0, count // per, some_heads, 0)
    base = 4 + count // per
    assert count % per == 0 and base + parts // 2 <= mlp_rows // UNIT
    gsecond[...] = jnp.zeros_like(gsecond)

    def late(r, carry):
        pl.when(r % 2 == 0)(lambda: net.tick(base + r // 2))
        here = att[pl.ds(pl.multiple_of(r * local, HD), local)]
        grads[r, mlp_rows : mlp_rows + local] = nn(here, branch[...]).astype(BF)
        grads[r, mlp_rows + local :] = nn(gqkv[r], normed1[...]).astype(BF)
        gsecond[...] += tn(gqkv[r], all_w[r, : 3 * local])[:rows]
        return carry

    lax.fori_loop(0, parts, late, 0)
    base = base + parts // 2
    ticks(base, base + 1)
    grad = gsecond[...]
    unit, scale = unit_of(tokens[...].astype(F32))
    gsecond[...] = middle[...] + norm_back(grad, unit, scale, vec[0:1])
    store_gx = pltpu.make_async_copy(gsecond, gx, local_sem.at[7])
    store_gx.start()
    small_sum[...] = jnp.zeros_like(small_sum)
    small_sum[0:1] = jnp.sum(grad * unit, axis=0, keepdims=True)
    small_sum[1:2] = jnp.sum(grad, axis=0, keepdims=True)
    small_sum[2:7] = sums_vec[0:5]
    for r in range(parts):
        small_sum[8 + 2 * r : 9 + 2 * r] = sums_up[r]
        mine = [head_sums[r * heads + h : r * heads + h + 1] for h in range(heads)]
        pieces = [v[:, n * HD : (n + 1) * HD] for n in range(3) for v in mine]
        pieces += [v[:, 3 * HD + n * HALF : 3 * HD + (n + 1) * HALF] for n in range(2) for v in mine]
        small_sum[9 + 2 * r : 10 + 2 * r] = jnp.concatenate(pieces, axis=1)
    base = base + 1
    exchanges = len(sums.peers)

    def step_small(t, carry):
        net.tick(t)
        for k in range(exchanges + 1):
            @pl.when(t == base + k)
            def _():
                if k > 0:
                    sums.finish(k - 1)
                if k == exchanges:
                    factor = lax.axis_size("dp") / small_sum[6:7]
                    factor_out[0] = factor[0, 0]
                    small_sum[...] *= factor
                if k < exchanges:
                    sums.copy(k).start()
        return carry

    lax.fori_loop(base, base + exchanges + 1, step_small, 0)
    stores = []
    start = 0
    for n, ref in enumerate((o_down, o_up, o_out, o_qkv)):
        if n == 2:
            ticks(base + exchanges + 1, max(net.ticks, base + exchanges + 1))
        stores.append(pltpu.make_async_copy(grads.at[1, pl.ds(start, ref.shape[0])], ref, local_sem.at[8 + n]))
        stores[-1].start()
        start += ref.shape[0]
    for copy in stores + [store_out, store_gx]:
        copy.wait()


def finish_body(vectors, local, up, down, out, qkv, small, factor, middle, gx, *rest):
    shared = len(vectors) + 2
    results, rest = rest[: 6 + shared], rest[6 + shared :]
    low, full, copies = rest[:6], rest[6:10], rest[10]
    sources = (up, down, out, qkv, middle, gx)
    targets = results[:4] + results[4 + shared :]
    loads = [pltpu.make_async_copy(a, b, copies.at[0, n]) for n, (a, b) in enumerate(zip(sources, low))]
    ready = full + low[4:]
    stores = [pltpu.make_async_copy(a, b, copies.at[1, n]) for n, (a, b) in enumerate(zip(ready, targets))]
    order = (3, 2, 0, 1, 5, 4)
    for n in order:
        loads[n].start()
    for n, row in enumerate(vectors):
        results[4 + n][...] = small[row : row + 1].reshape(small.shape[1])
    b_qkv, freqs = results[4 + len(vectors)], results[5 + len(vectors)]
    for n in range(3):
        b_qkv[n : n + 1] = small[9:10, n * local : (n + 1) * local]
    for n in range(2):
        for h in range(freqs.shape[0]):
            start = 3 * local + (n * freqs.shape[0] + h) * HALF
            freqs[h, n : n + 1] = small[9:10, start : start + HALF]
    for n in order:
        loads[n].wait()
        if n < 4:
            full[n][...] = low[n][...].astype(F32) * factor[0]
        stores[n].start()
    for n in order:
        stores[n].wait()


def sds(shape, dtype):
    return jax.ShapeDtypeStruct(shape, dtype)


def body(
    tokens,
    image_group,
    positions,
    keep_mask,
    norm1_gain,
    norm1_bias,
    w_qkv,
    b_qkv,
    rotary_freqs,
    w_out,
    b_out,
    norm2_gain,
    norm2_bias,
    w_up,
    b_up,
    w_down,
    b_down,
    cotangent,
):
    rows, width = tokens.shape
    wide = -(-rows // LANES) * LANES
    parts = lax.axis_size("mp")
    mp_index = lax.axis_index("mp")
    heads = rotary_freqs.shape[1]
    local = heads * HD
    units = w_up.shape[1]
    w_qkv_t = w_qkv.reshape(width, 3 * local).T
    count = parts * heads
    bits = powers("dp")
    sizes = steps_of(bits)
    stages = 8 + len(bits)
    total_rows = 2 * width + 4 * local
    unit_count = total_rows // UNIT
    pieces = total_rows // PIECE
    swaps = 2 + len(bits)
    in_vmem = pl.BlockSpec(memory_space=pltpu.VMEM)
    in_smem = pl.BlockSpec(memory_space=pltpu.SMEM)
    anywhere = pl.BlockSpec(memory_space=pl.ANY)
    dma = pltpu.SemaphoreType.DMA
    vmem = pltpu.VMEM
    out, gx, o_up, o_down, o_out, o_qkv, small_sum, factor = pl.pallas_call(
        functools.partial(layer_body, heads, rows),
        out_shape=[
            sds((rows, width), BF),
            sds((rows, width), F32),
            sds((width, units), BF),
            sds((units, width), BF),
            sds((local, width), BF),
            sds((3 * local, width), BF),
            sds((16, width), F32),
            sds((1,), F32),
        ],
        in_specs=[anywhere] * 12 + [in_smem] + [anywhere] * 5,
        out_specs=[anywhere] * 6 + [in_vmem, in_smem],
        scratch_shapes=[
            vmem(tokens.shape, BF),
        ]
        + [vmem((width,), F32)] * 6
        + [
            vmem(positions.shape, jnp.int32),
            vmem(keep_mask.shape, jnp.int32),
            vmem(b_qkv.shape, F32),
            vmem((heads, 2, HALF), F32),
            vmem(b_up.shape, BF),
            vmem((parts, total_rows, width), BF),
            vmem((parts, 8, width), F32),
            vmem((8, wide), F32),
            vmem((count, AUG, wide), BF),
            vmem((count, AUG, wide), BF),
            vmem((count, AUG, wide), BF),
            vmem((count, 8, wide), F32),
            vmem((count * HD, wide), BF),
            vmem((parts, heads * HALF, wide), F32),
            vmem((parts, heads * HALF, wide), F32),
            vmem((wide, width), BF),
            vmem((rows, width), F32),
            vmem((wide, width), BF),
            vmem((rows, width), BF),
            vmem((rows, width), F32),
            vmem((rows, width), F32),
            vmem((rows, units), BF),
            vmem((rows, units), F32),
            vmem((8, width), F32),
            vmem((rows, 1), F32),
            vmem((3, 16, wide), BF),
            vmem((parts, 1, units), F32),
            vmem((8, width), F32),
            vmem((3 * HD + 2 * HALF, LANES), F32),
            vmem((-(-count // 8) * 8, 3 * HD + 2 * HALF), F32),
            vmem((parts, total_rows, width), BF),
            vmem((SLOTS * UNIT, width), BF),
            vmem((SLOTS * UNIT, width), BF),
            vmem((SLOTS * UNIT, width), BF),
            vmem((swaps, 16, width), F32),
            dma((5, pieces)),
            dma((5, pieces)),
            dma((3,)),
            dma((3,)),
            dma((24,)),
            dma((stages, unit_count)),
            dma((stages, unit_count)),
            dma((swaps,)),
            dma((swaps,)),
        ]
        + [vmem((SLOTS * UNIT // 2, width), BF), vmem((3, SLOTS * UNIT // 8, width), BF)]
        + [vmem((SLOTS * size, width), BF) for size in sizes[2:]],
        compiler_params=pltpu.CompilerParams(vmem_limit_bytes=61 << 20, collective_id=0, has_side_effects=True),
    )(tokens, norm1_gain, norm1_bias, norm2_gain, norm2_bias, b_out, b_down, positions, keep_mask, b_qkv,
      rotary_freqs.transpose(1, 0, 2), b_up, image_group, cotangent, w_qkv_t, w_out, w_up, w_down)
    sums = (o_up, o_down, o_out, o_qkv)
    vectors = [0, 1, 2, 3, 4, 5, 8]
    finished = pl.pallas_call(
        functools.partial(finish_body, vectors, local),
        out_shape=[sds(ref.shape, F32) for ref in sums]
        + [sds((width,), F32)] * len(vectors)
        + [sds((3, local), F32), sds((heads, 2, HALF), F32), sds(out.shape, BF), sds(gx.shape, F32)],
        in_specs=[anywhere] * 4 + [in_vmem, in_smem, anywhere, anywhere],
        out_specs=[anywhere] * 4 + [in_vmem] * (len(vectors) + 2) + [anywhere] * 2,
        scratch_shapes=[vmem(ref.shape, BF) for ref in sums]
        + [vmem(out.shape, BF), vmem(gx.shape, F32)]
        + [vmem(ref.shape, F32) for ref in sums]
        + [dma((2, 6))],
        compiler_params=pltpu.CompilerParams(vmem_limit_bytes=60 << 20),
    )(*sums, small_sum, factor, out, gx)
    sum_w_up, sum_w_down, sum_w_out, sum_w_qkv, gain1, bias1, b_out_sum, gain2, bias2, b_down_sum, b_up_sum = finished[:11]
    b_qkv_sum, freqs_sum, out, gx = finished[11:]
    return (
        out,
        gx,
        gain1,
        bias1,
        sum_w_qkv.T.reshape(w_qkv.shape),
        b_qkv_sum,
        freqs_sum.transpose(1, 0, 2),
        sum_w_out,
        b_out_sum,
        gain2,
        bias2,
        sum_w_up,
        b_up_sum,
        sum_w_down,
        b_down_sum,
    )


def solution(mesh):
    placed = (
        P(("dp", "mp"), None),
        P("dp"),
        P(None, "dp"),
        P("dp"),
        P(),
        P(),
        P(None, None, "mp"),
        P(None, "mp"),
        P(None, "mp", None),
        P("mp", None),
        P(),
        P(),
        P(),
        P(None, "mp"),
        P("mp"),
        P("mp", None),
        P(),
        P(("dp", "mp"), None),
    )
    return jax.shard_map(
        body,
        mesh=mesh,
        in_specs=placed,
        out_specs=(
            P(("dp", "mp"), None),
            P(("dp", "mp"), None),
            P(),
            P(),
            P(None, None, "mp"),
            P(None, "mp"),
            P(None, "mp", None),
            P("mp", None),
            P(),
            P(),
            P(),
            P(None, "mp"),
            P("mp"),
            P("mp", None),
            P(),
        ),
        check_vma=False,
    )
```

```python
import math
import functools

import jax
import jax.numpy as jnp
from jax import lax
from jax.experimental import pallas as pl
from jax.experimental.pallas import tpu as pltpu
from jax.sharding import PartitionSpec as P

HD = 64
SIDE_SMALL = 14
SIDE_LARGE = 24
IMG_SMALL = 3
IMG_LARGE = 1
NORM_EPS = 1e-06
HIDE = -1e30
BF = jnp.bfloat16
F32 = jnp.float32
SCALE = 1.0 / math.sqrt(HD)
HALF = HD // 2
LANES = 128
AUG = HD + 16


def nn(a, b):
    return jnp.dot(a, b, preferred_element_type=F32)


def tn(a, b):
    return lax.dot_general(a, b, (((0,), (0,)), ((), ())), preferred_element_type=F32)


def nt(a, b):
    return lax.dot_general(a, b, (((1,), (1,)), ((), ())), preferred_element_type=F32)


def unit_of(values):
    mean = jnp.mean(values, axis=-1, keepdims=True)
    centered = values - mean
    variance = jnp.mean(centered * centered, axis=-1, keepdims=True)
    scale = lax.rsqrt(variance + NORM_EPS)
    return centered * scale, scale


def norm_back(grad, unit, scale, gain):
    u = grad * gain
    mean_u = jnp.mean(u, axis=-1, keepdims=True)
    mean_un = jnp.mean(u * unit, axis=-1, keepdims=True)
    return scale * (u - mean_u - unit * mean_un)


def gelu_both(v):
    cdf = 0.5 * (1.0 + lax.erf(v * (1.0 / math.sqrt(2.0))))
    pdf = jnp.exp(-0.5 * v * v) * (1.0 / math.sqrt(2.0 * math.pi))
    return v * cdf, cdf + v * pdf


def pad_rows(value, rows):
    return jnp.concatenate(
        [value, jnp.zeros((rows - value.shape[0],) + value.shape[1:], value.dtype)]
    )


def first_norm(tokens, vec, normed1):
    unit, _ = unit_of(tokens[...].astype(F32))
    normed = (unit * vec[0:1] + vec[1:2]).astype(BF)
    normed1[...] = pad_rows(normed, normed1.shape[0])


def masks(rows, place, group, feats, keep):
    wide = place.shape[1]
    slot = lax.broadcasted_iota(jnp.int32, (16, wide), 1)
    row = lax.broadcasted_iota(jnp.int32, (16, wide), 0)
    image_id = jnp.zeros((16, wide), jnp.int32)
    for is_large, side, images in ((0, SIDE_SMALL, IMG_SMALL), (1, SIDE_LARGE, IMG_LARGE)):
        mine = sum([(slot >= n * side * side).astype(jnp.int32) for n in range(1, images)], jnp.zeros((16, wide), jnp.int32))
        image_id = jnp.where(group[0] == is_large, mine, image_id)
    same = (image_id == row) & (row < max(IMG_SMALL, IMG_LARGE))
    hidden = jnp.logical_not(same & (place[2:3] > 0.5)) & (row < max(IMG_SMALL, IMG_LARGE))
    feats[0] = jnp.where(same, 1.0, 0.0).astype(BF)
    feats[1] = jnp.where(hidden, HIDE, 0.0).astype(BF)
    feats[2] = jnp.where(row == 0, 1.0, 0.0).astype(BF)
    keep[...] = place[...].T[:rows, 2:3]


def turns(r, heads, small, place, cosine, sine):
    start = 3 * heads * HD
    column = small[r].T[:, 1:2]
    f0 = column[start : start + heads * HALF]
    f1 = column[start + heads * HALF : start + 2 * heads * HALF]
    angles = f0 * place[0:1] + f1 * place[1:2]
    cosine[r] = jnp.cos(angles)
    sine[r] = jnp.sin(angles)


def attend_chunk(r, heads, rows, normed1, weights, hook, small, place, feats, q_all, k_all, v_all, lse, att, cosine, sine, proj):
    local = heads * HD
    column = small[r].T[:, 1:2]
    proj[...] = nt(weights[r, : 3 * local], normed1[...]) + column[: 3 * local]
    hook(1)
    for h in range(heads):
        cos_h = cosine[r, h * HALF : (h + 1) * HALF]
        sin_h = sine[r, h * HALF : (h + 1) * HALF]
        at = r * heads + h
        for base, ref, scale in ((0, q_all, SCALE), (local, k_all, 1.0)):
            a = proj[base + h * HD : base + h * HD + HALF]
            b = proj[base + h * HD + HALF : base + (h + 1) * HD]
            ref[at, :HALF] = ((a * cos_h - b * sin_h) * scale).astype(BF)
            ref[at, HALF:HD] = ((b * cos_h + a * sin_h) * scale).astype(BF)
        v_all[at, :HD] = proj[2 * local + h * HD : 2 * local + (h + 1) * HD].astype(BF)
        q_all[at, HD:] = feats[0]
        k_all[at, HD:] = feats[1]
        v_all[at, HD:] = feats[2]

    def head(h, carry):
        at = r * heads + h
        scores = tn(k_all[at, :, :rows], q_all[at])
        top = jnp.max(scores, axis=0, keepdims=True)
        terms = jnp.exp(scores - top).astype(BF)
        mixed = nn(v_all[at, :, :rows], terms)
        total = mixed[HD : HD + 1]
        att[pl.ds(pl.multiple_of(at * HD, HD), HD)] = (mixed[:HD] * (1.0 / total)).astype(BF)
        lse[at] = jnp.broadcast_to(top + jnp.log(total), lse.shape[1:])
        for n in range(heads - 1):
            pl.when(h == n)(functools.partial(hook, 2 + n))
        return carry

    lax.fori_loop(0, heads, head, 0)


def second_norm(rows, tokens, vec, att, wo, middle, normed2):
    branch = tn(att[...], wo)
    middle[...] = tokens[...].astype(F32) + branch[:rows] + vec[4:5]
    unit, _ = unit_of(middle[...])
    normed2[...] = (unit * vec[2:3] + vec[3:4]).astype(BF)


def mlp_chunk(r, normed2, g, wu, wd, small, mlp, gsecond, target, sums, active, slope, hook):
    width = normed2.shape[1]
    hook(-1)
    hidden = nn(normed2[...], wu[...]) + small[r][0:1]
    act, der = gelu_both(hidden)
    active[...] = act.astype(BF)
    slope[...] = der
    hook(0)
    target[: active.shape[1]] = tn(active[...], g[...]).astype(BF)
    hook(1)
    mlp[...] += nn(active[...], wd[...])
    gh = nt(g[...], wd[...]) * slope[...]
    active[...] = gh.astype(BF)
    sums[r] = jnp.sum(active[...].astype(F32), axis=0, keepdims=True)
    hook(2)
    target[active.shape[1] :] = tn(normed2[...], active[...]).astype(BF)
    hook(3)
    gsecond[...] += nt(active[...], wu[...])


def finish_mlp(cot, keep, vec, middle, mlp, gsecond, g, out, branch, sums_vec):
    out[...] = (middle[...] + mlp[...] + vec[5:6]).astype(BF)
    unit, scale = unit_of(middle[...])
    grad = gsecond[...]
    gm = cot[...] * keep[...] + norm_back(grad, unit, scale, vec[2:3])
    low = gm.astype(BF)
    sums_vec[...] = jnp.concatenate(
        [
            jnp.sum(low.astype(F32), axis=0, keepdims=True),
            jnp.sum(grad * unit, axis=0, keepdims=True),
            jnp.sum(grad, axis=0, keepdims=True),
            jnp.sum(g[...].astype(F32), axis=0, keepdims=True),
            jnp.full((4, grad.shape[1]), 1.0, F32) * jnp.sum(keep[...]),
        ]
    )
    middle[...] = gm
    branch[...] = pad_rows(low, branch.shape[0])


def attend_back(at, heads, rows, q_all, k_all, v_all, lse, att, gatt, cosine, sine, place, gqkv, column, sums):
    local = heads * HD
    r, h = at // heads, at % heads
    here = pl.ds(pl.multiple_of(at * HD, HD), HD)
    wide = q_all.shape[2]
    scores = tn(k_all[at, :, :rows], q_all[at])
    probs = jnp.exp(scores - lse[at, 0:1])
    go = gatt[here]
    inner = jnp.sum(go.astype(F32) * att[here].astype(F32), axis=0, keepdims=True)
    gp = tn(v_all[at, :HD, :rows], go)
    gs = (probs * (gp - inner)).astype(BF)
    gv = nt(go, probs.astype(BF))
    gk = nt(q_all[at, :HD], gs)
    gq = nn(k_all[at, :HD, :rows], gs) * SCALE
    hs = pl.ds(pl.multiple_of(h * HALF, HALF), HALF)
    cos_h, sin_h = cosine[r, hs], sine[r, hs]
    term = jnp.zeros((HALF, wide), F32)
    pad = jnp.zeros((HD, wide - rows), F32)
    gk = jnp.concatenate([gk, pad], axis=1)
    gv = jnp.concatenate([gv, pad], axis=1)
    lows = []
    for ref, grad, back in ((q_all, gq, 1.0 / SCALE), (k_all, gk, 1.0)):
        a, b = grad[:HALF], grad[HALF:]
        ra = ref[at, :HALF].astype(F32)
        rb = ref[at, HALF:HD].astype(F32)
        term += (b * ra - a * rb) * back
        lows.append(jnp.concatenate([a * cos_h + b * sin_h, b * cos_h - a * sin_h], axis=0).astype(BF))
    lows.append(gv.astype(BF))
    for n, low in enumerate(lows):
        gqkv[r, pl.ds(pl.multiple_of(n * local + h * HD, HD), HD)] = low
        total = jnp.sum(low.astype(F32), axis=1, keepdims=True)
        column[n * HD : (n + 1) * HD] = jnp.broadcast_to(total, (HD, LANES))
    for n in range(2):
        total = jnp.sum(term * place[n : n + 1], axis=1, keepdims=True)
        column[3 * HD + n * HALF : 3 * HD + (n + 1) * HALF] = jnp.broadcast_to(total, (HALF, LANES))
    sums[pl.ds(at, 1)] = column[...].T[0:1]


UNIT = 128
PIECE = 192
DEPTH = 3
SIZES = (192, 192, 192, 192, 192, 192, 192, 192, 192, 192, 192, 192)
PLAN = {
    ('p', 0, 2): (('a', 0),),
    ('p', 1, 1): (('a', 1),),
    ('p', 1, 3): (('a', 2), ('b', 0)),
    ('p', 4, 0): (('d', 0),),
    ('p', 4, 1): (('a', 3),),
    ('p', 2, 0): (('b', 1), ('d', 1), ('a', 4), ('b', 2)),
    ('p', 2, 1): (('d', 2),),
    ('p', 2, 3): (('b', 3), ('a', 5)),
    ('p', 3, 0): (('d', 3),),
    ('p', 3, 2): (('b', 4), ('a', 6)),
    ('p', 3, 3): (('d', 4),),
    ('f', 0, 0): (('a', 7), ('b', 5)),
    ('f', 0, 1): (('a', 8), ('d', 5), ('b', 6)),
    ('f', 0, 2): (('d', 6),),
    ('f', 0, 3): (('a', 9),),
    ('f', 0, 4): (('b', 7),),
    ('f', 1, 0): (('a', 10), ('d', 7)),
    ('f', 1, 1): (('b', 8),),
    ('f', 1, 2): (('a', 11), ('d', 8)),
    ('f', 1, 3): (('b', 9),),
    ('f', 1, 4): (('b', 10), ('d', 9)),
    ('f', 2, 0): (('d', 10), ('b', 11)),
    ('f', 2, 1): (('d', 11),),
}
SLOTS = 6
TILE = 16
BITS_MP = (1, 2)


def flip(axis, bit):
    me = lax.axis_index(axis)
    return {axis: me + bit * (1 - 2 * ((me // bit) % 2))}


def bit_of(axis, bit):
    return (lax.axis_index(axis) // bit) % 2


def powers(axis):
    size = lax.axis_size(axis)
    return [1 << k for k in range(size.bit_length() - 1)]


def greet(peers):
    barrier = pltpu.get_barrier_semaphore()
    for peer in peers:
        pl.semaphore_signal(barrier, inc=1, device_id=peer, device_id_type=pl.DeviceIdType.MESH)
    pl.semaphore_wait(barrier, len(peers))


def remote(src, dst, send, recv, peer):
    return pltpu.make_async_remote_copy(
        src_ref=src, dst_ref=dst, send_sem=send, recv_sem=recv, device_id=peer, device_id_type=pl.DeviceIdType.MESH
    )


def steps_of(bits):
    return [UNIT // 2, UNIT // 8] + [UNIT // 8] * (len(bits) - 3)


def quad_peer(bits, step):
    one, two = bit_of("dp", bits[0]), bit_of("dp", bits[1])
    other_one = 1 - one if step & 1 else one
    other_two = 1 - two if step & 2 else two
    me = lax.axis_index("dp")
    return {"dp": me + bits[0] * (other_one - one) + bits[1] * (other_two - two)}, other_one + 2 * other_two


class Gather:
    def __init__(self, weights, send, recv):
        self.weights, self.send, self.recv = weights, send, recv
        self.pieces = len(SIZES)
        assert sum(SIZES) == weights.shape[1]

    def rows(self, u, mine):
        start, half = sum(SIZES[:u]), SIZES[u] // 2
        upper = bit_of("dp", 1 + u % 2)
        return pl.ds(pl.multiple_of(start + (upper if mine else 1 - upper) * half, TILE), half)

    def copy(self, stage, u, source, target, rows, peer):
        return remote(
            self.weights.at[source, rows],
            self.weights.at[target, rows],
            self.send.at[stage, u],
            self.recv.at[stage, u],
            peer,
        )

    def own(self, u):
        return self.copy(0, u, 0, 1, pl.ds(pl.multiple_of(u * PIECE, TILE), PIECE), flip("mp", 1))

    def across(self, u):
        return self.copy(1, u, 0, 2, self.rows(u, True), flip("mp", 2))

    def beside(self, u):
        return self.copy(2, u, 2, 2, self.rows(u, True), flip("dp", 1 + u % 2))

    def pass_on(self, u, n):
        return self.copy(3 + n, u, 2, 3, self.rows(u, n == 0), flip("mp", 1))

    def owns(self, start, stop, begin):
        def each(u, carry):
            if begin:
                self.own(u).start()
            else:
                self.own(u).wait()
            return carry

        lax.fori_loop(start, stop, each, 0)

    def step(self, kind, u):
        if kind == "a":
            self.across(u).wait()
            if u + DEPTH < self.pieces:
                self.across(u + DEPTH).start()
            self.beside(u).start()
            self.pass_on(u, 0).start()
        elif kind == "b":
            self.beside(u).wait()
            self.pass_on(u, 1).start()
        else:
            for n in range(2):
                self.pass_on(u, n).wait()

    def at(self, *where):
        for kind, u in PLAN.get(where, ()):
            self.step(kind, u)


class Reducer:
    def __init__(self, grads, got1, got3, got2, got_dp, send, recv):
        self.keep, self.near, self.cross, self.far = (grads.at[n] for n in range(4))
        self.total = self.near
        self.units = grads.shape[1] // UNIT
        self.got1, self.got3, self.got2 = got1, got3, got2
        self.got_half, self.got_quad, self.got_whole = got_dp[0], got_dp[1], got_dp[2:]
        self.send, self.recv = send, recv
        bits = powers("dp")
        self.bits, self.four, self.rest = bits[0], bits[1:3], bits[3:]
        self.half, self.quarter = UNIT // 2, UNIT // 8
        self.base = bit_of("dp", self.bits) * self.half
        self.offset = self.base + quad_peer(self.four, 0)[1] * self.quarter
        self.ticks = self.units + 7 + len(self.rest)

    def rows(self, u, size, offset=0):
        return pl.ds(pl.multiple_of(u * UNIT + offset, TILE), size)

    def slot(self, u, size):
        return pl.ds(pl.multiple_of((u % SLOTS) * size, TILE), size)

    def copy(self, stage, u, source, target, peer):
        return remote(source, target, self.send.at[stage, u], self.recv.at[stage, u], peer)

    def first(self, u):
        at, here, peer = self.rows(u, UNIT), self.slot(u, UNIT), flip("mp", 1)
        return (
            self.copy(0, u, self.near.at[at], self.got1.at[here], peer),
            self.copy(1, u, self.far.at[at], self.got3.at[here], peer),
        )

    def second(self, u):
        return self.copy(2, u, self.cross.at[self.rows(u, UNIT)], self.got2.at[self.slot(u, UNIT)], flip("mp", 2))

    def halve(self, u):
        source = self.keep.at[self.rows(u, self.half, self.half - self.base)]
        return self.copy(3, u, source, self.got_half.at[self.slot(u, self.half)], flip("dp", self.bits))

    def quads(self, u):
        copies = []
        for step in range(1, 4):
            peer, place = quad_peer(self.four, step)
            source = self.keep.at[self.rows(u, self.quarter, self.base + place * self.quarter)]
            target = self.got_quad.at[step - 1, self.slot(u, self.quarter)]
            copies.append(self.copy(3 + step, u, source, target, peer))
        return copies

    def whole(self, u, k):
        source = self.keep.at[self.rows(u, self.quarter, self.offset)]
        return self.copy(7 + k, u, source, self.got_whole[k].at[self.slot(u, self.quarter)], flip("dp", self.rest[k]))

    def quads_back(self, u):
        part = self.total.at[self.rows(u, self.quarter, self.offset)]
        first = 6 + len(self.rest)
        return [self.copy(first + step, u, part, part, quad_peer(self.four, step)[0]) for step in range(1, 4)]

    def half_back(self, u):
        part = self.total.at[self.rows(u, self.half, self.base)]
        return self.copy(10 + len(self.rest), u, part, part, flip("dp", self.bits))

    def add(self, source, target, u, size, offset, terms):
        def tile(i, carry):
            at = pl.ds(pl.multiple_of(u * UNIT + offset + i * TILE, TILE), TILE)
            value = source[at].astype(F32)
            for ref in terms:
                value += ref[pl.ds(pl.multiple_of((u % SLOTS) * size + i * TILE, TILE), TILE)].astype(F32)
            target[at] = value.astype(BF)
            return carry

        lax.fori_loop(0, size // TILE, tile, 0, unroll=True)

    def tick(self, t):
        rest = len(self.rest)

        def at(lag, body):
            u = t - lag

            @pl.when((u >= 0) & (u < self.units))
            def _():
                body(u)

        def each(copies, begin):
            for copy in copies:
                if begin:
                    copy.start()
                else:
                    copy.wait()

        def start_first(u):
            each(self.first(u), True)

        def after_first(u):
            each(self.first(u), False)
            self.add(self.cross, self.cross, u, UNIT, 0, [self.got3])
            self.second(u).start()

        def after_second(u):
            self.second(u).wait()
            self.add(self.keep, self.keep, u, UNIT, 0, [self.got1, self.got2])
            self.halve(u).start()

        def after_half(u):
            self.halve(u).wait()
            self.add(self.keep, self.keep, u, self.half, self.base, [self.got_half])
            each(self.quads(u), True)

        def after_quads(u):
            each(self.quads(u), False)
            terms = [self.got_quad.at[n] for n in range(3)]
            self.add(self.keep, self.keep if rest else self.total, u, self.quarter, self.offset, terms)
            each([self.whole(u, 0)] if rest else self.quads_back(u), True)

        def after_whole(k):
            def body(u):
                self.whole(u, k).wait()
                last = k == rest - 1
                target = self.total if last else self.keep
                self.add(self.keep, target, u, self.quarter, self.offset, [self.got_whole[k]])
                each(self.quads_back(u) if last else [self.whole(u, k + 1)], True)

            return body

        def after_quads_back(u):
            each(self.quads_back(u), False)
            self.half_back(u).start()

        def after_half_back(u):
            self.half_back(u).wait()

        at(0, start_first)
        at(1, after_first)
        at(3, after_second)
        at(4, after_half)
        at(5, after_quads)
        for k in range(rest):
            at(6 + k, after_whole(k))
        at(6 + rest, after_quads_back)
        at(7 + rest, after_half_back)


class SmallSum:
    def __init__(self, value, got, send, recv):
        self.value, self.got, self.send, self.recv = value, got, send, recv
        self.peers = [flip("mp", b) for b in BITS_MP] + [flip("dp", b) for b in powers("dp")]

    def copy(self, k):
        return remote(self.value, self.got.at[k], self.send.at[k], self.recv.at[k], self.peers[k])

    def finish(self, k):
        self.copy(k).wait()
        value, got = self.value, self.got
        value[:8] += got[k, :8]
        if k == 0:
            value[8:10] += got[k, 10:12]
            value[12:14] += got[k, 14:16]
        elif k == 1:
            value[8:10] += got[k, 12:14]
        else:
            value[8:10] += got[k, 8:10]


def layer_body(
    heads,
    rows,
    tokens_in,
    gain1_in,
    bias1_in,
    gain2_in,
    bias2_in,
    bias_out_in,
    bias_down_in,
    positions_in,
    keep_mask_in,
    bias_qkv_in,
    freqs_in,
    bias_up_in,
    group,
    cot,
    s_qkv,
    s_out,
    s_up,
    s_down,
    out,
    gx,
    o_up,
    o_down,
    o_out,
    o_qkv,
    small_sum,
    factor_out,
    tokens,
    gain1,
    bias1,
    gain2,
    bias2,
    bias_out,
    bias_down,
    positions,
    keep_mask,
    bias_qkv,
    freqs,
    bias_up,
    all_w,
    small,
    place,
    q_all,
    k_all,
    v_all,
    lse,
    att,
    cosine,
    sine,
    normed1,
    middle,
    branch,
    g,
    mlp,
    gsecond,
    active,
    slope,
    vec,
    keep_col,
    feats,
    sums_up,
    sums_vec,
    column,
    head_sums,
    grads,
    got1,
    got3,
    got2,
    got_small,
    send_g,
    recv_g,
    send_s,
    recv_s,
    local_sem,
    send,
    recv,
    send_v,
    recv_v,
    *got_dp,
):
    parts, count = all_w.shape[0], q_all.shape[0]
    local = heads * HD
    width = tokens.shape[1]
    wide = q_all.shape[2]
    top = 4 * local
    units = (all_w.shape[1] - top) // 2
    mlp_rows = 2 * width
    up_rows, down_rows = pl.ds(top, width), pl.ds(top + width, units)
    loads, start = [], 0
    for n, ref in enumerate((s_qkv, s_out, s_up, s_down)):
        loads.append(pltpu.make_async_copy(ref, all_w.at[0, pl.ds(start, ref.shape[0])], local_sem.at[n]))
        start += ref.shape[0]
    load_cot = pltpu.make_async_copy(cot, slope, local_sem.at[5])
    early = []
    for n, (source, target) in enumerate(
        (
            (bias_up_in, bias_up),
            (bias_qkv_in, bias_qkv),
            (freqs_in, freqs),
            (tokens_in, tokens),
            (gain1_in, gain1),
            (bias1_in, bias1),
            (gain2_in, gain2),
            (bias2_in, bias2),
            (bias_out_in, bias_out),
            (bias_down_in, bias_down),
            (positions_in, positions),
            (keep_mask_in, keep_mask),
        )
    ):
        early.append(pltpu.make_async_copy(source, target, local_sem.at[12 + n]))
    for load in early[:3] + loads + early[3:]:
        load.start()
    for load in early[:3]:
        load.wait()
    small[0] = jnp.zeros_like(small[0])
    small[0, 0:1] = bias_up[...].reshape(1, units).astype(F32)
    row = [bias_qkv[n : n + 1] for n in range(3)] + [freqs[h, n : n + 1] for n in range(2) for h in range(heads)]
    small[0, 1:2] = jnp.concatenate(row, axis=1)
    both = {"mp": lax.axis_index("mp") + 1 * (1 - 2 * bit_of("mp", 1)) + 2 * (1 - 2 * bit_of("mp", 2))}
    sums = SmallSum(small_sum, got_small, send_v, recv_v)
    greet(sums.peers + [both])
    peers = [flip("mp", 1), flip("mp", 2), both]
    smalls = [
        remote(small.at[0], small.at[r], send_s.at[r - 1], recv_s.at[r - 1], peers[r - 1]) for r in range(1, 4)
    ]
    for copy in smalls:
        copy.start()
    weights = Gather(all_w, send_g, recv_g)
    for load in loads + early[3:]:
        load.wait()
    for u in range(DEPTH):
        weights.across(u).start()
    own_pieces = all_w.shape[1] // PIECE
    weights.owns(0, own_pieces, True)
    load_cot.start()
    for n, ref in enumerate((gain1, bias1, gain2, bias2, bias_out, bias_down)):
        vec[n : n + 1] = ref[...].reshape(1, width)
    first_norm(tokens, vec, normed1)
    own_part = lax.axis_index("mp")
    spot = jnp.concatenate([positions[...], keep_mask[...].reshape(1, keep_mask.shape[0])])
    mine = spot[:, :rows]
    for n in range(1, parts):
        mine = jnp.where(own_part == n, spot[:, n * rows : (n + 1) * rows], mine)
    place[...] = jnp.zeros_like(place)
    place[0:3, :rows] = mine.astype(F32)
    masks(rows, place, group, feats, keep_col)
    for copy in smalls:
        copy.wait()
    proj = mlp.at[: 3 * local, :wide]

    first_rows = 3 * local // PIECE
    for r in range(parts):
        if r < 2:
            turns(r, heads, small, place, cosine, sine)
        if r == 2:
            for n in range(2):
                weights.at("p", parts, n)
                turns(r + n, heads, small, place, cosine, sine)
            load_cot.wait()
            g[...] = (slope[...] * keep_col[...]).astype(BF)
            gsecond[...] = jnp.zeros_like(gsecond)
        weights.at("p", r, 0)
        if r == 1:
            weights.owns(0, first_rows, False)
        attend_chunk(
            r, heads, rows, normed1, all_w, functools.partial(weights.at, "p", r), small, place, feats,
            q_all, k_all, v_all, lse, att, cosine, sine, proj,
        )
    weights.owns(first_rows, own_pieces, False)
    weights.at("w", 0, 0)
    wo = jnp.concatenate([all_w[r, 3 * local : top] for r in range(parts)])
    normed2 = branch.at[:rows]
    second_norm(rows, tokens, vec, att, wo, middle, normed2)
    mlp[...] = jnp.zeros_like(mlp)

    net = Reducer(grads, got1, got3, got2, got_dp, send, recv)

    def between(r, n):
        for k in range(parts):
            if ("f", k, n + 1) in PLAN:
                pl.when(r == k)(functools.partial(weights.at, "f", k, n + 1))
        if n > 0:
            @pl.when(r == parts - 1)
            def _():
                net.tick(n - 1)

    def mlp_step(r, carry):
        mlp_chunk(
            r, normed2, g, all_w.at[r, up_rows], all_w.at[r, down_rows], small, mlp, gsecond,
            grads.at[r, pl.ds(0, mlp_rows)], sums_up, active, slope, functools.partial(between, r),
        )
        return carry

    lax.fori_loop(0, parts, mlp_step, 0)
    load_cot.start()

    def step(t, carry):
        net.tick(t)
        return carry

    def ticks(start, stop):
        lax.fori_loop(start, stop, step, 0)

    load_cot.wait()
    finish_mlp(slope, keep_col, vec, middle, mlp, gsecond, g, active, branch, sums_vec)
    store_out = pltpu.make_async_copy(active, out, local_sem.at[6])
    store_out.start()
    ticks(3, 4)
    gatt = all_w.at[0, down_rows, :wide]
    gqkv = all_w.at[:, pl.ds(top, 3 * local), :wide]
    wo = jnp.concatenate([all_w[r, 3 * local : top] for r in range(parts)])
    gatt[...] = nt(wo, branch[...]).astype(BF)

    per = 2

    def some_heads(i, carry):
        net.tick(4 + i)

        def head(n, c):
            attend_back(per * i + n, heads, rows, q_all, k_all, v_all, lse, att, gatt, cosine, sine, place, gqkv, column, head_sums)
            return c

        return lax.fori_loop(0, per, head, carry)

    lax.fori_loop(0, count // per, some_heads, 0)
    base = 4 + count // per
    assert count % per == 0 and base + parts // 2 <= mlp_rows // UNIT
    gsecond[...] = jnp.zeros_like(gsecond)

    def late(r, carry):
        pl.when(r % 2 == 0)(lambda: net.tick(base + r // 2))
        here = att[pl.ds(pl.multiple_of(r * local, HD), local)]
        grads[r, mlp_rows : mlp_rows + local] = nn(here, branch[...]).astype(BF)
        grads[r, mlp_rows + local :] = nn(gqkv[r], normed1[...]).astype(BF)
        gsecond[...] += tn(gqkv[r], all_w[r, : 3 * local])[:rows]
        return carry

    lax.fori_loop(0, parts, late, 0)
    base = base + parts // 2
    ticks(base, base + 1)
    grad = gsecond[...]
    unit, scale = unit_of(tokens[...].astype(F32))
    gsecond[...] = middle[...] + norm_back(grad, unit, scale, vec[0:1])
    store_gx = pltpu.make_async_copy(gsecond, gx, local_sem.at[7])
    store_gx.start()
    small_sum[...] = jnp.zeros_like(small_sum)
    small_sum[0:1] = jnp.sum(grad * unit, axis=0, keepdims=True)
    small_sum[1:2] = jnp.sum(grad, axis=0, keepdims=True)
    small_sum[2:7] = sums_vec[0:5]
    for r in range(parts):
        small_sum[8 + 2 * r : 9 + 2 * r] = sums_up[r]
        mine = [head_sums[r * heads + h : r * heads + h + 1] for h in range(heads)]
        pieces = [v[:, n * HD : (n + 1) * HD] for n in range(3) for v in mine]
        pieces += [v[:, 3 * HD + n * HALF : 3 * HD + (n + 1) * HALF] for n in range(2) for v in mine]
        small_sum[9 + 2 * r : 10 + 2 * r] = jnp.concatenate(pieces, axis=1)
    base = base + 1
    exchanges = len(sums.peers)

    def step_small(t, carry):
        net.tick(t)
        for k in range(exchanges + 1):
            @pl.when(t == base + k)
            def _():
                if k > 0:
                    sums.finish(k - 1)
                if k == exchanges:
                    factor = lax.axis_size("dp") / small_sum[6:7]
                    factor_out[0] = factor[0, 0]
                    small_sum[...] *= factor
                if k < exchanges:
                    sums.copy(k).start()
        return carry

    lax.fori_loop(base, base + exchanges + 1, step_small, 0)
    stores = []
    start = 0
    for n, ref in enumerate((o_down, o_up, o_out, o_qkv)):
        if n == 2:
            ticks(base + exchanges + 1, max(net.ticks, base + exchanges + 1))
        stores.append(pltpu.make_async_copy(grads.at[1, pl.ds(start, ref.shape[0])], ref, local_sem.at[8 + n]))
        stores[-1].start()
        start += ref.shape[0]
    for copy in stores + [store_out, store_gx]:
        copy.wait()


def finish_body(vectors, local, up, down, out, qkv, small, factor, middle, gx, *rest):
    shared = len(vectors) + 2
    results, rest = rest[: 6 + shared], rest[6 + shared :]
    low, full, copies = rest[:6], rest[6:10], rest[10]
    sources = (up, down, out, qkv, middle, gx)
    targets = results[:4] + results[4 + shared :]
    loads = [pltpu.make_async_copy(a, b, copies.at[0, n]) for n, (a, b) in enumerate(zip(sources, low))]
    ready = full + low[4:]
    stores = [pltpu.make_async_copy(a, b, copies.at[1, n]) for n, (a, b) in enumerate(zip(ready, targets))]
    order = (3, 2, 0, 1, 5, 4)
    for n in order:
        loads[n].start()
    for n, row in enumerate(vectors):
        results[4 + n][...] = small[row : row + 1].reshape(small.shape[1])
    b_qkv, freqs = results[4 + len(vectors)], results[5 + len(vectors)]
    for n in range(3):
        b_qkv[n : n + 1] = small[9:10, n * local : (n + 1) * local]
    for n in range(2):
        for h in range(freqs.shape[0]):
            start = 3 * local + (n * freqs.shape[0] + h) * HALF
            freqs[h, n : n + 1] = small[9:10, start : start + HALF]
    for n in order:
        loads[n].wait()
        if n < 4:
            full[n][...] = low[n][...].astype(F32) * factor[0]
        stores[n].start()
    for n in order:
        stores[n].wait()


def sds(shape, dtype):
    return jax.ShapeDtypeStruct(shape, dtype)


def body(
    tokens,
    image_group,
    positions,
    keep_mask,
    norm1_gain,
    norm1_bias,
    w_qkv,
    b_qkv,
    rotary_freqs,
    w_out,
    b_out,
    norm2_gain,
    norm2_bias,
    w_up,
    b_up,
    w_down,
    b_down,
    cotangent,
):
    rows, width = tokens.shape
    wide = -(-rows // LANES) * LANES
    parts = lax.axis_size("mp")
    mp_index = lax.axis_index("mp")
    heads = rotary_freqs.shape[1]
    local = heads * HD
    units = w_up.shape[1]
    w_qkv_t = w_qkv.reshape(width, 3 * local).T
    count = parts * heads
    bits = powers("dp")
    sizes = steps_of(bits)
    stages = 8 + len(bits)
    total_rows = 2 * width + 4 * local
    unit_count = total_rows // UNIT
    pieces = max(total_rows // PIECE, len(SIZES))
    swaps = 2 + len(bits)
    in_vmem = pl.BlockSpec(memory_space=pltpu.VMEM)
    in_smem = pl.BlockSpec(memory_space=pltpu.SMEM)
    anywhere = pl.BlockSpec(memory_space=pl.ANY)
    dma = pltpu.SemaphoreType.DMA
    vmem = pltpu.VMEM
    out, gx, o_up, o_down, o_out, o_qkv, small_sum, factor = pl.pallas_call(
        functools.partial(layer_body, heads, rows),
        out_shape=[
            sds((rows, width), BF),
            sds((rows, width), F32),
            sds((width, units), BF),
            sds((units, width), BF),
            sds((local, width), BF),
            sds((3 * local, width), BF),
            sds((16, width), F32),
            sds((1,), F32),
        ],
        in_specs=[anywhere] * 12 + [in_smem] + [anywhere] * 5,
        out_specs=[anywhere] * 6 + [in_vmem, in_smem],
        scratch_shapes=[
            vmem(tokens.shape, BF),
        ]
        + [vmem((width,), F32)] * 6
        + [
            vmem(positions.shape, jnp.int32),
            vmem(keep_mask.shape, jnp.int32),
            vmem(b_qkv.shape, F32),
            vmem((heads, 2, HALF), F32),
            vmem(b_up.shape, BF),
            vmem((parts, total_rows, width), BF),
            vmem((parts, 8, width), F32),
            vmem((8, wide), F32),
            vmem((count, AUG, wide), BF),
            vmem((count, AUG, wide), BF),
            vmem((count, AUG, wide), BF),
            vmem((count, 8, wide), F32),
            vmem((count * HD, wide), BF),
            vmem((parts, heads * HALF, wide), F32),
            vmem((parts, heads * HALF, wide), F32),
            vmem((wide, width), BF),
            vmem((rows, width), F32),
            vmem((wide, width), BF),
            vmem((rows, width), BF),
            vmem((rows, width), F32),
            vmem((rows, width), F32),
            vmem((rows, units), BF),
            vmem((rows, units), F32),
            vmem((8, width), F32),
            vmem((rows, 1), F32),
            vmem((3, 16, wide), BF),
            vmem((parts, 1, units), F32),
            vmem((8, width), F32),
            vmem((3 * HD + 2 * HALF, LANES), F32),
            vmem((-(-count // 8) * 8, 3 * HD + 2 * HALF), F32),
            vmem((parts, total_rows, width), BF),
            vmem((SLOTS * UNIT, width), BF),
            vmem((SLOTS * UNIT, width), BF),
            vmem((SLOTS * UNIT, width), BF),
            vmem((swaps, 16, width), F32),
            dma((5, pieces)),
            dma((5, pieces)),
            dma((3,)),
            dma((3,)),
            dma((24,)),
            dma((stages, unit_count)),
            dma((stages, unit_count)),
            dma((swaps,)),
            dma((swaps,)),
        ]
        + [vmem((SLOTS * UNIT // 2, width), BF), vmem((3, SLOTS * UNIT // 8, width), BF)]
        + [vmem((SLOTS * size, width), BF) for size in sizes[2:]],
        compiler_params=pltpu.CompilerParams(vmem_limit_bytes=61 << 20, collective_id=0, has_side_effects=True),
    )(tokens, norm1_gain, norm1_bias, norm2_gain, norm2_bias, b_out, b_down, positions, keep_mask, b_qkv,
      rotary_freqs.transpose(1, 0, 2), b_up, image_group, cotangent, w_qkv_t, w_out, w_up, w_down)
    sums = (o_up, o_down, o_out, o_qkv)
    vectors = [0, 1, 2, 3, 4, 5, 8]
    finished = pl.pallas_call(
        functools.partial(finish_body, vectors, local),
        out_shape=[sds(ref.shape, F32) for ref in sums]
        + [sds((width,), F32)] * len(vectors)
        + [sds((3, local), F32), sds((heads, 2, HALF), F32), sds(out.shape, BF), sds(gx.shape, F32)],
        in_specs=[anywhere] * 4 + [in_vmem, in_smem, anywhere, anywhere],
        out_specs=[anywhere] * 4 + [in_vmem] * (len(vectors) + 2) + [anywhere] * 2,
        scratch_shapes=[vmem(ref.shape, BF) for ref in sums]
        + [vmem(out.shape, BF), vmem(gx.shape, F32)]
        + [vmem(ref.shape, F32) for ref in sums]
        + [dma((2, 6))],
        compiler_params=pltpu.CompilerParams(vmem_limit_bytes=60 << 20),
    )(*sums, small_sum, factor, out, gx)
    sum_w_up, sum_w_down, sum_w_out, sum_w_qkv, gain1, bias1, b_out_sum, gain2, bias2, b_down_sum, b_up_sum = finished[:11]
    b_qkv_sum, freqs_sum, out, gx = finished[11:]
    return (
        out,
        gx,
        gain1,
        bias1,
        sum_w_qkv.T.reshape(w_qkv.shape),
        b_qkv_sum,
        freqs_sum.transpose(1, 0, 2),
        sum_w_out,
        b_out_sum,
        gain2,
        bias2,
        sum_w_up,
        b_up_sum,
        sum_w_down,
        b_down_sum,
    )


def solution(mesh):
    placed = (
        P(("dp", "mp"), None),
        P("dp"),
        P(None, "dp"),
        P("dp"),
        P(),
        P(),
        P(None, None, "mp"),
        P(None, "mp"),
        P(None, "mp", None),
        P("mp", None),
        P(),
        P(),
        P(),
        P(None, "mp"),
        P("mp"),
        P("mp", None),
        P(),
        P(("dp", "mp"), None),
    )
    return jax.shard_map(
        body,
        mesh=mesh,
        in_specs=placed,
        out_specs=(
            P(("dp", "mp"), None),
            P(("dp", "mp"), None),
            P(),
            P(),
            P(None, None, "mp"),
            P(None, "mp"),
            P(None, "mp", None),
            P("mp", None),
            P(),
            P(),
            P(),
            P(None, "mp"),
            P("mp"),
            P("mp", None),
            P(),
        ),
        check_vma=False,
    )
```

```python
import math
import functools

import jax
import jax.numpy as jnp
from jax import lax
from jax.experimental import pallas as pl
from jax.experimental.pallas import tpu as pltpu
from jax.sharding import PartitionSpec as P

HD = 64
SIDE_SMALL = 14
SIDE_LARGE = 24
IMG_SMALL = 3
IMG_LARGE = 1
NORM_EPS = 1e-06
HIDE = -1e30
BF = jnp.bfloat16
F32 = jnp.float32
SCALE = 1.0 / math.sqrt(HD)
HALF = HD // 2
LANES = 128
AUG = HD + 16


def nn(a, b):
    return jnp.dot(a, b, preferred_element_type=F32)


def tn(a, b):
    return lax.dot_general(a, b, (((0,), (0,)), ((), ())), preferred_element_type=F32)


def nt(a, b):
    return lax.dot_general(a, b, (((1,), (1,)), ((), ())), preferred_element_type=F32)


def unit_of(values):
    mean = jnp.mean(values, axis=-1, keepdims=True)
    centered = values - mean
    variance = jnp.mean(centered * centered, axis=-1, keepdims=True)
    scale = lax.rsqrt(variance + NORM_EPS)
    return centered * scale, scale


def norm_back(grad, unit, scale, gain):
    u = grad * gain
    mean_u = jnp.mean(u, axis=-1, keepdims=True)
    mean_un = jnp.mean(u * unit, axis=-1, keepdims=True)
    return scale * (u - mean_u - unit * mean_un)


def gelu_both(v):
    cdf = 0.5 * (1.0 + lax.erf(v * (1.0 / math.sqrt(2.0))))
    pdf = jnp.exp(-0.5 * v * v) * (1.0 / math.sqrt(2.0 * math.pi))
    return v * cdf, cdf + v * pdf


def pad_rows(value, rows):
    return jnp.concatenate(
        [value, jnp.zeros((rows - value.shape[0],) + value.shape[1:], value.dtype)]
    )


def first_norm(tokens, vec, normed1):
    unit, _ = unit_of(tokens[...].astype(F32))
    normed = (unit * vec[0:1] + vec[1:2]).astype(BF)
    normed1[...] = pad_rows(normed, normed1.shape[0])


def masks(rows, place, group, feats, keep):
    wide = place.shape[1]
    slot = lax.broadcasted_iota(jnp.int32, (16, wide), 1)
    row = lax.broadcasted_iota(jnp.int32, (16, wide), 0)
    image_id = jnp.zeros((16, wide), jnp.int32)
    for is_large, side, images in ((0, SIDE_SMALL, IMG_SMALL), (1, SIDE_LARGE, IMG_LARGE)):
        mine = sum([(slot >= n * side * side).astype(jnp.int32) for n in range(1, images)], jnp.zeros((16, wide), jnp.int32))
        image_id = jnp.where(group[0] == is_large, mine, image_id)
    same = (image_id == row) & (row < max(IMG_SMALL, IMG_LARGE))
    hidden = jnp.logical_not(same & (place[2:3] > 0.5)) & (row < max(IMG_SMALL, IMG_LARGE))
    feats[0] = jnp.where(same, 1.0, 0.0).astype(BF)
    feats[1] = jnp.where(hidden, HIDE, 0.0).astype(BF)
    feats[2] = jnp.where(row == 0, 1.0, 0.0).astype(BF)
    keep[...] = place[...].T[:rows, 2:3]


def turns(r, heads, small, place, cosine, sine):
    start = 3 * heads * HD
    column = small[r].T[:, 1:2]
    f0 = column[start : start + heads * HALF]
    f1 = column[start + heads * HALF : start + 2 * heads * HALF]
    angles = f0 * place[0:1] + f1 * place[1:2]
    cosine[r] = jnp.cos(angles)
    sine[r] = jnp.sin(angles)


def attend_chunk(r, heads, rows, normed1, weights, hook, small, place, feats, q_all, k_all, v_all, lse, att, cosine, sine, proj):
    local = heads * HD
    column = small[r].T[:, 1:2]
    proj[...] = nt(weights[r, : 3 * local], normed1[...]) + column[: 3 * local]
    hook(1)
    for h in range(heads):
        cos_h = cosine[r, h * HALF : (h + 1) * HALF]
        sin_h = sine[r, h * HALF : (h + 1) * HALF]
        at = r * heads + h
        for base, ref, scale in ((0, q_all, SCALE), (local, k_all, 1.0)):
            a = proj[base + h * HD : base + h * HD + HALF]
            b = proj[base + h * HD + HALF : base + (h + 1) * HD]
            ref[at, :HALF] = ((a * cos_h - b * sin_h) * scale).astype(BF)
            ref[at, HALF:HD] = ((b * cos_h + a * sin_h) * scale).astype(BF)
        v_all[at, :HD] = proj[2 * local + h * HD : 2 * local + (h + 1) * HD].astype(BF)
        q_all[at, HD:] = feats[0]
        k_all[at, HD:] = feats[1]
        v_all[at, HD:] = feats[2]

    def head(h, carry):
        at = r * heads + h
        scores = tn(k_all[at, :, :rows], q_all[at])
        top = jnp.max(scores, axis=0, keepdims=True)
        terms = jnp.exp(scores - top).astype(BF)
        mixed = nn(v_all[at, :, :rows], terms)
        total = mixed[HD : HD + 1]
        att[pl.ds(pl.multiple_of(at * HD, HD), HD)] = (mixed[:HD] * (1.0 / total)).astype(BF)
        lse[at] = jnp.broadcast_to(top + jnp.log(total), lse.shape[1:])
        for n in range(heads - 1):
            pl.when(h == n)(functools.partial(hook, 2 + n))
        return carry

    lax.fori_loop(0, heads, head, 0)


def second_norm(rows, tokens, vec, att, wo, middle, normed2):
    branch = tn(att[...], wo)
    middle[...] = tokens[...].astype(F32) + branch[:rows] + vec[4:5]
    unit, _ = unit_of(middle[...])
    normed2[...] = (unit * vec[2:3] + vec[3:4]).astype(BF)


def mlp_chunk(r, normed2, g, wu, wd, small, mlp, gsecond, target, sums, active, slope, hook):
    width = normed2.shape[1]
    hook(-1)
    hidden = nn(normed2[...], wu[...]) + small[r][0:1]
    act, der = gelu_both(hidden)
    active[...] = act.astype(BF)
    slope[...] = der
    hook(0)
    target[: active.shape[1]] = tn(active[...], g[...]).astype(BF)
    hook(1)
    mlp[...] += nn(active[...], wd[...])
    gh = nt(g[...], wd[...]) * slope[...]
    active[...] = gh.astype(BF)
    sums[r] = jnp.sum(active[...].astype(F32), axis=0, keepdims=True)
    hook(2)
    target[active.shape[1] :] = tn(normed2[...], active[...]).astype(BF)
    hook(3)
    gsecond[...] += nt(active[...], wu[...])


def finish_mlp(cot, keep, vec, middle, mlp, gsecond, g, out, branch, sums_vec):
    out[...] = (middle[...] + mlp[...] + vec[5:6]).astype(BF)
    unit, scale = unit_of(middle[...])
    grad = gsecond[...]
    gm = cot[...] * keep[...] + norm_back(grad, unit, scale, vec[2:3])
    low = gm.astype(BF)
    sums_vec[...] = jnp.concatenate(
        [
            jnp.sum(low.astype(F32), axis=0, keepdims=True),
            jnp.sum(grad * unit, axis=0, keepdims=True),
            jnp.sum(grad, axis=0, keepdims=True),
            jnp.sum(g[...].astype(F32), axis=0, keepdims=True),
            jnp.full((4, grad.shape[1]), 1.0, F32) * jnp.sum(keep[...]),
        ]
    )
    middle[...] = gm
    branch[...] = pad_rows(low, branch.shape[0])


def attend_back(at, heads, rows, q_all, k_all, v_all, lse, att, gatt, cosine, sine, place, gqkv, column, sums):
    local = heads * HD
    r, h = at // heads, at % heads
    here = pl.ds(pl.multiple_of(at * HD, HD), HD)
    wide = q_all.shape[2]
    scores = tn(k_all[at, :, :rows], q_all[at])
    probs = jnp.exp(scores - lse[at, 0:1])
    go = gatt[here]
    inner = jnp.sum(go.astype(F32) * att[here].astype(F32), axis=0, keepdims=True)
    gp = tn(v_all[at, :HD, :rows], go)
    gs = (probs * (gp - inner)).astype(BF)
    gv = nt(go, probs.astype(BF))
    gk = nt(q_all[at, :HD], gs)
    gq = nn(k_all[at, :HD, :rows], gs) * SCALE
    hs = pl.ds(pl.multiple_of(h * HALF, HALF), HALF)
    cos_h, sin_h = cosine[r, hs], sine[r, hs]
    term = jnp.zeros((HALF, wide), F32)
    pad = jnp.zeros((HD, wide - rows), F32)
    gk = jnp.concatenate([gk, pad], axis=1)
    gv = jnp.concatenate([gv, pad], axis=1)
    lows = []
    for ref, grad, back in ((q_all, gq, 1.0 / SCALE), (k_all, gk, 1.0)):
        a, b = grad[:HALF], grad[HALF:]
        ra = ref[at, :HALF].astype(F32)
        rb = ref[at, HALF:HD].astype(F32)
        term += (b * ra - a * rb) * back
        lows.append(jnp.concatenate([a * cos_h + b * sin_h, b * cos_h - a * sin_h], axis=0).astype(BF))
    lows.append(gv.astype(BF))
    for n, low in enumerate(lows):
        gqkv[r, pl.ds(pl.multiple_of(n * local + h * HD, HD), HD)] = low
        total = jnp.sum(low.astype(F32), axis=1, keepdims=True)
        column[n * HD : (n + 1) * HD] = jnp.broadcast_to(total, (HD, LANES))
    for n in range(2):
        total = jnp.sum(term * place[n : n + 1], axis=1, keepdims=True)
        column[3 * HD + n * HALF : 3 * HD + (n + 1) * HALF] = jnp.broadcast_to(total, (HALF, LANES))
    sums[pl.ds(at, 1)] = column[...].T[0:1]


UNIT = 128
PIECE = 192
DEPTH = 3
SIZES = (192, 192, 192, 192, 192, 192, 192, 192, 192, 192, 192, 192)
PLAN = {
    ('p', 0, 2): (('a', 0),),
    ('p', 1, 1): (('a', 1),),
    ('p', 1, 3): (('a', 2), ('b', 0)),
    ('p', 4, 0): (('d', 0),),
    ('p', 4, 1): (('a', 3),),
    ('p', 2, 0): (('b', 1), ('d', 1), ('a', 4), ('b', 2)),
    ('p', 2, 1): (('d', 2),),
    ('p', 2, 3): (('b', 3), ('a', 5)),
    ('p', 3, 0): (('d', 3),),
    ('p', 3, 2): (('b', 4), ('a', 6)),
    ('p', 3, 3): (('d', 4),),
    ('f', 0, 0): (('a', 7), ('b', 5)),
    ('f', 0, 1): (('a', 8), ('d', 5), ('b', 6)),
    ('f', 0, 2): (('d', 6),),
    ('f', 0, 3): (('a', 9),),
    ('f', 0, 4): (('b', 7),),
    ('f', 1, 0): (('a', 10), ('d', 7)),
    ('f', 1, 1): (('b', 8),),
    ('f', 1, 2): (('a', 11), ('d', 8)),
    ('f', 1, 3): (('b', 9),),
    ('f', 1, 4): (('b', 10), ('d', 9)),
    ('f', 2, 0): (('d', 10), ('b', 11)),
    ('f', 2, 1): (('d', 11),),
}
SLOTS = 6
TILE = 16
BITS_MP = (1, 2)


def flip(axis, bit):
    me = lax.axis_index(axis)
    return {axis: me + bit * (1 - 2 * ((me // bit) % 2))}


def bit_of(axis, bit):
    return (lax.axis_index(axis) // bit) % 2


def powers(axis):
    size = lax.axis_size(axis)
    return [1 << k for k in range(size.bit_length() - 1)]


def greet(peers):
    barrier = pltpu.get_barrier_semaphore()
    for peer in peers:
        pl.semaphore_signal(barrier, inc=1, device_id=peer, device_id_type=pl.DeviceIdType.MESH)
    pl.semaphore_wait(barrier, len(peers))


def remote(src, dst, send, recv, peer):
    return pltpu.make_async_remote_copy(
        src_ref=src, dst_ref=dst, send_sem=send, recv_sem=recv, device_id=peer, device_id_type=pl.DeviceIdType.MESH
    )


def steps_of(bits):
    return [UNIT // 2, UNIT // 8] + [UNIT // 8] * (len(bits) - 3)


def quad_peer(bits, step):
    one, two = bit_of("dp", bits[0]), bit_of("dp", bits[1])
    other_one = 1 - one if step & 1 else one
    other_two = 1 - two if step & 2 else two
    me = lax.axis_index("dp")
    return {"dp": me + bits[0] * (other_one - one) + bits[1] * (other_two - two)}, other_one + 2 * other_two


class Gather:
    def __init__(self, weights, send, recv):
        self.weights, self.send, self.recv = weights, send, recv
        self.pieces = len(SIZES)
        assert sum(SIZES) == weights.shape[1]

    def rows(self, u, mine):
        start, half = sum(SIZES[:u]), SIZES[u] // 2
        upper = bit_of("dp", 1 + u % 2)
        return pl.ds(pl.multiple_of(start + (upper if mine else 1 - upper) * half, TILE), half)

    def copy(self, stage, u, source, target, rows, peer):
        return remote(
            self.weights.at[source, rows],
            self.weights.at[target, rows],
            self.send.at[stage, u],
            self.recv.at[stage, u],
            peer,
        )

    def own(self, u):
        return self.copy(0, u, 0, 1, pl.ds(pl.multiple_of(u * PIECE, TILE), PIECE), flip("mp", 1))

    def across(self, u):
        return self.copy(1, u, 0, 2, self.rows(u, True), flip("mp", 2))

    def beside(self, u):
        return self.copy(2, u, 2, 2, self.rows(u, True), flip("dp", 1 + u % 2))

    def pass_on(self, u, n):
        return self.copy(3 + n, u, 2, 3, self.rows(u, n == 0), flip("mp", 1))

    def owns(self, start, stop, begin):
        def each(u, carry):
            if begin:
                self.own(u).start()
            else:
                self.own(u).wait()
            return carry

        lax.fori_loop(start, stop, each, 0)

    def step(self, kind, u):
        if kind == "a":
            self.across(u).wait()
            if u + DEPTH < self.pieces:
                self.across(u + DEPTH).start()
            self.beside(u).start()
            self.pass_on(u, 0).start()
        elif kind == "b":
            self.beside(u).wait()
            self.pass_on(u, 1).start()
        else:
            for n in range(2):
                self.pass_on(u, n).wait()

    def at(self, *where):
        for kind, u in PLAN.get(where, ()):
            self.step(kind, u)


class Reducer:
    def __init__(self, grads, got1, got3, got2, got_dp, send, recv):
        self.keep, self.near, self.cross, self.far = (grads.at[n] for n in range(4))
        self.total = self.near
        self.units = grads.shape[1] // UNIT
        self.got1, self.got3, self.got2 = got1, got3, got2
        self.got_half, self.got_quad, self.got_whole = got_dp[0], got_dp[1], got_dp[2:]
        self.send, self.recv = send, recv
        bits = powers("dp")
        self.bits, self.four, self.rest = bits[0], bits[1:3], bits[3:]
        self.half, self.quarter = UNIT // 2, UNIT // 8
        self.base = bit_of("dp", self.bits) * self.half
        self.offset = self.base + quad_peer(self.four, 0)[1] * self.quarter
        self.ticks = self.units + 7 + len(self.rest)

    def rows(self, u, size, offset=0):
        return pl.ds(pl.multiple_of(u * UNIT + offset, TILE), size)

    def slot(self, u, size):
        return pl.ds(pl.multiple_of((u % SLOTS) * size, TILE), size)

    def copy(self, stage, u, source, target, peer):
        return remote(source, target, self.send.at[stage, u], self.recv.at[stage, u], peer)

    def first(self, u):
        at, here, peer = self.rows(u, UNIT), self.slot(u, UNIT), flip("mp", 1)
        return (
            self.copy(0, u, self.near.at[at], self.got1.at[here], peer),
            self.copy(1, u, self.far.at[at], self.got3.at[here], peer),
        )

    def second(self, u):
        return self.copy(2, u, self.cross.at[self.rows(u, UNIT)], self.got2.at[self.slot(u, UNIT)], flip("mp", 2))

    def halve(self, u):
        source = self.keep.at[self.rows(u, self.half, self.half - self.base)]
        return self.copy(3, u, source, self.got_half.at[self.slot(u, self.half)], flip("dp", self.bits))

    def quads(self, u):
        copies = []
        for step in range(1, 4):
            peer, place = quad_peer(self.four, step)
            source = self.keep.at[self.rows(u, self.quarter, self.base + place * self.quarter)]
            target = self.got_quad.at[step - 1, self.slot(u, self.quarter)]
            copies.append(self.copy(3 + step, u, source, target, peer))
        return copies

    def whole(self, u, k):
        source = self.keep.at[self.rows(u, self.quarter, self.offset)]
        return self.copy(7 + k, u, source, self.got_whole[k].at[self.slot(u, self.quarter)], flip("dp", self.rest[k]))

    def quads_back(self, u):
        part = self.total.at[self.rows(u, self.quarter, self.offset)]
        first = 6 + len(self.rest)
        return [self.copy(first + step, u, part, part, quad_peer(self.four, step)[0]) for step in range(1, 4)]

    def half_back(self, u):
        part = self.total.at[self.rows(u, self.half, self.base)]
        return self.copy(10 + len(self.rest), u, part, part, flip("dp", self.bits))

    def add(self, source, target, u, size, offset, terms):
        def tile(i, carry):
            at = pl.ds(pl.multiple_of(u * UNIT + offset + i * TILE, TILE), TILE)
            value = source[at].astype(F32)
            for ref in terms:
                value += ref[pl.ds(pl.multiple_of((u % SLOTS) * size + i * TILE, TILE), TILE)].astype(F32)
            target[at] = value.astype(BF)
            return carry

        lax.fori_loop(0, size // TILE, tile, 0, unroll=True)

    def tick(self, t):
        rest = len(self.rest)

        def at(lag, body):
            u = t - lag

            @pl.when((u >= 0) & (u < self.units))
            def _():
                body(u)

        def each(copies, begin):
            for copy in copies:
                if begin:
                    copy.start()
                else:
                    copy.wait()

        def start_first(u):
            each(self.first(u), True)

        def after_first(u):
            each(self.first(u), False)
            self.add(self.cross, self.cross, u, UNIT, 0, [self.got3])
            self.second(u).start()

        def after_second(u):
            self.second(u).wait()
            self.add(self.keep, self.keep, u, UNIT, 0, [self.got1, self.got2])
            self.halve(u).start()

        def after_half(u):
            self.halve(u).wait()
            self.add(self.keep, self.keep, u, self.half, self.base, [self.got_half])
            each(self.quads(u), True)

        def after_quads(u):
            each(self.quads(u), False)
            terms = [self.got_quad.at[n] for n in range(3)]
            self.add(self.keep, self.keep if rest else self.total, u, self.quarter, self.offset, terms)
            each([self.whole(u, 0)] if rest else self.quads_back(u), True)

        def after_whole(k):
            def body(u):
                self.whole(u, k).wait()
                last = k == rest - 1
                target = self.total if last else self.keep
                self.add(self.keep, target, u, self.quarter, self.offset, [self.got_whole[k]])
                each(self.quads_back(u) if last else [self.whole(u, k + 1)], True)

            return body

        def after_quads_back(u):
            each(self.quads_back(u), False)
            self.half_back(u).start()

        def after_half_back(u):
            self.half_back(u).wait()

        at(0, start_first)
        at(1, after_first)
        at(3, after_second)
        at(4, after_half)
        at(5, after_quads)
        for k in range(rest):
            at(6 + k, after_whole(k))
        at(6 + rest, after_quads_back)
        at(7 + rest, after_half_back)


class SmallSum:
    def __init__(self, value, got, send, recv):
        self.value, self.got, self.send, self.recv = value, got, send, recv
        self.peers = [flip("mp", b) for b in BITS_MP] + [flip("dp", b) for b in powers("dp")]

    def copy(self, k):
        return remote(self.value, self.got.at[k], self.send.at[k], self.recv.at[k], self.peers[k])

    def finish(self, k):
        self.copy(k).wait()
        value, got = self.value, self.got
        value[:8] += got[k, :8]
        if k == 0:
            value[8:10] += got[k, 10:12]
            value[12:14] += got[k, 14:16]
        elif k == 1:
            value[8:10] += got[k, 12:14]
        else:
            value[8:10] += got[k, 8:10]


def layer_body(
    heads,
    rows,
    tokens_in,
    gain1_in,
    bias1_in,
    gain2_in,
    bias2_in,
    bias_out_in,
    bias_down_in,
    positions_in,
    keep_mask_in,
    bias_qkv_in,
    freqs_in,
    bias_up_in,
    group,
    cot,
    s_qkv,
    s_out,
    s_up,
    s_down,
    out,
    gx,
    o_up,
    o_down,
    o_out,
    o_qkv,
    small_sum,
    factor_out,
    tokens,
    gain1,
    bias1,
    gain2,
    bias2,
    bias_out,
    bias_down,
    positions,
    keep_mask,
    bias_qkv,
    freqs,
    bias_up,
    all_w,
    small,
    place,
    q_all,
    k_all,
    v_all,
    lse,
    att,
    cosine,
    sine,
    normed1,
    middle,
    branch,
    g,
    mlp,
    gsecond,
    active,
    slope,
    vec,
    keep_col,
    feats,
    sums_up,
    sums_vec,
    column,
    head_sums,
    grads,
    got1,
    got3,
    got2,
    got_small,
    send_g,
    recv_g,
    send_s,
    recv_s,
    local_sem,
    send,
    recv,
    send_v,
    recv_v,
    *got_dp,
):
    parts, count = all_w.shape[0], q_all.shape[0]
    local = heads * HD
    width = tokens.shape[1]
    wide = q_all.shape[2]
    top = 4 * local
    units = (all_w.shape[1] - top) // 2
    mlp_rows = 2 * width
    up_rows, down_rows = pl.ds(top, width), pl.ds(top + width, units)
    loads, start = [], 0
    for n, ref in enumerate((s_qkv, s_out, s_up, s_down)):
        loads.append(pltpu.make_async_copy(ref, all_w.at[0, pl.ds(start, ref.shape[0])], local_sem.at[n]))
        start += ref.shape[0]
    load_cot = pltpu.make_async_copy(cot, slope, local_sem.at[5])
    early = []
    for n, (source, target) in enumerate(
        (
            (bias_up_in, bias_up),
            (bias_qkv_in, bias_qkv),
            (freqs_in, freqs),
            (tokens_in, tokens),
            (gain1_in, gain1),
            (bias1_in, bias1),
            (gain2_in, gain2),
            (bias2_in, bias2),
            (bias_out_in, bias_out),
            (bias_down_in, bias_down),
            (positions_in, positions),
            (keep_mask_in, keep_mask),
        )
    ):
        early.append(pltpu.make_async_copy(source, target, local_sem.at[12 + n]))
    for load in early[:3] + loads + early[3:]:
        load.start()
    for load in early[:3]:
        load.wait()
    small[0] = jnp.zeros_like(small[0])
    small[0, 0:1] = bias_up[...].reshape(1, units).astype(F32)
    row = [bias_qkv[n : n + 1] for n in range(3)] + [freqs[h, n : n + 1] for n in range(2) for h in range(heads)]
    small[0, 1:2] = jnp.concatenate(row, axis=1)
    both = {"mp": lax.axis_index("mp") + 1 * (1 - 2 * bit_of("mp", 1)) + 2 * (1 - 2 * bit_of("mp", 2))}
    sums = SmallSum(small_sum, got_small, send_v, recv_v)
    greet(sums.peers + [both])
    peers = [flip("mp", 1), flip("mp", 2), both]
    smalls = [
        remote(small.at[0], small.at[r], send_s.at[r - 1], recv_s.at[r - 1], peers[r - 1]) for r in range(1, 4)
    ]
    for copy in smalls:
        copy.start()
    weights = Gather(all_w, send_g, recv_g)
    for load in loads + early[3:]:
        load.wait()
    for u in range(DEPTH):
        weights.across(u).start()
    own_pieces = all_w.shape[1] // PIECE
    weights.owns(0, own_pieces, True)
    load_cot.start()
    for n, ref in enumerate((gain1, bias1, gain2, bias2, bias_out, bias_down)):
        vec[n : n + 1] = ref[...].reshape(1, width)
    first_norm(tokens, vec, normed1)
    own_part = lax.axis_index("mp")
    spot = jnp.concatenate([positions[...], keep_mask[...].reshape(1, keep_mask.shape[0])])
    mine = spot[:, :rows]
    for n in range(1, parts):
        mine = jnp.where(own_part == n, spot[:, n * rows : (n + 1) * rows], mine)
    place[...] = jnp.zeros_like(place)
    place[0:3, :rows] = mine.astype(F32)
    masks(rows, place, group, feats, keep_col)
    for copy in smalls:
        copy.wait()
    proj = mlp.at[: 3 * local, :wide]

    first_rows = 3 * local // PIECE
    for r in range(parts):
        if r < 2:
            turns(r, heads, small, place, cosine, sine)
        if r == 2:
            for n in range(2):
                weights.at("p", parts, n)
                turns(r + n, heads, small, place, cosine, sine)
            load_cot.wait()
            g[...] = (slope[...] * keep_col[...]).astype(BF)
            gsecond[...] = jnp.zeros_like(gsecond)
        weights.at("p", r, 0)
        if r == 1:
            weights.owns(0, first_rows, False)
        attend_chunk(
            r, heads, rows, normed1, all_w, functools.partial(weights.at, "p", r), small, place, feats,
            q_all, k_all, v_all, lse, att, cosine, sine, proj,
        )
    weights.owns(first_rows, own_pieces, False)
    weights.at("w", 0, 0)
    wo = jnp.concatenate([all_w[r, 3 * local : top] for r in range(parts)])
    normed2 = branch.at[:rows]
    second_norm(rows, tokens, vec, att, wo, middle, normed2)
    mlp[...] = jnp.zeros_like(mlp)

    net = Reducer(grads, got1, got3, got2, got_dp, send, recv)

    def between(r, n):
        for k in range(parts):
            if ("f", k, n + 1) in PLAN:
                pl.when(r == k)(functools.partial(weights.at, "f", k, n + 1))
        if n > 0:
            @pl.when(r == parts - 1)
            def _():
                net.tick(n - 1)

    def mlp_step(r, carry):
        mlp_chunk(
            r, normed2, g, all_w.at[r, up_rows], all_w.at[r, down_rows], small, mlp, gsecond,
            grads.at[r, pl.ds(0, mlp_rows)], sums_up, active, slope, functools.partial(between, r),
        )
        return carry

    lax.fori_loop(0, parts, mlp_step, 0)
    load_cot.start()

    def step(t, carry):
        net.tick(t)
        return carry

    def ticks(start, stop):
        lax.fori_loop(start, stop, step, 0)

    load_cot.wait()
    finish_mlp(slope, keep_col, vec, middle, mlp, gsecond, g, active, branch, sums_vec)
    store_out = pltpu.make_async_copy(active, out, local_sem.at[6])
    store_out.start()
    ticks(3, 4)
    gatt = all_w.at[0, down_rows, :wide]
    gqkv = all_w.at[:, pl.ds(top, 3 * local), :wide]
    wo = jnp.concatenate([all_w[r, 3 * local : top] for r in range(parts)])
    gatt[...] = nt(wo, branch[...]).astype(BF)

    per = 2

    def some_heads(i, carry):
        net.tick(4 + i)

        def head(n, c):
            attend_back(per * i + n, heads, rows, q_all, k_all, v_all, lse, att, gatt, cosine, sine, place, gqkv, column, head_sums)
            return c

        return lax.fori_loop(0, per, head, carry)

    lax.fori_loop(0, count // per, some_heads, 0)
    base = 4 + count // per
    assert count % per == 0 and base + parts // 2 <= mlp_rows // UNIT
    gsecond[...] = jnp.zeros_like(gsecond)

    def late(r, carry):
        pl.when(r % 2 == 0)(lambda: net.tick(base + r // 2))
        here = att[pl.ds(pl.multiple_of(r * local, HD), local)]
        grads[r, mlp_rows : mlp_rows + local] = nn(here, branch[...]).astype(BF)
        grads[r, mlp_rows + local :] = nn(gqkv[r], normed1[...]).astype(BF)
        return carry

    lax.fori_loop(0, parts, late, 0)
    base = base + parts // 2

    def back(r, carry):
        pl.when(r % 2 == 0)(lambda: net.tick(base + r // 2))
        gsecond[...] += tn(gqkv[r], all_w[r, : 3 * local])[:rows]
        return carry

    lax.fori_loop(0, parts, back, 0)
    late_done = base + parts // 2
    ticks(late_done, late_done + 1)
    grad = gsecond[...]
    unit, scale = unit_of(tokens[...].astype(F32))
    gsecond[...] = middle[...] + norm_back(grad, unit, scale, vec[0:1])
    store_gx = pltpu.make_async_copy(gsecond, gx, local_sem.at[7])
    store_gx.start()
    small_sum[...] = jnp.zeros_like(small_sum)
    small_sum[0:1] = jnp.sum(grad * unit, axis=0, keepdims=True)
    small_sum[1:2] = jnp.sum(grad, axis=0, keepdims=True)
    small_sum[2:7] = sums_vec[0:5]
    for r in range(parts):
        small_sum[8 + 2 * r : 9 + 2 * r] = sums_up[r]
        mine = [head_sums[r * heads + h : r * heads + h + 1] for h in range(heads)]
        pieces = [v[:, n * HD : (n + 1) * HD] for n in range(3) for v in mine]
        pieces += [v[:, 3 * HD + n * HALF : 3 * HD + (n + 1) * HALF] for n in range(2) for v in mine]
        small_sum[9 + 2 * r : 10 + 2 * r] = jnp.concatenate(pieces, axis=1)
    base = late_done + 1
    exchanges = len(sums.peers)

    def step_small(t, carry):
        net.tick(t)
        for k in range(exchanges + 1):
            @pl.when(t == base + k)
            def _():
                if k > 0:
                    sums.finish(k - 1)
                if k == exchanges:
                    factor = lax.axis_size("dp") / small_sum[6:7]
                    factor_out[0] = factor[0, 0]
                    small_sum[...] *= factor
                if k < exchanges:
                    sums.copy(k).start()
        return carry

    lax.fori_loop(base, base + exchanges + 1, step_small, 0)
    stores = []
    start = 0
    for n, ref in enumerate((o_down, o_up, o_out, o_qkv)):
        if n == 2:
            ticks(base + exchanges + 1, max(net.ticks, base + exchanges + 1))
        stores.append(pltpu.make_async_copy(grads.at[1, pl.ds(start, ref.shape[0])], ref, local_sem.at[8 + n]))
        stores[-1].start()
        start += ref.shape[0]
    for copy in stores + [store_out, store_gx]:
        copy.wait()


def finish_body(vectors, local, up, down, out, qkv, small, factor, middle, gx, *rest):
    shared = len(vectors) + 2
    results, rest = rest[: 6 + shared], rest[6 + shared :]
    low, full, copies = rest[:6], rest[6:10], rest[10]
    sources = (up, down, out, qkv, middle, gx)
    targets = results[:4] + results[4 + shared :]
    loads = [pltpu.make_async_copy(a, b, copies.at[0, n]) for n, (a, b) in enumerate(zip(sources, low))]
    ready = full + low[4:]
    stores = [pltpu.make_async_copy(a, b, copies.at[1, n]) for n, (a, b) in enumerate(zip(ready, targets))]
    order = (3, 2, 0, 1, 5, 4)
    for n in order:
        loads[n].start()
    for n, row in enumerate(vectors):
        results[4 + n][...] = small[row : row + 1].reshape(small.shape[1])
    b_qkv, freqs = results[4 + len(vectors)], results[5 + len(vectors)]
    for n in range(3):
        b_qkv[n : n + 1] = small[9:10, n * local : (n + 1) * local]
    for n in range(2):
        for h in range(freqs.shape[0]):
            start = 3 * local + (n * freqs.shape[0] + h) * HALF
            freqs[h, n : n + 1] = small[9:10, start : start + HALF]
    for n in order:
        loads[n].wait()
        if n < 4:
            full[n][...] = low[n][...].astype(F32) * factor[0]
        stores[n].start()
    for n in order:
        stores[n].wait()


def sds(shape, dtype):
    return jax.ShapeDtypeStruct(shape, dtype)


def body(
    tokens,
    image_group,
    positions,
    keep_mask,
    norm1_gain,
    norm1_bias,
    w_qkv,
    b_qkv,
    rotary_freqs,
    w_out,
    b_out,
    norm2_gain,
    norm2_bias,
    w_up,
    b_up,
    w_down,
    b_down,
    cotangent,
):
    rows, width = tokens.shape
    wide = -(-rows // LANES) * LANES
    parts = lax.axis_size("mp")
    mp_index = lax.axis_index("mp")
    heads = rotary_freqs.shape[1]
    local = heads * HD
    units = w_up.shape[1]
    w_qkv_t = w_qkv.reshape(width, 3 * local).T
    count = parts * heads
    bits = powers("dp")
    sizes = steps_of(bits)
    stages = 8 + len(bits)
    total_rows = 2 * width + 4 * local
    unit_count = total_rows // UNIT
    pieces = max(total_rows // PIECE, len(SIZES))
    swaps = 2 + len(bits)
    in_vmem = pl.BlockSpec(memory_space=pltpu.VMEM)
    in_smem = pl.BlockSpec(memory_space=pltpu.SMEM)
    anywhere = pl.BlockSpec(memory_space=pl.ANY)
    dma = pltpu.SemaphoreType.DMA
    vmem = pltpu.VMEM
    out, gx, o_up, o_down, o_out, o_qkv, small_sum, factor = pl.pallas_call(
        functools.partial(layer_body, heads, rows),
        out_shape=[
            sds((rows, width), BF),
            sds((rows, width), F32),
            sds((width, units), BF),
            sds((units, width), BF),
            sds((local, width), BF),
            sds((3 * local, width), BF),
            sds((16, width), F32),
            sds((1,), F32),
        ],
        in_specs=[anywhere] * 12 + [in_smem] + [anywhere] * 5,
        out_specs=[anywhere] * 6 + [in_vmem, in_smem],
        scratch_shapes=[
            vmem(tokens.shape, BF),
        ]
        + [vmem((width,), F32)] * 6
        + [
            vmem(positions.shape, jnp.int32),
            vmem(keep_mask.shape, jnp.int32),
            vmem(b_qkv.shape, F32),
            vmem((heads, 2, HALF), F32),
            vmem(b_up.shape, BF),
            vmem((parts, total_rows, width), BF),
            vmem((parts, 8, width), F32),
            vmem((8, wide), F32),
            vmem((count, AUG, wide), BF),
            vmem((count, AUG, wide), BF),
            vmem((count, AUG, wide), BF),
            vmem((count, 8, wide), F32),
            vmem((count * HD, wide), BF),
            vmem((parts, heads * HALF, wide), F32),
            vmem((parts, heads * HALF, wide), F32),
            vmem((wide, width), BF),
            vmem((rows, width), F32),
            vmem((wide, width), BF),
            vmem((rows, width), BF),
            vmem((rows, width), F32),
            vmem((rows, width), F32),
            vmem((rows, units), BF),
            vmem((rows, units), F32),
            vmem((8, width), F32),
            vmem((rows, 1), F32),
            vmem((3, 16, wide), BF),
            vmem((parts, 1, units), F32),
            vmem((8, width), F32),
            vmem((3 * HD + 2 * HALF, LANES), F32),
            vmem((-(-count // 8) * 8, 3 * HD + 2 * HALF), F32),
            vmem((parts, total_rows, width), BF),
            vmem((SLOTS * UNIT, width), BF),
            vmem((SLOTS * UNIT, width), BF),
            vmem((SLOTS * UNIT, width), BF),
            vmem((swaps, 16, width), F32),
            dma((5, pieces)),
            dma((5, pieces)),
            dma((3,)),
            dma((3,)),
            dma((24,)),
            dma((stages, unit_count)),
            dma((stages, unit_count)),
            dma((swaps,)),
            dma((swaps,)),
        ]
        + [vmem((SLOTS * UNIT // 2, width), BF), vmem((3, SLOTS * UNIT // 8, width), BF)]
        + [vmem((SLOTS * size, width), BF) for size in sizes[2:]],
        compiler_params=pltpu.CompilerParams(vmem_limit_bytes=61 << 20, collective_id=0, has_side_effects=True),
    )(tokens, norm1_gain, norm1_bias, norm2_gain, norm2_bias, b_out, b_down, positions, keep_mask, b_qkv,
      rotary_freqs.transpose(1, 0, 2), b_up, image_group, cotangent, w_qkv_t, w_out, w_up, w_down)
    sums = (o_up, o_down, o_out, o_qkv)
    vectors = [0, 1, 2, 3, 4, 5, 8]
    finished = pl.pallas_call(
        functools.partial(finish_body, vectors, local),
        out_shape=[sds(ref.shape, F32) for ref in sums]
        + [sds((width,), F32)] * len(vectors)
        + [sds((3, local), F32), sds((heads, 2, HALF), F32), sds(out.shape, BF), sds(gx.shape, F32)],
        in_specs=[anywhere] * 4 + [in_vmem, in_smem, anywhere, anywhere],
        out_specs=[anywhere] * 4 + [in_vmem] * (len(vectors) + 2) + [anywhere] * 2,
        scratch_shapes=[vmem(ref.shape, BF) for ref in sums]
        + [vmem(out.shape, BF), vmem(gx.shape, F32)]
        + [vmem(ref.shape, F32) for ref in sums]
        + [dma((2, 6))],
        compiler_params=pltpu.CompilerParams(vmem_limit_bytes=60 << 20),
    )(*sums, small_sum, factor, out, gx)
    sum_w_up, sum_w_down, sum_w_out, sum_w_qkv, gain1, bias1, b_out_sum, gain2, bias2, b_down_sum, b_up_sum = finished[:11]
    b_qkv_sum, freqs_sum, out, gx = finished[11:]
    return (
        out,
        gx,
        gain1,
        bias1,
        sum_w_qkv.T.reshape(w_qkv.shape),
        b_qkv_sum,
        freqs_sum.transpose(1, 0, 2),
        sum_w_out,
        b_out_sum,
        gain2,
        bias2,
        sum_w_up,
        b_up_sum,
        sum_w_down,
        b_down_sum,
    )


def solution(mesh):
    placed = (
        P(("dp", "mp"), None),
        P("dp"),
        P(None, "dp"),
        P("dp"),
        P(),
        P(),
        P(None, None, "mp"),
        P(None, "mp"),
        P(None, "mp", None),
        P("mp", None),
        P(),
        P(),
        P(),
        P(None, "mp"),
        P("mp"),
        P("mp", None),
        P(),
        P(("dp", "mp"), None),
    )
    return jax.shard_map(
        body,
        mesh=mesh,
        in_specs=placed,
        out_specs=(
            P(("dp", "mp"), None),
            P(("dp", "mp"), None),
            P(),
            P(),
            P(None, None, "mp"),
            P(None, "mp"),
            P(None, "mp", None),
            P("mp", None),
            P(),
            P(),
            P(),
            P(None, "mp"),
            P("mp"),
            P("mp", None),
            P(),
        ),
        check_vma=False,
    )
```
